32 devices in a mesh: shard: 8 (over z, x), replica: 4 (over y, core).
Axes of the slice: x: 2, y: 2, z: 4, core: 2. Of those that a mesh axis runs over, the one named last changes fastest.
Arguments:
- inputs: bfloat16 [4, 1024, 1280], P('replica', 'shard'), may hold values from -6 to 6
- segment_ids: int32 [4, 1024], P('replica', 'shard'), may hold values from 0 to 4, as said below
- positions: int32 [4, 1024], P('replica', 'shard'), may hold values from 0 to 799, as said below
- gain_one: bfloat16 [1280], P('shard'), may hold values from 0.5 to 1.5
- w_qkv: bfloat16 [1280, 3840], P('shard'), may hold values from -0.15625 to 0.15625
- b_query: bfloat16 [1280], P('shard'), may hold values from -3 to 3
- b_value: bfloat16 [1280], P('shard'), may hold values from -3 to 3
- query_scale: bfloat16 [80], P('shard'), may hold values from -1 to 1
- w_out: bfloat16 [1280, 1280], P('shard'), may hold values from -0.625 to 0.625
- b_out: bfloat16 [1280], P('shard'), may hold values from -3 to 3
- gain_two: bfloat16 [1280], P('shard'), may hold values from 0.5 to 1.5
- w_up: bfloat16 [1280, 1280], P('shard'), may hold values from -0.15625 to 0.15625
- b_up: bfloat16 [1280], P('shard'), may hold values from -3 to 3
- w_down: bfloat16 [1280, 1280], P('shard'), may hold values from -0.15625 to 0.15625
- b_down: bfloat16 [1280], P('shard'), may hold values from -3 to 3
- cotangent: bfloat16 [4, 1024, 1280], P('replica', 'shard'), may hold values from -6 to 6
Outputs:
- output: bfloat16 [4, 1024, 1280], P('replica', 'shard')
- input_grad: float32 [4, 1024, 1280], P('replica', 'shard')
- grad_gain_one: float32 [1280], P('shard')
- grad_w_qkv: float32 [1280, 3840], P('shard')
- grad_b_query: float32 [1280], P('shard')
- grad_b_value: float32 [1280], P('shard')
- grad_query_scale: float32 [80], P('shard')
- grad_w_out: float32 [1280, 1280], P('shard')
- grad_b_out: float32 [1280], P('shard')
- grad_gain_two: float32 [1280], P('shard')
- grad_w_up: float32 [1280, 1280], P('shard')
- grad_b_up: float32 [1280], P('shard')
- grad_w_down: float32 [1280, 1280], P('shard')
- grad_b_down: float32 [1280], P('shard')
The draws below stay inside these ranges and needn't reach their ends.
Inputs may be any that keep to these rules, and one draw needn't show every extreme that they name: `segment_ids`: along each sequence every document is one run of consecutive tokens, numbered 1, 2, 3, ... in order; the first document has 127 tokens, the second 800, each later one 60 to 800 except the last, which the padding or the sequence's end may cut short. Each sequence ends in 0 to min(64, 799) padding tokens of segment 0, which form one run. In the first sequence every document after the second has 60 tokens, save a last one cut short by the sequence's end, and there is no padding. `positions`: the place of each token within its run (a document, or the padding), counting from 0 at the run's first token.
All inputs are finite; a program needn't handle non-finite values.
Results may differ from the reference program's by a relative error of at most 0.011.
Values may be sent and summed in bfloat16 or wider, within the bound.
A program may use at most 192 MiB of HBM per device.

```python
import math
import jax
import jax.numpy as jnp
from jax import lax

D = 1280
HEADS = 16
HEAD = 80
FF = 1280
BLOCK = 128
DOC_MIN = 60
DOC_MAX = 800
LENGTH = 1024
SEQS = 4


def document_layout(key):
    count = LENGTH // DOC_MIN + 2
    length_key, padding_key = jax.random.split(jax.random.fold_in(key, 11))
    sizes = jax.random.randint(length_key, (SEQS, count), DOC_MIN, DOC_MAX + 1).astype(jnp.int32)
    sizes = sizes.at[0, 2:].set(DOC_MIN)
    sizes = sizes.at[:, 0].set(BLOCK - 1).at[:, 1].set(DOC_MAX)
    ends = jnp.cumsum(sizes, axis=1).astype(jnp.int32)
    starts = ends - sizes
    padding = jax.random.randint(padding_key, (SEQS, 1), 0, min(LENGTH // 16, DOC_MAX - 1) + 1).astype(jnp.int32)
    padding = padding.at[0, 0].set(0)
    places = jnp.arange(LENGTH, dtype=jnp.int32)[None, :]
    index = jnp.sum((ends[:, None, :] <= places[:, :, None]).astype(jnp.int32), axis=2)
    begins = jnp.take_along_axis(starts, index, axis=1)
    live = places < LENGTH - padding
    segments = jnp.where(live, index + 1, 0)
    run_start = jnp.where(live, begins, LENGTH - padding)
    return (segments.astype(jnp.int32), (places - run_start).astype(jnp.int32))


def draw_segment_ids(key, part):
    return document_layout(key)[0]


def draw_positions(key, part):
    return document_layout(key)[1]


def shard_levels(rng, dims, shards, smallest, top_value):
    def one(dim, shards_of):
        steps = jax.random.uniform(jax.random.fold_in(jax.random.fold_in(rng, 6), dim), (shards_of,), jnp.float32, smallest / len(shards), top_value / len(shards))
        return jnp.repeat(jnp.exp(steps), dims[dim] // shards_of).reshape((-1,) + (1,) * (len(dims) - dim - 1))

    level = one(*shards[0])
    for cut in shards[1:]:
        level = level * one(*cut)
    return level


def gaussian(rng, shape, spread, limit, cuts=(), kind=jnp.bfloat16):
    values = jax.random.normal(rng, shape, jnp.float32) * spread
    if len(cuts) > 0:
        values = shard_levels(rng, shape, cuts, -0.22, 0.18) * values
    return jnp.clip(values, min=-limit, max=limit).astype(kind)


def setup_inputs(seed: int = 0) -> dict:
    key_of = jax.random.split(jax.random.key(seed), 17)
    return {
        "inputs": gaussian(key_of[0], (SEQS, LENGTH, D), 1.0, 6.0, ((0, 4), (1, 8))),
        "segment_ids": draw_segment_ids(jax.random.fold_in(key_of[16], 71), 0),
        "positions": draw_positions(jax.random.fold_in(key_of[16], 71), 0),
        "gain_one": jnp.clip(1.0 + 0.1 * jax.random.normal(key_of[3], (D,), jnp.float32), 0.5, 1.5).astype(jnp.bfloat16),
        "w_qkv": gaussian(key_of[4], (D, 3 * D), D ** -0.5, 0.15625, ((0, 8),)),
        "b_query": gaussian(key_of[5], (D,), 0.5, 3.0, ((0, 8),)),
        "b_value": gaussian(key_of[6], (D,), 0.5, 3.0, ((0, 8),)),
        "query_scale": jnp.clip(jax.random.uniform(key_of[7], (HEAD,), jnp.float32, -1.0, 1.0) * shard_levels(key_of[7], (HEAD,), ((0, 8),), -0.4, 0.0), -1.0, 1.0).astype(jnp.bfloat16),
        "w_out": gaussian(key_of[8], (D, D), (D // 16) ** -0.5, 0.625, ((0, 8),)),
        "b_out": gaussian(key_of[9], (D,), 0.5, 3.0, ((0, 8),)),
        "gain_two": jnp.clip(1.0 + 0.1 * jax.random.normal(key_of[10], (D,), jnp.float32), 0.5, 1.5).astype(jnp.bfloat16),
        "w_up": gaussian(key_of[11], (D, FF), D ** -0.5, 0.15625, ((0, 8),)),
        "b_up": gaussian(key_of[12], (FF,), 0.5, 3.0, ((0, 8),)),
        "w_down": gaussian(key_of[13], (FF, D), FF ** -0.5, 0.15625, ((0, 8),)),
        "b_down": gaussian(key_of[14], (D,), 0.5, 3.0, ((0, 8),)),
        "cotangent": gaussian(key_of[15], (SEQS, LENGTH, D), 1.0, 6.0, ((0, 4), (1, 8))),
    }


EPS = 1e-06
QUERY_BASE = 1.442695041
MASKED = -1000000000.0
HIGHEST_PRECISION = lax.Precision.HIGHEST

@jax.custom_vjp
def low(v):
    return lax.optimization_barrier(v.astype(jnp.bfloat16)).astype(jnp.float32)

@jax.custom_vjp
def low_back(v):
    return v

def low_keep(v):
    return (low(v), None)

def low_pass(kept, grad):
    return (grad,)

def back_keep(v):
    return (v, None)

def back_low(kept, grad):
    return (low(grad),)
low.defvjp(low_keep, low_pass)
low_back.defvjp(back_keep, back_low)

def norm_apply(rows_in, gain):
    scale = lax.rsqrt(lax.optimization_barrier(jnp.mean(rows_in * rows_in, axis=-1, keepdims=True)) + EPS)
    return rows_in * scale * gain

def layer_forward(inputs_f, segments, places, gain_one, w_qkv, b_query, b_value, query_scale, w_out, b_out, gain_two, w_up, b_up, w_down, b_down):
    length = inputs_f.shape[0]
    width = inputs_f.shape[1]
    normed = low(norm_apply(inputs_f, gain_one))
    projected = low_back(jnp.dot(normed, w_qkv, precision=HIGHEST_PRECISION))
    factor = QUERY_BASE / math.sqrt(HEAD) * jax.nn.softplus(query_scale)
    query = (projected[:, :width] + b_query).reshape(length, HEADS, HEAD) * factor
    queries = low(query)
    keys = low(projected[:, width:2 * width].reshape(length, HEADS, HEAD))
    values = low((projected[:, 2 * width:] + b_value).reshape(length, HEADS, HEAD))
    raw = low_back(jnp.einsum('qhe,khe->hqk', queries, keys, precision=HIGHEST_PRECISION))
    allowed = (segments[:, None] == segments[None, :]) & (places[None, :] <= places[:, None])
    scores = jnp.where(allowed[None], raw, MASKED)
    top = lax.optimization_barrier(jnp.max(scores, axis=-1, keepdims=True))
    log_total = top + jnp.log(lax.optimization_barrier(jnp.sum(jnp.exp(scores - top), axis=-1, keepdims=True)))
    probs = low(jnp.exp(scores - log_total))
    context = jnp.einsum('hqk,khe->qhe', probs, values, precision=HIGHEST_PRECISION).reshape(length, width)
    keep = (segments != 0).astype(jnp.float32)[:, None]
    attended = low(low_back(context * keep))
    mixed = inputs_f + low_back(jnp.dot(attended, w_out, precision=HIGHEST_PRECISION)) + b_out
    normed_two = low(norm_apply(mixed, gain_two))
    hidden = low_back(jnp.dot(normed_two, w_up, precision=HIGHEST_PRECISION)) + b_up
    activation = low(jax.nn.silu(hidden))
    return mixed + low_back(jnp.dot(activation, w_down, precision=HIGHEST_PRECISION)) + b_down

def reference(inputs, segment_ids, positions, gain_one, w_qkv, b_query, b_value, query_scale, w_out, b_out, gain_two, w_up, b_up, w_down, b_down, cotangent):
    params = tuple((weight.astype(jnp.float32) for weight in (gain_one, w_qkv, b_query, b_value, query_scale, w_out, b_out, gain_two, w_up, b_up, w_down, b_down)))

    def one_sequence(totals, item):
        rows_in, segments, places, cotangent_rows = item

        def forward(inputs_f, *weights):
            return layer_forward(inputs_f, segments, places, *weights)
        result, pull = jax.vjp(forward, rows_in.astype(jnp.float32), *params)
        grads = pull(cotangent_rows.astype(jnp.float32))
        totals = tuple((total + grad for total, grad in zip(totals, grads[1:])))
        return (totals, (result.astype(jnp.bfloat16), grads[0]))
    start_totals = tuple((jnp.zeros(weight.shape, jnp.float32) for weight in params))
    sums, stacked = lax.scan(one_sequence, start_totals, (inputs, segment_ids, positions, cotangent))
    return (stacked[0], stacked[1], sums[0], sums[1], sums[2], sums[3], sums[4], sums[5], sums[6], sums[7], sums[8], sums[9], sums[10], sums[11])
```

```python
import functools
import math

import jax
import jax.numpy as jnp
from jax import lax
from jax.experimental import pallas as pl
from jax.experimental.pallas import tpu as pltpu
from jax.sharding import PartitionSpec as P

HEADS = 16
HEAD = 80
DOC_MAX = 800
EPS = 1e-06
QUERY_BASE = 1.442695041
MASKED = -1000000000.0
MESH = pl.DeviceIdType.MESH
MAJOR = 4
VMEM = pl.BlockSpec(memory_space=pltpu.VMEM)
ANY = pl.BlockSpec(memory_space=pl.ANY)
F32 = jnp.float32
BF16 = jnp.bfloat16


class Place:
    def __init__(self, shards):
        self.shards = shards
        self.minor = shards // MAJOR
        self.me = lax.axis_index("shard")
        self.rep = lax.axis_index("replica")
        self.a = self.me // self.minor
        self.b = lax.rem(self.me, self.minor)
        self.started = []

    def at(self, da, db):
        a = lax.rem(self.a + da + MAJOR, MAJOR)
        b = lax.rem(self.b + db + self.minor, self.minor)
        return a * self.minor + b

    def flip(self, mask):
        bit = lax.rem(self.rep // mask, 2)
        return self.rep + mask - 2 * mask * bit

    def greet(self, masks):
        barrier = pltpu.get_barrier_semaphore()
        count = 0
        for da in range(MAJOR):
            for db in range(self.minor):
                if da or db:
                    pl.semaphore_signal(
                        barrier, inc=1, device_id=(self.at(da, db), self.rep), device_id_type=MESH
                    )
                    count += 1
        for mask in masks:
            pl.semaphore_signal(
                barrier, inc=1, device_id=(self.me, self.flip(mask)), device_id_type=MESH
            )
            count += 1
        pl.semaphore_wait(barrier, count)

    def send(self, src, dst, ssem, rsem, shard=None, rep=None):
        copy = pltpu.make_async_remote_copy(
            src_ref=src,
            dst_ref=dst,
            send_sem=ssem,
            recv_sem=rsem,
            device_id=(self.me if shard is None else shard, self.rep if rep is None else rep),
            device_id_type=MESH,
        )
        copy.start()
        self.started.append(copy)
        return copy

    def arrived(self, dst, ssem, rsem):
        pltpu.make_async_remote_copy(
            src_ref=dst,
            dst_ref=dst,
            send_sem=ssem,
            recv_sem=rsem,
            device_id=(self.me, self.rep),
            device_id_type=MESH,
        ).wait_recv()

    def settle(self):
        for copy in self.started:
            copy.wait_send()
        self.started = []


def masks_of(parts):
    return {4: (2, 1), 2: (1,), 1: ()}[parts]


def others(place):
    return [(da, db) for da in range(MAJOR) for db in range(place.minor) if da or db]


def front_kernel(
    shards, wparts, fparts, qblock,
    x_ref, packet_ref, bias_ref, wq_ref, ffn_ref,
    normed_ref, qkv_ref, query_ref, log_ref, att_ref, vec_ref, start_ref, wcols_ref, ffn_out,
    xg, packets, turned, context,
    x_send, x_recv, p_send, p_recv, w_send, w_recv, f_send, f_recv, f_local, a_send, a_recv,
):
    at = Place(shards)
    me, minor = at.me, at.minor
    block, width = x_ref.shape
    length = shards * block
    slab = width // shards
    local = slab // HEAD
    peers = others(at)
    fmasks = masks_of(fparts)
    wmasks = masks_of(wparts)
    at.greet(tuple(sorted(set(fmasks) | set(wmasks))))
    fpart = lax.rem(at.rep, fparts)
    wpart = lax.rem(at.rep, wparts)

    for i, (da, db) in enumerate(peers):
        at.send(packet_ref, packets.at[me], p_send.at[i], p_recv.at[me], shard=at.at(da, db))
    xg[me] = x_ref[...]
    packets[me] = packet_ref[...]
    k = 0
    for da in range(1, MAJOR):
        at.send(xg.at[me], xg.at[me], x_send.at[k], x_recv.at[me], shard=at.at(da, 0))
        k += 1
    for db in range(1, minor):
        at.send(xg.at[me], xg.at[me], x_send.at[k], x_recv.at[me], shard=at.at(0, db))
        k += 1
    for i, (da, db) in enumerate(peers):
        dest = at.at(da, db)
        at.send(
            wq_ref.at[dest, wpart], wcols_ref.at[me, wpart], w_send.at[i], w_recv.at[me, wpart], shard=dest
        )
    own = pltpu.make_async_copy(wq_ref.at[me], wcols_ref.at[me], f_local.at[0])
    own.start()
    own_ffn = pltpu.make_async_copy(ffn_ref, ffn_out.at[:, me], f_local.at[1])
    own_ffn.start()
    fk = 0
    for db in range(1, minor):
        at.send(
            ffn_ref.at[:, fpart], ffn_out.at[:, me, fpart], f_send.at[fk], f_recv.at[me, fpart],
            shard=at.at(0, db),
        )
        fk += 1

    for da in range(1, MAJOR):
        origin = at.at(-da, 0)
        at.arrived(xg.at[origin], x_send.at[0], x_recv.at[origin])
        for db in range(1, minor):
            at.send(xg.at[origin], xg.at[origin], x_send.at[k], x_recv.at[origin], shard=at.at(0, db))
            k += 1
    for da in range(1, MAJOR):
        at.send(
            ffn_ref.at[:, fpart], ffn_out.at[:, me, fpart], f_send.at[fk], f_recv.at[me, fpart],
            shard=at.at(da, 0),
        )
        fk += 1

    wk = len(peers)
    for mask in wmasks:
        for da, db in peers:
            origin = at.at(-da, -db)
            slot = wcols_ref.at[origin, wpart]
            at.arrived(slot, w_send.at[0], w_recv.at[origin, wpart])
            at.send(slot, slot, w_send.at[wk], w_recv.at[origin, wpart], rep=at.flip(mask))
            wk += 1
    for da, db in peers:
        origin = at.at(-da, -db)
        last = wparts - 1 - wpart
        at.arrived(wcols_ref.at[origin, last], w_send.at[0], w_recv.at[origin, last])
    own.wait()
    turned[...] = wcols_ref[...].reshape(width, 3 * slab).T

    for da, db in peers:
        origin = at.at(-da, -db)
        at.arrived(packets.at[origin], p_send.at[0], p_recv.at[origin])
    vectors = jnp.zeros((8, width), F32)
    scales = jnp.zeros((1, 128), F32)
    lanes = lax.broadcasted_iota(jnp.int32, (8, width), 1)
    for j in range(shards):
        piece = packets[j]
        wide = jnp.concatenate([piece, jnp.zeros((8, width - piece.shape[1]), F32)], axis=1)
        wide = jnp.where(lanes < slab, wide, 0.0)
        vectors = vectors + (pltpu.roll(wide, j * slab, 1) if j else wide)
        scales = scales + piece[5:6, :128]
        start_ref[:, j * block : (j + 1) * block] = jnp.broadcast_to(piece[6:7, :block], (8, block))
    rows = lax.broadcasted_iota(jnp.int32, (8, width), 0)
    vec_ref[...] = jnp.where(rows < 5, vectors, 0.0)
    vec_ref[5:6, :128] = scales
    gain = vec_ref[0:1, :]
    column = jnp.broadcast_to(scales, (128, 128)).T[:HEAD, 0:1]
    soft = jnp.maximum(column, 0.0) + jnp.log(1.0 + jnp.exp(-jnp.abs(column)))
    factor = jnp.concatenate([QUERY_BASE / math.sqrt(HEAD) * soft] * local, axis=0)
    bias_query = bias_ref[:, 0:1]
    bias_value = bias_ref[:, 1:2]

    def project(origin):
        rows_in = xg[origin].astype(F32)
        scale = lax.rsqrt(jnp.mean(rows_in * rows_in, axis=-1, keepdims=True) + EPS)
        normed = (rows_in * scale * gain).astype(BF16)
        tokens = pl.ds(pl.multiple_of(origin * block, block), block)
        normed_ref[tokens, :] = normed
        out = lax.dot_general(
            turned[...], normed, (((1,), (1,)), ((), ())), preferred_element_type=F32
        )
        query = out[:slab] + bias_query
        query_ref[:, tokens] = query
        qkv_ref[:slab, tokens] = (query * factor).astype(BF16)
        qkv_ref[slab : 2 * slab, tokens] = out[slab : 2 * slab].astype(BF16)
        qkv_ref[2 * slab :, tokens] = (out[2 * slab :] + bias_value).astype(BF16)

    def project_major(i, carry):
        project(at.at(-i, 0))
        return carry

    def project_minor(i, carry):
        origin = at.at(-lax.rem(i, MAJOR), -(1 + i // MAJOR))
        at.arrived(xg.at[origin], x_send.at[0], x_recv.at[origin])
        project(origin)
        return carry

    lax.fori_loop(0, MAJOR, project_major, 0)
    lax.fori_loop(0, shards - MAJOR, project_minor, 0)

    log_ref[...] = jnp.zeros_like(log_ref)
    for i in range(length // qblock):
        reach = (i + 1) * qblock
        span = slice(i * qblock, reach)
        starts = start_ref[0:1, span]
        key_place = lax.broadcasted_iota(jnp.int32, (reach, qblock), 0).astype(F32)
        query_place = (i * qblock + lax.broadcasted_iota(jnp.int32, (1, qblock), 1)).astype(F32)
        allowed = (key_place >= starts) & (key_place <= query_place)
        for h in range(local):
            head = slice(h * HEAD, (h + 1) * HEAD)
            queries = qkv_ref[h * HEAD : (h + 1) * HEAD, span]
            keys = qkv_ref[slab + h * HEAD : slab + (h + 1) * HEAD, :reach]
            values = qkv_ref[2 * slab + h * HEAD : 2 * slab + (h + 1) * HEAD, :reach]
            scores = lax.dot_general(
                keys, queries, (((0,), (0,)), ((), ())), preferred_element_type=F32
            )
            scores = jnp.where(allowed, scores, MASKED)
            top = jnp.max(scores, axis=0, keepdims=True)
            powers = jnp.exp(scores - top)
            total = jnp.sum(powers, axis=0, keepdims=True)
            probs = (powers * (1.0 / total)).astype(BF16)
            log_ref[h : h + 1, span] = top + jnp.log(total)
            context[head, span] = jnp.dot(values, probs, preferred_element_type=F32).astype(BF16)
        for j in range(i * qblock // block, reach // block):
            @pl.when(me != j)
            def _():
                pltpu.make_async_remote_copy(
                    src_ref=context.at[:, j * block : (j + 1) * block],
                    dst_ref=att_ref.at[pl.ds(pl.multiple_of(me * slab, slab), slab), :],
                    send_sem=a_send.at[j],
                    recv_sem=a_recv.at[me],
                    device_id=(j, at.rep),
                    device_id_type=MESH,
                ).start()

            @pl.when(me == j)
            def _():
                att_ref[pl.ds(pl.multiple_of(me * slab, slab), slab), :] = context[
                    :, j * block : (j + 1) * block
                ]

    def share(origin, have, mask, fk):
        for part in have:
            slot = ffn_out.at[:, origin, part]
            at.send(slot, slot, f_send.at[fk], f_recv.at[origin, part], rep=at.flip(mask))
            fk += 1
        return fk

    def flipped(part, mask):
        bit = lax.rem(part // mask, 2)
        return part + mask - 2 * mask * bit

    own_parts = [fpart]
    for da in range(1, MAJOR):
        origin = at.at(-da, 0)
        slot = ffn_out.at[:, origin, fpart]
        at.arrived(slot, f_send.at[0], f_recv.at[origin, fpart])
        for db in range(1, minor):
            at.send(slot, slot, f_send.at[fk], f_recv.at[origin, fpart], shard=at.at(0, db))
            fk += 1
        for mask in fmasks:
            fk = share(origin, own_parts, mask, fk)
    for db in range(1, minor):
        for da in range(MAJOR):
            origin = at.at(-da, -db)
            slot = ffn_out.at[:, origin, fpart]
            at.arrived(slot, f_send.at[0], f_recv.at[origin, fpart])
            for mask in fmasks:
                fk = share(origin, own_parts, mask, fk)
    order = [(da, 0) for da in range(1, MAJOR)]
    order += [(da, db) for db in range(1, minor) for da in range(MAJOR)]
    got = []
    for n, mask in enumerate(fmasks):
        fresh = [flipped(part, mask) for part in own_parts + got]
        for da, db in order:
            origin = at.at(-da, -db)
            for part in fresh:
                at.arrived(ffn_out.at[:, origin, part], f_send.at[0], f_recv.at[origin, part])
            for later in fmasks[n + 1 :]:
                fk = share(origin, fresh, later, fk)
        got = got + fresh
    for da, db in peers:
        origin = at.at(-da, -db)
        at.arrived(
            att_ref.at[pl.ds(pl.multiple_of(origin * slab, slab), slab), :],
            a_send.at[0],
            a_recv.at[origin],
        )
    own_ffn.wait()
    for j in range(shards):
        @pl.when(me != j)
        def _():
            pltpu.make_async_remote_copy(
                src_ref=context.at[:, j * block : (j + 1) * block],
                dst_ref=context.at[:, j * block : (j + 1) * block],
                send_sem=a_send.at[j],
                recv_sem=a_recv.at[0],
                device_id=(j, at.rep),
                device_id_type=MESH,
            ).wait_send()
    at.settle()


def parts_of(rows, unit, most):
    parts = most
    while parts > 1 and rows % (parts * unit):
        parts //= 2
    return parts


def front(shards, inputs, packet, biases, wq, ffn):
    block, width = inputs.shape
    slab = width // shards
    length = shards * block
    local = slab // HEAD
    wparts = wq.shape[1]
    fparts = ffn.shape[1]
    minor = shards // MAJOR
    qblock = 2 * block
    peers = shards - 1
    shapes = (
        jax.ShapeDtypeStruct((length, width), BF16),
        jax.ShapeDtypeStruct((3 * slab, length), BF16),
        jax.ShapeDtypeStruct((slab, length), F32),
        jax.ShapeDtypeStruct((8, length), F32),
        jax.ShapeDtypeStruct((width, block), BF16),
        jax.ShapeDtypeStruct((8, width), F32),
        jax.ShapeDtypeStruct((8, length), F32),
        jax.ShapeDtypeStruct((shards,) + wq.shape[1:], BF16),
        jax.ShapeDtypeStruct((3, shards) + ffn.shape[1:], BF16),
    )
    dma = pltpu.SemaphoreType.DMA
    plane = MAJOR * minor - 1
    f_sends = plane + plane * (fparts - 1)
    return pl.pallas_call(
        functools.partial(front_kernel, shards, wparts, fparts, qblock),
        out_shape=shapes,
        in_specs=[VMEM, VMEM, VMEM, VMEM, ANY],
        out_specs=[VMEM] * 8 + [ANY],
        scratch_shapes=[
            pltpu.VMEM((shards, block, width), BF16),
            pltpu.VMEM((shards, 8, packet.shape[1]), F32),
            pltpu.VMEM((3 * slab, width), BF16),
            pltpu.VMEM((slab, length), BF16),
            dma((plane,)),
            dma((shards,)),
            dma((peers,)),
            dma((shards,)),
            dma((peers * wparts,)),
            dma((shards, wparts)),
            dma((f_sends + 8,)),
            dma((shards, fparts)),
            dma((2,)),
            dma((shards,)),
            dma((shards,)),
        ],
        compiler_params=pltpu.CompilerParams(
            collective_id=0, has_side_effects=True, vmem_limit_bytes=56 << 20
        ),
        name="front",
    )(inputs, packet, biases, wq, ffn)


def prepare(inputs, segment_ids, positions, gain_one, w_qkv, b_query, b_value, query_scale, w_out, b_out, gain_two, w_up, b_up, w_down, b_down):
    shards = lax.axis_size("shard")
    me = lax.axis_index("shard")
    block, width = inputs.shape
    slab = width // shards
    starts = (me * block + lax.iota(jnp.int32, block) - positions.reshape(block)).astype(F32)
    rows = jnp.stack(
        [jnp.pad(v.astype(F32), (0, 256 - slab)) for v in (gain_one, b_out, gain_two, b_up, b_down)]
    )
    scale_row = lax.dynamic_update_slice(
        jnp.zeros((1, 256), F32), query_scale.astype(F32)[None], (0, me * query_scale.shape[0])
    )
    start_row = jnp.pad(starts, (0, 256 - block))[None]
    packet = jnp.concatenate([rows, scale_row, start_row, jnp.zeros((1, 256), F32)], axis=0)
    biases = jnp.stack([b_query, b_value], axis=1).astype(F32)
    wparts = parts_of(slab, 16, 2)
    fparts = parts_of(slab, 8, 4)
    wq = (
        w_qkv.reshape(slab, 3, shards, slab)
        .transpose(2, 0, 1, 3)
        .reshape(shards, wparts, slab // wparts, 3 * slab)
    )
    ffn = jnp.stack([w_out, w_up, w_down]).reshape(3, fparts, slab // fparts, width)
    return packet, biases, wq, ffn


def flipped(part, mask):
    bit = lax.rem(part // mask, 2)
    return part + mask - 2 * mask * bit


def back_kernel(
    shards, replicas, parts, qblock,
    g_ref, dctx_ref, qkv_ref, query_ref, log_ref, start_ref, normed_ref, wcols_ref, vec_ref, row_ref,
    fin_ref, gw_ref, gn_ref, small_ref,
    dctx, grads, turned, proj,
    own, from_core, from_y, from_x, from_z, extra,
    part_gn, gn_x, gn_z,
    gw, gw_core, gw_y, gw_sum, gw_land, gw_extra,
    windows, small_land, small_got,
    d_send, d_recv, o_sem, c_send, c_recv, y_send, y_recv, x_send, x_recv, z_send, z_recv,
    r_send, r_recv, e_send, e_recv,
    nx_send, nx_recv, nz_send, nz_recv,
    wc_send, wc_recv, wy_send, wy_recv, wa_send, wa_recv, wr_send, wr_recv, we_send, we_recv,
    v_send, v_recv, b_send, b_recv,
):
    at = Place(shards)
    me, minor = at.me, at.minor
    slab3, length = qkv_ref.shape
    slab = slab3 // 3
    local = slab // HEAD
    block = length // shards
    width = normed_ref.shape[1]
    peers = others(at)
    halves = max(parts // 2, 1)
    core = lax.rem(at.rep, 2)
    mine = lax.rem(at.rep, parts)
    km = mine // 2 if parts > 1 else 0
    every = []
    mask = 1
    while mask < replicas:
        every.append(mask)
        mask *= 2
    extras = [m for m in every if m >= parts]
    at.greet(tuple(every))
    mats = (2, 1, 0)

    for i, (da, db) in enumerate(peers):
        dest = at.at(da, db)
        at.send(
            dctx_ref.at[pl.ds(pl.multiple_of(dest * slab, slab), slab), :],
            dctx.at[:, pl.ds(pl.multiple_of(me * block, block), block)],
            d_send.at[i], d_recv.at[me], shard=dest,
        )
    locals_ = {}
    for m in mats:
        for k in range(halves):
            if parts > 1:
                at.send(
                    g_ref.at[m, :, (1 - core) + 2 * k], from_core.at[m, k],
                    c_send.at[m, k], c_recv.at[m, k], rep=at.flip(1),
                )
            copy = pltpu.make_async_copy(
                g_ref.at[m, :, core + 2 * k if parts > 1 else 0], own.at[m, k], o_sem.at[m, k]
            )
            copy.start()
            locals_[m, k] = copy
    dctx[:, pl.ds(pl.multiple_of(me * block, block), block)] = dctx_ref[
        pl.ds(pl.multiple_of(me * slab, slab), slab), :
    ]

    def after_core(m):
        for k in range(halves):
            locals_[m, k].wait()
            if parts > 1:
                at.arrived(from_core.at[m, k], c_send.at[m, k], c_recv.at[m, k])
        if parts > 1:
            def add(j, carry):
                for k in range(halves):
                    own[m, k, j] = own[m, k, j] + from_core[m, k, j]
                return carry
            lax.fori_loop(0, shards, add, 0)
        if parts == 4:
            at.send(own.at[m, 1 - km], from_y.at[m], y_send.at[m], y_recv.at[m], rep=at.flip(2))

    def after_y(m):
        if parts == 4:
            at.arrived(from_y.at[m], y_send.at[m], y_recv.at[m])
            def add(j, carry):
                own[m, km, j] = own[m, km, j] + from_y[m, j]
                return carry
            lax.fori_loop(0, shards, add, 0)
        for db in range(1, minor):
            for da in range(MAJOR):
                at.send(
                    own.at[m, km, at.at(da, db)], from_x.at[m, db - 1, at.at(da, db) // minor],
                    x_send.at[m, db - 1, da], x_recv.at[m, db - 1, at.at(da, db) // minor],
                    shard=at.at(0, db),
                )

    def after_x(m):
        for da in range(1, MAJOR + 1):
            to = at.at(da, 0)
            ta = to // minor
            total = own[m, km, to].astype(F32)
            for db in range(1, minor):
                at.arrived(from_x.at[m, db - 1, ta], x_send.at[m, db - 1, 0], x_recv.at[m, db - 1, ta])
                total = total + from_x[m, db - 1, ta].astype(F32)
            own[m, km, to] = total.astype(BF16)
            if da < MAJOR:
                at.send(
                    own.at[m, km, to], from_z.at[m, da - 1], z_send.at[m, da - 1], z_recv.at[m, da - 1],
                    shard=to,
                )

    def after_z(m):
        total = own[m, km, me].astype(F32)
        for da in range(1, MAJOR):
            at.arrived(from_z.at[m, da - 1], z_send.at[m, da - 1], z_recv.at[m, da - 1])
            total = total + from_z[m, da - 1].astype(F32)
        fin_ref[mine, m] = total.astype(BF16)

    for m in mats:
        after_core(m)

    for da, db in peers:
        origin = at.at(-da, -db)
        at.arrived(
            dctx.at[:, pl.ds(pl.multiple_of(origin * block, block), block)], d_send.at[0], d_recv.at[origin]
        )

    scales = vec_ref[5:6, :128]
    column = jnp.broadcast_to(scales, (128, 128)).T[:HEAD, 0:1]
    base = QUERY_BASE / math.sqrt(HEAD)
    soft = jnp.maximum(column, 0.0) + jnp.log(1.0 + jnp.exp(-jnp.abs(column)))
    factor = base * soft
    grads[...] = jnp.zeros_like(grads)

    def attend(i):
        reach = (i + 1) * qblock
        span = slice(i * qblock, reach)
        starts = start_ref[0:1, span]
        key_place = lax.broadcasted_iota(jnp.int32, (reach, qblock), 0).astype(F32)
        query_place = (i * qblock + lax.broadcasted_iota(jnp.int32, (1, qblock), 1)).astype(F32)
        allowed = (key_place >= starts) & (key_place <= query_place)
        for h in range(local):
            queries = qkv_ref[h * HEAD : (h + 1) * HEAD, span]
            keys = qkv_ref[slab + h * HEAD : slab + (h + 1) * HEAD, :reach]
            values = qkv_ref[2 * slab + h * HEAD : 2 * slab + (h + 1) * HEAD, :reach]
            gctx = dctx[h * HEAD : (h + 1) * HEAD, span]
            turn = (((0,), (0,)), ((), ()))
            both = (((1,), (1,)), ((), ()))
            scores = lax.dot_general(keys, queries, turn, preferred_element_type=F32)
            probs = jnp.where(allowed, jnp.exp(scores - log_ref[h : h + 1, span]), 0.0)
            gprobs = lax.dot_general(values, gctx, turn, preferred_element_type=F32)
            delta = jnp.sum(probs * gprobs, axis=0, keepdims=True)
            gscores = (probs * (gprobs - delta)).astype(BF16)
            low = probs.astype(BF16)
            grads[h * HEAD : (h + 1) * HEAD, span] = jnp.dot(
                keys, gscores, preferred_element_type=F32
            )
            kv = slice(slab + h * HEAD, slab + (h + 1) * HEAD)
            grads[kv, :reach] += lax.dot_general(queries, gscores, both, preferred_element_type=F32)
            kv = slice(2 * slab + h * HEAD, 2 * slab + (h + 1) * HEAD)
            grads[kv, :reach] += lax.dot_general(gctx, low, both, preferred_element_type=F32)

    steps = length // qblock
    for i in range(steps):
        attend(i)
        if i == steps - 2:
            after_y(mats[0])

    gscale = jnp.zeros((HEAD, 1), F32)
    for h in range(local):
        rows = slice(h * HEAD, (h + 1) * HEAD)
        scaled = grads[rows, :]
        gscale = gscale + jnp.sum(scaled * query_ref[rows, :], axis=1, keepdims=True)
        grads[rows, :] = scaled * factor
    gscale = gscale * (base / (1.0 + jnp.exp(-column)))
    bias_q = jnp.sum(grads[:slab, :], axis=1, keepdims=True)
    bias_v = jnp.sum(grads[2 * slab :, :], axis=1, keepdims=True)
    turned[:slab3, :] = grads[...].astype(BF16)
    proj[...] = turned[...].T[:, :slab3]

    wcols = wcols_ref[...].reshape(width, slab3)
    gain_rows = jnp.zeros((8, width), F32)

    def partial(origin, acc):
        tokens = pl.ds(pl.multiple_of(origin * block, block), block)
        out = lax.dot_general(
            proj[tokens, :], wcols, (((1,), (1,)), ((), ())), preferred_element_type=F32
        )
        part_gn[origin] = out.astype(BF16)
        weighted = out * normed_ref[tokens, :].astype(F32)
        return acc + jnp.sum(weighted.reshape(block // 8, 8, width), axis=0)

    def away(i, acc):
        db = 1 + i // MAJOR
        to = at.at(lax.rem(i + 1, MAJOR), db)
        acc = partial(to, acc)
        pltpu.make_async_remote_copy(
            src_ref=part_gn.at[to], dst_ref=gn_x.at[db - 1, to // minor],
            send_sem=nx_send.at[db - 1, to // minor], recv_sem=nx_recv.at[db - 1, to // minor],
            device_id=(at.at(0, db), at.rep), device_id_type=MESH,
        ).start()
        return acc

    gain_rows = lax.fori_loop(0, shards - MAJOR, away, gain_rows)
    gain_rows = lax.fori_loop(0, MAJOR, lambda i, acc: partial(at.at(i, 0), acc), gain_rows)
    gain_row = jnp.sum(gain_rows, axis=0, keepdims=True) / vec_ref[0:1, :]

    rows = row_ref[...]
    place = lax.broadcasted_iota(jnp.int32, (8, width), 0)
    rows = jnp.where(place == 0, jnp.broadcast_to(gain_row, (8, width)), rows)
    turn_in = jnp.concatenate(
        [jnp.broadcast_to(gscale, (HEAD, 128)), jnp.zeros((128 - HEAD, 128), F32)], axis=0
    )
    scale_row = jnp.broadcast_to(turn_in.T[0:1, :], (8, 128))
    scale_tile = jnp.where(lax.broadcasted_iota(jnp.int32, (8, 128), 0) == 5, scale_row, 0.0)
    for j in range(shards):
        first = j * slab // 128 * 128
        window = rows[:, first : min(first + 384, width)]
        if window.shape[1] < 384:
            window = jnp.concatenate([window, jnp.zeros((8, 384 - window.shape[1]), F32)], axis=1)
        windows[j, :, :384] = window
        windows[j, :, 384:] = scale_tile
    for i, (da, db) in enumerate(peers):
        dest = at.at(da, db)
        at.send(windows.at[dest], small_land.at[me], v_send.at[i], v_recv.at[me], shard=dest)
    small_land[me] = windows[me]

    rp = width // (shards * parts)
    whole = lax.dot_general(
        normed_ref[...], proj[...], (((0,), (0,)), ((), ())), preferred_element_type=F32
    )
    gw[...] = whole.reshape(shards, parts, rp, slab3).astype(BF16)
    for k in range(halves):
        if parts > 1:
            at.send(
                gw.at[:, (1 - core) + 2 * k], gw_core.at[k], wc_send.at[k], wc_recv.at[k], rep=at.flip(1)
            )
    for m in mats[1:]:
        after_y(m)
    for k in range(halves):
        if parts > 1:
            at.arrived(gw_core.at[k], wc_send.at[k], wc_recv.at[k])
            part = core + 2 * k
            gw_core[k] = gw[:, part] + gw_core[k]
    if parts == 4:
        at.send(gw_core.at[1 - km], gw_y, wy_send.at[0], wy_recv.at[0], rep=at.flip(2))

    for da in range(1, MAJOR + 1):
        to = at.at(da, 0)
        ta = to // minor
        total = part_gn[to].astype(F32)
        for db in range(1, minor):
            at.arrived(gn_x.at[db - 1, ta], nx_send.at[db - 1, 0], nx_recv.at[db - 1, ta])
            total = total + gn_x[db - 1, ta].astype(F32)
        if da < MAJOR:
            part_gn[to] = total.astype(BF16)
            at.send(part_gn.at[to], gn_z.at[da - 1], nz_send.at[da - 1], nz_recv.at[da - 1], shard=to)
        else:
            gn_ref[...] = total
    for m in mats:
        after_x(m)

    if parts == 4:
        at.arrived(gw_y, wy_send.at[0], wy_recv.at[0])
        gw_sum[...] = gw_core[km] + gw_y[...]
    elif parts > 1:
        gw_sum[...] = gw_core[0]
    else:
        gw_sum[...] = gw[:, 0]
    for i, (da, db) in enumerate(peers):
        dest = at.at(da, db)
        at.send(gw_sum.at[dest], gw_land.at[me], wa_send.at[i], wa_recv.at[me], shard=dest)
    gw_land[me] = gw_sum[me]

    for da, db in peers:
        origin = at.at(-da, -db)
        at.arrived(small_land.at[origin], v_send.at[0], v_recv.at[origin])
    small = jnp.sum(small_land[...], axis=0)
    sides = jnp.concatenate(
        [
            jnp.where(
                lax.broadcasted_iota(jnp.int32, (slab, 128), 1) == 6,
                bias_q,
                jnp.where(lax.broadcasted_iota(jnp.int32, (slab, 128), 1) == 7, bias_v, 0.0),
            ),
            jnp.zeros((256 - slab, 128), F32),
        ],
        axis=0,
    )
    sides = jnp.concatenate([sides[:128].T[:8], sides[128:].T[:8]], axis=1)
    shift = lax.rem(me * slab, 128)
    window = pltpu.roll(small[:, :384], lax.rem(384 - shift, 384), 1)
    tall = lax.broadcasted_iota(jnp.int32, (8, 256), 0)
    small_got[0, :, :256] = jnp.where(tall < 5, window[:, :256], sides)
    unit = HEAD // shards
    small_got[0, :, 256:] = pltpu.roll(small[:, 384:], lax.rem(128 - me * unit, 128), 1)
    for n, mask in enumerate(every):
        at.send(small_got.at[2 * n], small_got.at[2 * n + 1], b_send.at[n], b_recv.at[n], rep=at.flip(mask))
        at.arrived(small_got.at[2 * n + 1], b_send.at[n], b_recv.at[n])
        small_got[2 * n + 2] = small_got[2 * n] + small_got[2 * n + 1]
    small_ref[...] = small_got[2 * len(every)]

    for m in mats:
        after_z(m)
    for n, mask in enumerate(extras):
        at.send(fin_ref.at[mine], extra.at[n], e_send.at[n], e_recv.at[n], rep=at.flip(mask))
        at.arrived(extra.at[n], e_send.at[n], e_recv.at[n])
        at.started[-1].wait_send()
        at.started.pop()
        fin_ref[mine] = fin_ref[mine] + extra[n]
    for da, db in peers:
        origin = at.at(-da, -db)
        at.arrived(gw_land.at[origin], wa_send.at[0], wa_recv.at[origin])
    gw_ref[mine] = gw_land[...]
    for n, mask in enumerate(extras):
        at.send(gw_ref.at[mine], gw_extra.at[n], we_send.at[n], we_recv.at[n], rep=at.flip(mask))
        at.arrived(gw_extra.at[n], we_send.at[n], we_recv.at[n])
        at.started[-1].wait_send()
        at.started.pop()
        gw_ref[mine] = gw_ref[mine] + gw_extra[n]
    have = [mine]
    rk = 0
    for mask in masks_of(parts):
        for part in have:
            at.send(fin_ref.at[part], fin_ref.at[part], r_send.at[rk], r_recv.at[part], rep=at.flip(mask))
            at.send(gw_ref.at[part], gw_ref.at[part], wr_send.at[rk], wr_recv.at[part], rep=at.flip(mask))
            rk += 1
        fresh = [flipped(part, mask) for part in have]
        for part in fresh:
            at.arrived(fin_ref.at[part], r_send.at[0], r_recv.at[part])
            at.arrived(gw_ref.at[part], wr_send.at[0], wr_recv.at[part])
        have = have + fresh

    total = gn_ref[...]
    for da in range(1, MAJOR):
        at.arrived(gn_z.at[da - 1], nz_send.at[da - 1], nz_recv.at[da - 1])
        total = total + gn_z[da - 1].astype(F32)
    gn_ref[...] = total
    for db in range(1, minor):
        for i in range(MAJOR):
            pltpu.make_async_remote_copy(
                src_ref=part_gn.at[me], dst_ref=part_gn.at[me],
                send_sem=nx_send.at[db - 1, i], recv_sem=nx_recv.at[db - 1, i],
                device_id=(at.at(0, db), at.rep), device_id_type=MESH,
            ).wait_send()
    at.settle()


def back(shards, replicas, grads, dctx, qkv, query, log, start, normed, wcols, vec, rows):
    parts, rp, width = grads.shape[2:]
    slab3, length = qkv.shape
    slab = slab3 // 3
    block = length // shards
    minor = shards // MAJOR
    halves = max(parts // 2, 1)
    peers = shards - 1
    dma = pltpu.SemaphoreType.DMA
    bits = (replicas - 1).bit_length()
    more = max(bits - (parts - 1).bit_length(), 1)
    vm = pltpu.VMEM
    turned_rows = -(-slab3 // 128) * 128
    return pl.pallas_call(
        functools.partial(back_kernel, shards, replicas, parts, 2 * block),
        out_shape=(
            jax.ShapeDtypeStruct((parts, 3, rp, width), BF16),
            jax.ShapeDtypeStruct((parts, shards, rp, slab3), BF16),
            jax.ShapeDtypeStruct((block, width), F32),
            jax.ShapeDtypeStruct((8, 384), F32),
        ),
        in_specs=[ANY] + [VMEM] * 9,
        out_specs=[VMEM] * 4,
        scratch_shapes=[
            vm((slab, length), BF16),
            vm((slab3, length), F32),
            vm((turned_rows, length), BF16),
            vm((length, slab3), BF16),
            vm((3, halves, shards, rp, width), BF16),
            vm((3, halves, shards, rp, width), BF16),
            vm((3, shards, rp, width), BF16),
            vm((3, minor - 1, MAJOR, rp, width), BF16),
            vm((3, MAJOR - 1, rp, width), BF16),
            vm((more, 3, rp, width), BF16),
            vm((shards, block, width), BF16),
            vm((minor - 1, MAJOR, block, width), BF16),
            vm((MAJOR - 1, block, width), BF16),
            vm((shards, parts, rp, slab3), BF16),
            vm((halves, shards, rp, slab3), BF16),
            vm((shards, rp, slab3), BF16),
            vm((shards, rp, slab3), BF16),
            vm((shards, rp, slab3), BF16),
            vm((more, shards, rp, slab3), BF16),
            vm((shards, 8, 512), F32),
            vm((shards, 8, 512), F32),
            vm((2 * bits + 1, 8, 384), F32),
            dma((peers,)), dma((shards,)),
            dma((3, halves)), dma((3, halves)), dma((3, halves)),
            dma((3,)), dma((3,)),
            dma((3, minor - 1, MAJOR)), dma((3, minor - 1, MAJOR)),
            dma((3, MAJOR - 1)), dma((3, MAJOR - 1)),
            dma((max(parts - 1, 1),)), dma((parts,)),
            dma((more,)), dma((more,)),
            dma((minor - 1, MAJOR)), dma((minor - 1, MAJOR)),
            dma((MAJOR - 1,)), dma((MAJOR - 1,)),
            dma((halves,)), dma((halves,)),
            dma((1,)), dma((1,)),
            dma((peers,)), dma((shards,)),
            dma((max(parts - 1, 1),)), dma((parts,)),
            dma((more,)), dma((more,)),
            dma((peers,)), dma((shards,)),
            dma((bits,)), dma((bits,)),
        ],
        compiler_params=pltpu.CompilerParams(
            collective_id=1, has_side_effects=True, vmem_limit_bytes=58 << 20
        ),
        name="back",
    )(grads, dctx, qkv, query, log, start, normed, wcols, vec, rows)


def middle(x, att, keep, weights, vec, cotangent):
    width = x.shape[1]
    w_out, w_up, w_down = weights
    b_out, gain_two, b_up, b_down = vec[1], vec[2], vec[3], vec[4]
    x = x.astype(F32)
    att = att * keep.astype(BF16)[None, :]
    mixed = x + lax.dot_general(att, w_out, (((0,), (0,)), ((), ())), preferred_element_type=F32) + b_out
    r = lax.rsqrt(jnp.mean(mixed * mixed, axis=-1, keepdims=True) + EPS)
    normed = (mixed * r * gain_two).astype(BF16)
    hidden = jnp.dot(normed, w_up, preferred_element_type=F32) + b_up
    s = 1.0 / (1.0 + jnp.exp(-hidden))
    act = (hidden * s).astype(BF16)
    output = (mixed + jnp.dot(act, w_down, preferred_element_type=F32) + b_down).astype(BF16)
    cot = cotangent.astype(F32)
    both = (((1,), (1,)), ((), ()))
    tokens = (((0,), (0,)), ((), ()))
    g_down = lax.dot_general(act, cotangent, tokens, preferred_element_type=F32)
    g_act = lax.dot_general(cotangent, w_down, both, preferred_element_type=F32)
    g_hidden = g_act * (s + hidden * s * (1.0 - s))
    low = g_hidden.astype(BF16)
    g_up = lax.dot_general(normed, low, tokens, preferred_element_type=F32)
    g_normed = lax.dot_general(low, w_up, both, preferred_element_type=F32)
    g_mixed = cot + r * gain_two * g_normed - mixed * (r * r * r) * jnp.mean(
        mixed * gain_two * g_normed, axis=-1, keepdims=True
    )
    g_low = g_mixed.astype(BF16)
    g_out = jnp.dot(att, g_low, preferred_element_type=F32)
    dctx = lax.dot_general(w_out, g_low, both, preferred_element_type=F32).astype(BF16) * keep.astype(BF16)[None, :]
    rows = jnp.stack(
        [jnp.zeros(width, F32), g_mixed.sum(0), (g_normed * mixed * r).sum(0), g_hidden.sum(0), cot.sum(0)]
        + [jnp.zeros(width, F32)] * 3
    )
    grads = jnp.stack([g_out.astype(BF16), g_up.astype(BF16), g_down.astype(BF16)])
    return output, g_mixed, grads, dctx, rows


def on_device(
    inputs, segment_ids, positions, gain_one, w_qkv, b_query, b_value, query_scale, w_out, b_out,
    gain_two, w_up, b_up, w_down, b_down, cotangent,
):
    shards = lax.axis_size("shard")
    replicas = lax.axis_size("replica")
    block, width = inputs.shape[1:]
    slab = width // shards
    x = inputs.reshape(block, width)
    packet, biases, wq, ffn = prepare(
        x, segment_ids, positions, gain_one, w_qkv, b_query, b_value, query_scale, w_out, b_out,
        gain_two, w_up, b_up, w_down, b_down,
    )
    normed, qkv, query, log, att, vec, start, wcols, weights = front(shards, x, packet, biases, wq, ffn)
    shape = weights.shape
    keep = segment_ids.reshape(block) != 0
    output, g_mixed, grads, dctx, rows = middle(
        x, att, keep, weights.reshape(3, width, width), vec, cotangent.reshape(block, width)
    )
    fin, gw, gn, small = back(
        shards, replicas, grads.reshape(shape), dctx, qkv, query, log, start, normed, wcols, vec, rows
    )
    parts, rp = fin.shape[0], fin.shape[2]
    fin = fin.transpose(1, 0, 2, 3).reshape(3, slab, width).astype(F32)
    gw = gw.reshape(parts, shards, rp, 3, slab).transpose(0, 2, 3, 1, 4).reshape(slab, 3 * width).astype(F32)
    xf = x.astype(F32)
    r = lax.rsqrt(jnp.mean(xf * xf, axis=-1, keepdims=True) + EPS)
    gain = vec[0]
    input_grad = g_mixed + r * gain * gn - xf * (r * r * r) * jnp.mean(xf * gain * gn, axis=-1, keepdims=True)
    unit = HEAD // shards
    return (
        output[None], input_grad[None], small[0, :slab], gw, small[6, :slab], small[7, :slab],
        small[5, 256 : 256 + unit], fin[0], small[1, :slab], small[2, :slab], fin[1], small[3, :slab],
        fin[2], small[4, :slab],
    )


def solution(mesh):
    rows = P("replica", "shard", None)
    ids = P("replica", "shard")
    vector = P("shard")
    matrix = P("shard", None)
    in_specs = (
        rows, ids, ids, vector, matrix, vector, vector, vector, matrix, vector, vector, matrix, vector,
        matrix, vector, rows,
    )
    out_specs = (
        rows, rows, vector, matrix, vector, vector, vector, matrix, vector, vector, matrix, vector, matrix,
        vector,
    )
    return jax.shard_map(on_device, mesh=mesh, in_specs=in_specs, out_specs=out_specs, check_vma=False)
```

```python
import functools
import math

import jax
import jax.numpy as jnp
from jax import lax
from jax.experimental import pallas as pl
from jax.experimental.pallas import tpu as pltpu
from jax.sharding import PartitionSpec as P

HEADS = 16
HEAD = 80
EPS = 1e-06
QUERY_BASE = 1.442695041
MASKED = -1000000000.0
MESH = pl.DeviceIdType.MESH
MAJOR = 4
VMEM = pl.BlockSpec(memory_space=pltpu.VMEM)
ANY = pl.BlockSpec(memory_space=pl.ANY)
F32 = jnp.float32
BF16 = jnp.bfloat16
NN = (((1,), (0,)), ((), ()))
NT = (((1,), (1,)), ((), ()))
TN = (((0,), (0,)), ((), ()))


def dot(lhs, rhs, dims=NN):
    return lax.dot_general(lhs, rhs, dims, preferred_element_type=F32)


class Place:
    def __init__(self, shards):
        self.shards = shards
        self.minor = shards // MAJOR
        self.me = lax.axis_index("shard")
        self.rep = lax.axis_index("replica")
        self.a = self.me // self.minor
        self.b = lax.rem(self.me, self.minor)
        self.started = []

    def at(self, da, db):
        a = lax.rem(self.a + da + MAJOR, MAJOR)
        b = lax.rem(self.b + db + self.minor, self.minor)
        return a * self.minor + b

    def peers(self):
        return [(da, db) for da in range(MAJOR) for db in range(self.minor) if da or db]

    def flip(self, mask):
        bit = lax.rem(self.rep // mask, 2)
        return self.rep + mask - 2 * mask * bit

    def greet(self, masks):
        barrier = pltpu.get_barrier_semaphore()
        for da, db in self.peers():
            pl.semaphore_signal(
                barrier, inc=1, device_id=(self.at(da, db), self.rep), device_id_type=MESH
            )
        for mask in masks:
            pl.semaphore_signal(
                barrier, inc=1, device_id=(self.me, self.flip(mask)), device_id_type=MESH
            )
        pl.semaphore_wait(barrier, len(self.peers()) + len(masks))

    def send(self, src, dst, ssem, rsem, shard=None, rep=None, when=None):
        copy = pltpu.make_async_remote_copy(
            src_ref=src,
            dst_ref=dst,
            send_sem=ssem,
            recv_sem=rsem,
            device_id=(self.me if shard is None else shard, self.rep if rep is None else rep),
            device_id_type=MESH,
        )
        if when is None:
            copy.start()
        else:
            @pl.when(when)
            def _():
                copy.start()
        self.started.append((when, copy))

    def arrived(self, dst, rsem):
        pltpu.make_async_remote_copy(
            src_ref=dst,
            dst_ref=dst,
            send_sem=rsem,
            recv_sem=rsem,
            device_id=(self.me, self.rep),
            device_id_type=MESH,
        ).wait_recv()

    def settle(self):
        for when, copy in self.started:
            if when is None:
                copy.wait_send()
            else:
                @pl.when(when)
                def _():
                    copy.wait_send()
        self.started = []


class Line:
    def __init__(self, at, slot, major_send, minor_send, recv):
        self.at, self.slot = at, slot
        self.major_send, self.minor_send, self.recv = major_send, minor_send, recv

    def onward(self, origin, up, down, d):
        at = self.at
        if up is not None:
            at.send(
                self.slot(origin), self.slot(origin), self.major_send.at[0, d], self.recv(origin),
                shard=lax.min(at.a + 1, MAJOR - 1) * at.minor + at.b, when=up,
            )
        if down is not None:
            at.send(
                self.slot(origin), self.slot(origin), self.major_send.at[1, d], self.recv(origin),
                shard=lax.max(at.a - 1, 0) * at.minor + at.b, when=down,
            )

    def across(self, origin, when=None):
        at = self.at
        for db in range(1, at.minor):
            at.send(
                self.slot(origin), self.slot(origin), self.minor_send.at[origin // at.minor, db - 1],
                self.recv(origin), shard=at.at(0, db), when=when,
            )

    def begin(self):
        at = self.at
        self.onward(at.me, at.a + 1 < MAJOR, at.a > 0, 0)
        self.across(at.me)

    def step(self, d, then=None):
        at = self.at
        for side in (-1, 1):
            ok = (at.a - d >= 0) if side < 0 else (at.a + d < MAJOR)
            origin = lax.max(at.a - d, 0) if side < 0 else lax.min(at.a + d, MAJOR - 1)
            origin = origin * at.minor + at.b

            @pl.when(ok)
            def _():
                at.arrived(self.slot(origin), self.recv(origin))

            if d + 1 < MAJOR:
                if side < 0:
                    self.onward(origin, ok & (at.a + 1 < MAJOR), None, d)
                else:
                    self.onward(origin, None, ok & (at.a > 0), d)
            self.across(origin, when=ok)
            if then is not None:
                then(origin, ok)


def parts_of(rows):
    return 4 if rows % 32 == 0 else 2


def part_box(part, parts, rows, cols):
    if parts == 4:
        i, j, rows = lax.rem(part, 2), part // 2, rows // 2
    else:
        i, j = 0, part
    return i * rows, rows, j * (cols // 2), cols // 2


def flipped(part, mask):
    bit = lax.rem(part // mask, 2)
    return part + mask - 2 * mask * bit


def front_kernel(
    shards, wparts, fparts, qblock,
    x_ref, small_ref, w_ref, wout_ref, wup_ref, wdown_ref, cot_ref,
    normed_ref, qkv_ref, query_ref, log_ref, vec_ref, start_ref, wcols_ref,
    out_ref, gmixed_ref, xt_ref, dy_ref, dctx_ref, row_ref,
    xg, packets, pieces, turned, context, att, weights,
    xm_send, xn_send, x_recv, p_send, p_recv, w_send, w_recv, wc_send,
    fm_send, fn_send, f_recv, fy_send, fc_send, local_sem, a_send, a_recv,
):
    at = Place(shards)
    me, minor = at.me, at.minor
    block, width = x_ref.shape
    length = shards * block
    slab = width // shards
    slab3 = 3 * slab
    local = slab // HEAD
    peers = at.peers()
    masks = (2, 1) if fparts == 4 else (1,)
    fpart = lax.rem(at.rep, fparts)
    wpart = lax.rem(at.rep, wparts)

    loads = []
    for m, ref in enumerate((wout_ref, wup_ref, wdown_ref)):
        copy = pltpu.make_async_copy(
            ref, weights.at[m, pl.ds(pl.multiple_of(me * slab, 16), slab), :], local_sem.at[m]
        )
        copy.start()
        loads.append(copy)
    xg[me] = x_ref[...]
    packets[me] = small_ref[:8]
    at.greet(masks)

    def wslot(origin, part):
        row, rows, col, cols = part_box(part, fparts, slab, width)
        return weights.at[
            :,
            pl.ds(pl.multiple_of(origin * slab + row, 16), rows),
            pl.ds(pl.multiple_of(col, 128), cols),
        ]

    rows_line = Line(at, lambda o: xg.at[o], xm_send, xn_send, lambda o: x_recv.at[o])
    ffn_line = Line(
        at, lambda o: wslot(o, fpart), fm_send, fn_send, lambda o: f_recv.at[o, fpart]
    )

    def to_replicas(origin, when=None):
        slot = wslot(origin, fpart)
        for mask in masks:
            sem = fy_send.at[origin] if mask == 2 else fc_send.at[origin, 0]
            at.send(slot, slot, sem, f_recv.at[origin, fpart], rep=at.flip(mask), when=when)

    rows_line.begin()
    for i, (da, db) in enumerate(peers):
        at.send(packets.at[me], packets.at[me], p_send.at[i], p_recv.at[me], shard=at.at(da, db))
    for copy in loads:
        copy.wait()
    ffn_line.begin()

    cut = slab // wparts
    for j in range(shards):
        for t in range(3):
            first = t * width + j * slab
            pieces[j, :, :, t * slab : (t + 1) * slab] = w_ref[:, first : first + slab].reshape(
                wparts, cut, slab
            )
    for i, (da, db) in enumerate(peers):
        dest = at.at(da, db)
        at.send(
            pieces.at[dest, wpart], wcols_ref.at[me, wpart], w_send.at[i], w_recv.at[me, wpart], shard=dest
        )
    wcols_ref[me] = pieces[me]

    rows_line.step(1)
    ffn_line.step(1, to_replicas)

    def ffn_minor(distance):
        for db in range(1, minor):
            sides = ((-1, 1) if distance else (0,))
            for side in sides:
                a = at.a + side * distance
                ok = None
                if distance:
                    ok = (a >= 0) & (a < MAJOR)
                origin = lax.max(lax.min(a, MAJOR - 1), 0) * minor + lax.rem(at.b + db, minor)
                slot = wslot(origin, fpart)
                if ok is None:
                    at.arrived(slot, f_recv.at[origin, fpart])
                else:
                    @pl.when(ok)
                    def _():
                        at.arrived(slot, f_recv.at[origin, fpart])
                to_replicas(origin, ok)

    ffn_minor(0)

    if wparts == 2:
        for i, (da, db) in enumerate(peers):
            origin = at.at(-da, -db)
            slot = wcols_ref.at[origin, wpart]
            at.arrived(slot, w_recv.at[origin, wpart])
            at.send(slot, slot, wc_send.at[i], w_recv.at[origin, wpart], rep=at.flip(1))

    for da, db in peers:
        origin = at.at(-da, -db)
        at.arrived(packets.at[origin], p_recv.at[origin])
    vectors = jnp.zeros((8, width), F32)
    scales = jnp.zeros((1, 128), F32)
    lanes = lax.broadcasted_iota(jnp.int32, (8, width), 1)
    unit = HEAD // shards
    for j in range(shards):
        piece = packets[j]
        wide = jnp.concatenate([piece, jnp.zeros((8, width - piece.shape[1]), F32)], axis=1)
        wide = jnp.where(lanes < slab, wide, 0.0)
        vectors = vectors + (pltpu.roll(wide, j * slab, 1) if j else wide)
        scale = jnp.where(lanes[0:1, :128] < unit, piece[5:6, :128], 0.0)
        scales = scales + (pltpu.roll(scale, j * unit, 1) if j else scale)
        start_ref[:, j * block : (j + 1) * block] = jnp.broadcast_to(piece[6:7, :block], (8, block))
    rows = lax.broadcasted_iota(jnp.int32, (8, width), 0)
    vec_ref[...] = jnp.where(rows < 5, vectors, 0.0)
    vec_ref[5:6, :128] = scales
    gain = vec_ref[0:1, :]
    column = jnp.broadcast_to(scales, (128, 128)).T[:HEAD, 0:1]
    soft = jnp.maximum(column, 0.0) + jnp.log(1.0 + jnp.exp(-jnp.abs(column)))
    factor = jnp.concatenate([QUERY_BASE / math.sqrt(HEAD) * soft] * local, axis=0)
    own = small_ref[8:16, :]
    tall = jnp.concatenate([own, jnp.zeros((120, 256), F32)], axis=0)
    tall = jnp.concatenate([tall[:, :128].T, tall[:, 128:].T], axis=0)
    bias_query = tall[:slab, 0:1]
    bias_value = tall[:slab, 1:2]

    rows_line.step(2)
    ffn_line.step(2, to_replicas)
    ffn_minor(1)
    for da, db in peers:
        origin = at.at(-da, -db)
        last = wparts - 1 - wpart
        at.arrived(wcols_ref.at[origin, last], w_recv.at[origin, last])
    turned[...] = wcols_ref[...].reshape(width, slab3).T

    def project(origin):
        rows_in = xg[origin].astype(F32)
        scale = lax.rsqrt(jnp.mean(rows_in * rows_in, axis=-1, keepdims=True) + EPS)
        normed = (rows_in * scale * gain).astype(BF16)
        tokens = pl.ds(pl.multiple_of(origin * block, block), block)
        normed_ref[tokens, :] = normed
        out = dot(turned[...], normed, NT)
        query = out[:slab] + bias_query
        query_ref[:, tokens] = query
        qkv_ref[:slab, tokens] = (query * factor).astype(BF16)
        qkv_ref[slab : 2 * slab, tokens] = out[slab : 2 * slab].astype(BF16)
        qkv_ref[2 * slab :, tokens] = (out[2 * slab :] + bias_value).astype(BF16)

    rows_line.step(3)
    ffn_line.step(3, to_replicas)

    def project_major(i, carry):
        project(at.at(i, 0))
        return carry

    def project_minor(i, carry):
        origin = at.at(lax.rem(i, MAJOR), 1 + i // MAJOR)
        at.arrived(xg.at[origin], x_recv.at[origin])
        project(origin)
        return carry

    lax.fori_loop(0, MAJOR, project_major, 0)
    ffn_minor(2)
    lax.fori_loop(0, shards - MAJOR, project_minor, 0)
    ffn_minor(3)

    log_ref[...] = jnp.zeros_like(log_ref)
    for i in range(length // qblock):
        reach = (i + 1) * qblock
        span = slice(i * qblock, reach)
        starts = start_ref[0:1, span]
        key_place = lax.broadcasted_iota(jnp.int32, (reach, qblock), 0).astype(F32)
        query_place = (i * qblock + lax.broadcasted_iota(jnp.int32, (1, qblock), 1)).astype(F32)
        allowed = (key_place >= starts) & (key_place <= query_place)
        for h in range(local):
            head = slice(h * HEAD, (h + 1) * HEAD)
            queries = qkv_ref[h * HEAD : (h + 1) * HEAD, span]
            keys = qkv_ref[slab + h * HEAD : slab + (h + 1) * HEAD, :reach]
            values = qkv_ref[2 * slab + h * HEAD : 2 * slab + (h + 1) * HEAD, :reach]
            scores = jnp.where(allowed, dot(keys, queries, TN), MASKED)
            top = jnp.max(scores, axis=0, keepdims=True)
            powers = jnp.exp(scores - top)
            total = jnp.sum(powers, axis=0, keepdims=True)
            probs = (powers * (1.0 / total)).astype(BF16)
            log_ref[h : h + 1, span] = top + jnp.log(total)
            context[head, span] = dot(values, probs).astype(BF16)
        mine = pl.ds(pl.multiple_of(me * slab, 16), slab)
        for j in range(i * qblock // block, reach // block):
            piece = slice(j * block, (j + 1) * block)
            at.send(context.at[:, piece], att.at[mine, :], a_send.at[j], a_recv.at[me], shard=j, when=me != j)

            @pl.when(me == j)
            def _():
                att[mine, :] = context[:, piece]

    order = [(0, db) for db in range(1, minor)]
    order += [(da, db) for da in range(1, MAJOR) for db in range(minor)]
    if fparts == 4:
        for da, db in order:
            origin = at.at(da, db)
            part = flipped(fpart, 2)
            slot = wslot(origin, part)
            at.arrived(slot, f_recv.at[origin, part])
            at.send(slot, slot, fc_send.at[origin, 1], f_recv.at[origin, part], rep=at.flip(1))
    for da, db in peers:
        origin = at.at(-da, -db)
        at.arrived(att.at[pl.ds(pl.multiple_of(origin * slab, 16), slab), :], a_recv.at[origin])
    others = [flipped(fpart, 1)] + ([flipped(flipped(fpart, 1), 2)] if fparts == 4 else [])
    for da, db in order:
        origin = at.at(da, db)
        for part in others:
            at.arrived(wslot(origin, part), f_recv.at[origin, part])

    keep_row = small_ref[10:11, :block]
    b_out, gain_two, b_up, b_down = (vec_ref[i : i + 1, :] for i in range(1, 5))
    att_t = (att[...].astype(F32) * keep_row).astype(BF16)
    halves = xt_ref.shape[2]
    xt_ref[0] = att_t.reshape(shards, halves, slab // halves, block)
    mixed = x_ref[...].astype(F32) + dot(att_t.T, weights[0]) + b_out
    r = lax.rsqrt(jnp.mean(mixed * mixed, axis=-1, keepdims=True) + EPS)
    normed_two = (mixed * r * gain_two).astype(BF16)
    xt_ref[1] = normed_two.T.reshape(shards, halves, slab // halves, block)
    hidden = dot(normed_two, weights[1]) + b_up
    s = 1.0 / (1.0 + jnp.exp(-hidden))
    act = (hidden * s).astype(BF16)
    xt_ref[2] = act.T.reshape(shards, halves, slab // halves, block)
    out_ref[...] = (mixed + dot(act, weights[2]) + b_down).astype(BF16)
    dy_ref[2] = cot_ref[...]
    cot = cot_ref[...].astype(F32)
    g_hidden = dot(cot_ref[...], weights[2], NT) * (s + hidden * s * (1.0 - s))
    low = g_hidden.astype(BF16)
    dy_ref[1] = low
    g_normed = dot(low, weights[1], NT)
    weighted = gain_two * g_normed
    g_mixed = cot + r * weighted - mixed * (r * r * r) * jnp.mean(mixed * weighted, axis=-1, keepdims=True)
    gmixed_ref[...] = g_mixed
    low = g_mixed.astype(BF16)
    dy_ref[0] = low
    dctx_ref[...] = (dot(weights[0], low, NT).astype(BF16).astype(F32) * keep_row).astype(BF16)
    row_ref[...] = jnp.zeros_like(row_ref)
    row_ref[1:2, :] = jnp.sum(g_mixed, axis=0, keepdims=True)
    row_ref[2:3, :] = jnp.sum(g_normed * mixed * r, axis=0, keepdims=True)
    row_ref[3:4, :] = jnp.sum(g_hidden, axis=0, keepdims=True)
    row_ref[4:5, :] = jnp.sum(cot, axis=0, keepdims=True)
    at.settle()


def front(shards, inputs, small, w_qkv, w_out, w_up, w_down, cotangent):
    block, width = inputs.shape
    slab = width // shards
    length = shards * block
    wparts = 2 if slab % 32 == 0 else 1
    fparts = parts_of(slab)
    halves = 2 if fparts == 4 else 1
    minor = shards // MAJOR
    peers = shards - 1
    shape = jax.ShapeDtypeStruct
    shapes = (
        shape((length, width), BF16),
        shape((3 * slab, length), BF16),
        shape((slab, length), F32),
        shape((8, length), F32),
        shape((8, width), F32),
        shape((8, length), F32),
        shape((shards, wparts, slab // wparts, 3 * slab), BF16),
        shape((block, width), BF16),
        shape((block, width), F32),
        shape((3, shards, halves, slab // halves, block), BF16),
        shape((3, block, width), BF16),
        shape((width, block), BF16),
        shape((8, width), F32),
    )
    dma = pltpu.SemaphoreType.DMA
    vm = pltpu.VMEM
    return pl.pallas_call(
        functools.partial(front_kernel, shards, wparts, fparts, 2 * block),
        out_shape=shapes,
        in_specs=[VMEM] * 3 + [ANY] * 3 + [VMEM],
        out_specs=[VMEM] * len(shapes),
        scratch_shapes=[
            vm((shards, block, width), BF16),
            vm((shards, 8, 256), F32),
            vm((shards, wparts, slab // wparts, 3 * slab), BF16),
            vm((3 * slab, width), BF16),
            vm((slab, length), BF16),
            vm((width, block), BF16),
            vm((3, width, width), BF16),
            dma((2, MAJOR)), dma((MAJOR, minor - 1)), dma((shards,)),
            dma((peers,)), dma((shards,)),
            dma((peers,)), dma((shards, wparts)), dma((peers,)),
            dma((2, MAJOR)), dma((MAJOR, minor - 1)), dma((shards, fparts)),
            dma((shards,)), dma((shards, 2)),
            dma((3,)), dma((shards,)), dma((shards,)),
        ],
        compiler_params=pltpu.CompilerParams(
            collective_id=0, has_side_effects=True, vmem_limit_bytes=58 << 20
        ),
        name="front",
    )(inputs, small, w_qkv, w_out, w_up, w_down, cotangent)


def pack(positions, segment_ids, gain_one, b_query, b_value, query_scale, b_out, gain_two, b_up, b_down):
    block = positions.shape[-1]
    me = lax.axis_index("shard")
    starts = (me * block + lax.iota(jnp.int32, block) - positions.reshape(block)).astype(F32)
    keep = (segment_ids.reshape(block) != 0).astype(F32)
    table = {
        0: gain_one, 1: b_out, 2: gain_two, 3: b_up, 4: b_down, 5: query_scale, 6: starts,
        8: b_query, 9: b_value, 10: keep,
    }
    total = jnp.zeros((16, 256), F32)
    for row, vector in table.items():
        total = total + jnp.pad(vector.astype(F32)[None], ((row, 15 - row), (0, 256 - vector.shape[0])))
    return total


def masks_of(parts):
    return {4: (2, 1), 2: (1,), 1: ()}[parts]


def others(at):
    return at.peers()


def back_kernel(
    shards, replicas, parts, qblock,
    g_ref, dctx_ref, qkv_ref, query_ref, log_ref, start_ref, normed_ref, wcols_ref, vec_ref, row_ref,
    fin_ref, gw_ref, gn_ref, small_ref,
    dctx, grads, turned, proj,
    own, from_core, from_y, from_x, from_z, extra,
    part_gn, gn_x, gn_z,
    gw, gw_core, gw_y, gw_sum, gw_land, gw_extra,
    windows, small_land, small_got,
    d_send, d_recv, o_sem, c_send, c_recv, y_send, y_recv, x_send, x_recv, z_send, z_recv,
    r_send, r_recv, e_send, e_recv,
    nx_send, nx_recv, nz_send, nz_recv,
    wc_send, wc_recv, wy_send, wy_recv, wa_send, wa_recv, wr_send, wr_recv, we_send, we_recv,
    v_send, v_recv, b_send, b_recv,
):
    at = Place(shards)
    me, minor = at.me, at.minor
    slab3, length = qkv_ref.shape
    slab = slab3 // 3
    local = slab // HEAD
    block = length // shards
    width = normed_ref.shape[1]
    peers = others(at)
    halves = max(parts // 2, 1)
    core = lax.rem(at.rep, 2)
    mine = lax.rem(at.rep, parts)
    km = mine // 2 if parts > 1 else 0
    every = []
    mask = 1
    while mask < replicas:
        every.append(mask)
        mask *= 2
    extras = [m for m in every if m >= parts]
    at.greet(tuple(every))
    mats = (2, 1, 0)

    for i, (da, db) in enumerate(peers):
        dest = at.at(da, db)
        at.send(
            dctx_ref.at[pl.ds(pl.multiple_of(dest * slab, slab), slab), :],
            dctx.at[:, pl.ds(pl.multiple_of(me * block, block), block)],
            d_send.at[i], d_recv.at[me], shard=dest,
        )
    locals_ = {}
    for m in mats:
        for k in range(halves):
            if parts > 1:
                at.send(
                    g_ref.at[m, :, (1 - core) + 2 * k], from_core.at[m, k],
                    c_send.at[m, k], c_recv.at[m, k], rep=at.flip(1),
                )
            copy = pltpu.make_async_copy(
                g_ref.at[m, :, core + 2 * k if parts > 1 else 0], own.at[m, k], o_sem.at[m, k]
            )
            copy.start()
            locals_[m, k] = copy
    dctx[:, pl.ds(pl.multiple_of(me * block, block), block)] = dctx_ref[
        pl.ds(pl.multiple_of(me * slab, slab), slab), :
    ]

    def after_core(m):
        for k in range(halves):
            locals_[m, k].wait()
            if parts > 1:
                at.arrived(from_core.at[m, k], c_recv.at[m, k])
        if parts > 1:
            def add(j, carry):
                for k in range(halves):
                    own[m, k, j] = own[m, k, j] + from_core[m, k, j]
                return carry
            lax.fori_loop(0, shards, add, 0)
        if parts == 4:
            at.send(own.at[m, 1 - km], from_y.at[m], y_send.at[m], y_recv.at[m], rep=at.flip(2))

    def after_y(m):
        if parts == 4:
            at.arrived(from_y.at[m], y_recv.at[m])
            def add(j, carry):
                own[m, km, j] = own[m, km, j] + from_y[m, j]
                return carry
            lax.fori_loop(0, shards, add, 0)
        for db in range(1, minor):
            for da in range(MAJOR):
                at.send(
                    own.at[m, km, at.at(da, db)], from_x.at[m, db - 1, at.at(da, db) // minor],
                    x_send.at[m, db - 1, da], x_recv.at[m, db - 1, at.at(da, db) // minor],
                    shard=at.at(0, db),
                )

    def after_x(m):
        for da in range(1, MAJOR + 1):
            to = at.at(da, 0)
            ta = to // minor
            total = own[m, km, to].astype(F32)
            for db in range(1, minor):
                at.arrived(from_x.at[m, db - 1, ta], x_recv.at[m, db - 1, ta])
                total = total + from_x[m, db - 1, ta].astype(F32)
            own[m, km, to] = total.astype(BF16)
            if da < MAJOR:
                at.send(
                    own.at[m, km, to], from_z.at[m, da - 1], z_send.at[m, da - 1], z_recv.at[m, da - 1],
                    shard=to,
                )

    def after_z(m):
        total = own[m, km, me].astype(F32)
        for da in range(1, MAJOR):
            at.arrived(from_z.at[m, da - 1], z_recv.at[m, da - 1])
            total = total + from_z[m, da - 1].astype(F32)
        fin_ref[mine, m] = total.astype(BF16)

    for m in mats:
        after_core(m)

    for da, db in peers:
        origin = at.at(-da, -db)
        at.arrived(
            dctx.at[:, pl.ds(pl.multiple_of(origin * block, block), block)], d_recv.at[origin]
        )

    scales = vec_ref[5:6, :128]
    column = jnp.broadcast_to(scales, (128, 128)).T[:HEAD, 0:1]
    base = QUERY_BASE / math.sqrt(HEAD)
    soft = jnp.maximum(column, 0.0) + jnp.log(1.0 + jnp.exp(-jnp.abs(column)))
    factor = base * soft
    grads[...] = jnp.zeros_like(grads)

    def attend(i):
        reach = (i + 1) * qblock
        span = slice(i * qblock, reach)
        starts = start_ref[0:1, span]
        key_place = lax.broadcasted_iota(jnp.int32, (reach, qblock), 0).astype(F32)
        query_place = (i * qblock + lax.broadcasted_iota(jnp.int32, (1, qblock), 1)).astype(F32)
        allowed = (key_place >= starts) & (key_place <= query_place)
        for h in range(local):
            queries = qkv_ref[h * HEAD : (h + 1) * HEAD, span]
            keys = qkv_ref[slab + h * HEAD : slab + (h + 1) * HEAD, :reach]
            values = qkv_ref[2 * slab + h * HEAD : 2 * slab + (h + 1) * HEAD, :reach]
            gctx = dctx[h * HEAD : (h + 1) * HEAD, span]
            turn = (((0,), (0,)), ((), ()))
            both = (((1,), (1,)), ((), ()))
            scores = lax.dot_general(keys, queries, turn, preferred_element_type=F32)
            probs = jnp.where(allowed, jnp.exp(scores - log_ref[h : h + 1, span]), 0.0)
            gprobs = lax.dot_general(values, gctx, turn, preferred_element_type=F32)
            delta = jnp.sum(probs * gprobs, axis=0, keepdims=True)
            gscores = (probs * (gprobs - delta)).astype(BF16)
            low = probs.astype(BF16)
            grads[h * HEAD : (h + 1) * HEAD, span] = jnp.dot(
                keys, gscores, preferred_element_type=F32
            )
            kv = slice(slab + h * HEAD, slab + (h + 1) * HEAD)
            grads[kv, :reach] += lax.dot_general(queries, gscores, both, preferred_element_type=F32)
            kv = slice(2 * slab + h * HEAD, 2 * slab + (h + 1) * HEAD)
            grads[kv, :reach] += lax.dot_general(gctx, low, both, preferred_element_type=F32)

    steps = length // qblock
    for i in range(steps):
        attend(i)
        if i == steps - 2:
            after_y(mats[0])

    gscale = jnp.zeros((HEAD, 1), F32)
    for h in range(local):
        rows = slice(h * HEAD, (h + 1) * HEAD)
        scaled = grads[rows, :]
        gscale = gscale + jnp.sum(scaled * query_ref[rows, :], axis=1, keepdims=True)
        grads[rows, :] = scaled * factor
    gscale = gscale * (base / (1.0 + jnp.exp(-column)))
    bias_q = jnp.sum(grads[:slab, :], axis=1, keepdims=True)
    bias_v = jnp.sum(grads[2 * slab :, :], axis=1, keepdims=True)
    turned[:slab3, :] = grads[...].astype(BF16)
    proj[...] = turned[...].T[:, :slab3]

    wcols = wcols_ref[...].reshape(width, slab3)
    gain_rows = jnp.zeros((8, width), F32)

    def partial(origin, acc):
        tokens = pl.ds(pl.multiple_of(origin * block, block), block)
        out = lax.dot_general(
            proj[tokens, :], wcols, (((1,), (1,)), ((), ())), preferred_element_type=F32
        )
        part_gn[origin] = out.astype(BF16)
        weighted = out * normed_ref[tokens, :].astype(F32)
        return acc + jnp.sum(weighted.reshape(block // 8, 8, width), axis=0)

    def away(i, acc):
        db = 1 + i // MAJOR
        to = at.at(lax.rem(i + 1, MAJOR), db)
        acc = partial(to, acc)
        pltpu.make_async_remote_copy(
            src_ref=part_gn.at[to], dst_ref=gn_x.at[db - 1, to // minor],
            send_sem=nx_send.at[db - 1, to // minor], recv_sem=nx_recv.at[db - 1, to // minor],
            device_id=(at.at(0, db), at.rep), device_id_type=MESH,
        ).start()
        return acc

    gain_rows = lax.fori_loop(0, shards - MAJOR, away, gain_rows)
    gain_rows = lax.fori_loop(0, MAJOR, lambda i, acc: partial(at.at(i, 0), acc), gain_rows)
    gain_row = jnp.sum(gain_rows, axis=0, keepdims=True) / vec_ref[0:1, :]

    rows = row_ref[...]
    place = lax.broadcasted_iota(jnp.int32, (8, width), 0)
    rows = jnp.where(place == 0, jnp.broadcast_to(gain_row, (8, width)), rows)
    turn_in = jnp.concatenate(
        [jnp.broadcast_to(gscale, (HEAD, 128)), jnp.zeros((128 - HEAD, 128), F32)], axis=0
    )
    scale_row = jnp.broadcast_to(turn_in.T[0:1, :], (8, 128))
    scale_tile = jnp.where(lax.broadcasted_iota(jnp.int32, (8, 128), 0) == 5, scale_row, 0.0)
    for j in range(shards):
        first = j * slab // 128 * 128
        window = rows[:, first : min(first + 384, width)]
        if window.shape[1] < 384:
            window = jnp.concatenate([window, jnp.zeros((8, 384 - window.shape[1]), F32)], axis=1)
        windows[j, :, :384] = window
        windows[j, :, 384:] = scale_tile
    for i, (da, db) in enumerate(peers):
        dest = at.at(da, db)
        at.send(windows.at[dest], small_land.at[me], v_send.at[i], v_recv.at[me], shard=dest)
    small_land[me] = windows[me]

    rp = width // (shards * parts)
    whole = lax.dot_general(
        normed_ref[...], proj[...], (((0,), (0,)), ((), ())), preferred_element_type=F32
    )
    gw[...] = whole.reshape(shards, parts, rp, slab3).astype(BF16)
    for k in range(halves):
        if parts > 1:
            at.send(
                gw.at[:, (1 - core) + 2 * k], gw_core.at[k], wc_send.at[k], wc_recv.at[k], rep=at.flip(1)
            )
    for m in mats[1:]:
        after_y(m)
    for k in range(halves):
        if parts > 1:
            at.arrived(gw_core.at[k], wc_recv.at[k])
            part = core + 2 * k
            gw_core[k] = gw[:, part] + gw_core[k]
    if parts == 4:
        at.send(gw_core.at[1 - km], gw_y, wy_send.at[0], wy_recv.at[0], rep=at.flip(2))

    for da in range(1, MAJOR + 1):
        to = at.at(da, 0)
        ta = to // minor
        total = part_gn[to].astype(F32)
        for db in range(1, minor):
            at.arrived(gn_x.at[db - 1, ta], nx_recv.at[db - 1, ta])
            total = total + gn_x[db - 1, ta].astype(F32)
        if da < MAJOR:
            part_gn[to] = total.astype(BF16)
            at.send(part_gn.at[to], gn_z.at[da - 1], nz_send.at[da - 1], nz_recv.at[da - 1], shard=to)
        else:
            gn_ref[...] = total
    for m in mats:
        after_x(m)

    if parts == 4:
        at.arrived(gw_y, wy_recv.at[0])
        gw_sum[...] = gw_core[km] + gw_y[...]
    elif parts > 1:
        gw_sum[...] = gw_core[0]
    else:
        gw_sum[...] = gw[:, 0]
    for i, (da, db) in enumerate(peers):
        dest = at.at(da, db)
        at.send(gw_sum.at[dest], gw_land.at[me], wa_send.at[i], wa_recv.at[me], shard=dest)
    gw_land[me] = gw_sum[me]

    for da, db in peers:
        origin = at.at(-da, -db)
        at.arrived(small_land.at[origin], v_recv.at[origin])
    small = jnp.sum(small_land[...], axis=0)
    sides = jnp.concatenate(
        [
            jnp.where(
                lax.broadcasted_iota(jnp.int32, (slab, 128), 1) == 6,
                bias_q,
                jnp.where(lax.broadcasted_iota(jnp.int32, (slab, 128), 1) == 7, bias_v, 0.0),
            ),
            jnp.zeros((256 - slab, 128), F32),
        ],
        axis=0,
    )
    sides = jnp.concatenate([sides[:128].T[:8], sides[128:].T[:8]], axis=1)
    shift = lax.rem(me * slab, 128)
    window = pltpu.roll(small[:, :384], lax.rem(384 - shift, 384), 1)
    tall = lax.broadcasted_iota(jnp.int32, (8, 256), 0)
    small_got[0, :, :256] = jnp.where(tall < 5, window[:, :256], sides)
    unit = HEAD // shards
    small_got[0, :, 256:] = pltpu.roll(small[:, 384:], lax.rem(128 - me * unit, 128), 1)
    for n, mask in enumerate(every):
        at.send(small_got.at[2 * n], small_got.at[2 * n + 1], b_send.at[n], b_recv.at[n], rep=at.flip(mask))
        at.arrived(small_got.at[2 * n + 1], b_recv.at[n])
        small_got[2 * n + 2] = small_got[2 * n] + small_got[2 * n + 1]
    small_ref[...] = small_got[2 * len(every)]

    for m in mats:
        after_z(m)
    for n, mask in enumerate(extras):
        at.send(fin_ref.at[mine], extra.at[n], e_send.at[n], e_recv.at[n], rep=at.flip(mask))
        at.arrived(extra.at[n], e_recv.at[n])
        at.started[-1][1].wait_send()
        at.started.pop()
        fin_ref[mine] = fin_ref[mine] + extra[n]
    for da, db in peers:
        origin = at.at(-da, -db)
        at.arrived(gw_land.at[origin], wa_recv.at[origin])
    gw_ref[mine] = gw_land[...]
    for n, mask in enumerate(extras):
        at.send(gw_ref.at[mine], gw_extra.at[n], we_send.at[n], we_recv.at[n], rep=at.flip(mask))
        at.arrived(gw_extra.at[n], we_recv.at[n])
        at.started[-1][1].wait_send()
        at.started.pop()
        gw_ref[mine] = gw_ref[mine] + gw_extra[n]
    have = [mine]
    rk = 0
    for mask in masks_of(parts):
        for part in have:
            at.send(fin_ref.at[part], fin_ref.at[part], r_send.at[rk], r_recv.at[part], rep=at.flip(mask))
            at.send(gw_ref.at[part], gw_ref.at[part], wr_send.at[rk], wr_recv.at[part], rep=at.flip(mask))
            rk += 1
        fresh = [flipped(part, mask) for part in have]
        for part in fresh:
            at.arrived(fin_ref.at[part], r_recv.at[part])
            at.arrived(gw_ref.at[part], wr_recv.at[part])
        have = have + fresh

    total = gn_ref[...]
    for da in range(1, MAJOR):
        at.arrived(gn_z.at[da - 1], nz_recv.at[da - 1])
        total = total + gn_z[da - 1].astype(F32)
    gn_ref[...] = total
    for db in range(1, minor):
        for i in range(MAJOR):
            pltpu.make_async_remote_copy(
                src_ref=part_gn.at[me], dst_ref=part_gn.at[me],
                send_sem=nx_send.at[db - 1, i], recv_sem=nx_recv.at[db - 1, i],
                device_id=(at.at(0, db), at.rep), device_id_type=MESH,
            ).wait_send()
    at.settle()


def back(shards, replicas, grads, dctx, qkv, query, log, start, normed, wcols, vec, rows):
    parts, rp, width = grads.shape[2:]
    slab3, length = qkv.shape
    slab = slab3 // 3
    block = length // shards
    minor = shards // MAJOR
    halves = max(parts // 2, 1)
    peers = shards - 1
    dma = pltpu.SemaphoreType.DMA
    bits = (replicas - 1).bit_length()
    more = max(bits - (parts - 1).bit_length(), 1)
    vm = pltpu.VMEM
    turned_rows = -(-slab3 // 128) * 128
    return pl.pallas_call(
        functools.partial(back_kernel, shards, replicas, parts, 2 * block),
        out_shape=(
            jax.ShapeDtypeStruct((parts, 3, rp, width), BF16),
            jax.ShapeDtypeStruct((parts, shards, rp, slab3), BF16),
            jax.ShapeDtypeStruct((block, width), F32),
            jax.ShapeDtypeStruct((8, 384), F32),
        ),
        in_specs=[ANY] + [VMEM] * 9,
        out_specs=[VMEM] * 4,
        scratch_shapes=[
            vm((slab, length), BF16),
            vm((slab3, length), F32),
            vm((turned_rows, length), BF16),
            vm((length, slab3), BF16),
            vm((3, halves, shards, rp, width), BF16),
            vm((3, halves, shards, rp, width), BF16),
            vm((3, shards, rp, width), BF16),
            vm((3, minor - 1, MAJOR, rp, width), BF16),
            vm((3, MAJOR - 1, rp, width), BF16),
            vm((more, 3, rp, width), BF16),
            vm((shards, block, width), BF16),
            vm((minor - 1, MAJOR, block, width), BF16),
            vm((MAJOR - 1, block, width), BF16),
            vm((shards, parts, rp, slab3), BF16),
            vm((halves, shards, rp, slab3), BF16),
            vm((shards, rp, slab3), BF16),
            vm((shards, rp, slab3), BF16),
            vm((shards, rp, slab3), BF16),
            vm((more, shards, rp, slab3), BF16),
            vm((shards, 8, 512), F32),
            vm((shards, 8, 512), F32),
            vm((2 * bits + 1, 8, 384), F32),
            dma((peers,)), dma((shards,)),
            dma((3, halves)), dma((3, halves)), dma((3, halves)),
            dma((3,)), dma((3,)),
            dma((3, minor - 1, MAJOR)), dma((3, minor - 1, MAJOR)),
            dma((3, MAJOR - 1)), dma((3, MAJOR - 1)),
            dma((max(parts - 1, 1),)), dma((parts,)),
            dma((more,)), dma((more,)),
            dma((minor - 1, MAJOR)), dma((minor - 1, MAJOR)),
            dma((MAJOR - 1,)), dma((MAJOR - 1,)),
            dma((halves,)), dma((halves,)),
            dma((1,)), dma((1,)),
            dma((peers,)), dma((shards,)),
            dma((max(parts - 1, 1),)), dma((parts,)),
            dma((more,)), dma((more,)),
            dma((peers,)), dma((shards,)),
            dma((bits,)), dma((bits,)),
        ],
        compiler_params=pltpu.CompilerParams(
            collective_id=1, has_side_effects=True, vmem_limit_bytes=58 << 20
        ),
        name="back",
    )(grads, dctx, qkv, query, log, start, normed, wcols, vec, rows)


def on_device(
    inputs, segment_ids, positions, gain_one, w_qkv, b_query, b_value, query_scale, w_out, b_out,
    gain_two, w_up, b_up, w_down, b_down, cotangent,
):
    shards = lax.axis_size("shard")
    replicas = lax.axis_size("replica")
    block, width = inputs.shape[1:]
    slab = width // shards
    x = inputs.reshape(block, width)
    small = pack(positions, segment_ids, gain_one, b_query, b_value, query_scale, b_out, gain_two, b_up, b_down)
    normed, qkv, query, log, vec, start, wcols, output, g_mixed, xt, dy, dctx, rows = front(
        shards, x, small, w_qkv, w_out, w_up, w_down, cotangent.reshape(block, width)
    )
    grads = jnp.einsum("mat,mtd->mad", xt.reshape(3, width, block), dy, preferred_element_type=F32).astype(BF16)
    parts = 4 if (width // shards) % 32 == 0 else 2
    fin, gw, gn, small = back(
        shards, replicas, grads.reshape(3, shards, parts, slab // parts, width), dctx, qkv, query, log, start, normed, wcols, vec, rows
    )
    parts, rp = fin.shape[0], fin.shape[2]
    fin = fin.transpose(1, 0, 2, 3).reshape(3, slab, width).astype(F32)
    gw = gw.reshape(parts, shards, rp, 3, slab).transpose(0, 2, 3, 1, 4).reshape(slab, 3 * width).astype(F32)
    xf = x.astype(F32)
    r = lax.rsqrt(jnp.mean(xf * xf, axis=-1, keepdims=True) + EPS)
    gain = vec[0]
    input_grad = g_mixed + r * gain * gn - xf * (r * r * r) * jnp.mean(xf * gain * gn, axis=-1, keepdims=True)
    unit = HEAD // shards
    return (
        output[None], input_grad[None], small[0, :slab], gw, small[6, :slab], small[7, :slab],
        small[5, 256 : 256 + unit], fin[0], small[1, :slab], small[2, :slab], fin[1], small[3, :slab],
        fin[2], small[4, :slab],
    )


def solution(mesh):
    rows = P("replica", "shard", None)
    ids = P("replica", "shard")
    vector = P("shard")
    matrix = P("shard", None)
    in_specs = (
        rows, ids, ids, vector, matrix, vector, vector, vector, matrix, vector, vector, matrix, vector,
        matrix, vector, rows,
    )
    out_specs = (
        rows, rows, vector, matrix, vector, vector, vector, matrix, vector, vector, matrix, vector, matrix,
        vector,
    )
    return jax.shard_map(on_device, mesh=mesh, in_specs=in_specs, out_specs=out_specs, check_vma=False)
```

```python
import functools
import math

import jax
import jax.numpy as jnp
from jax import lax
from jax.experimental import pallas as pl
from jax.experimental.pallas import tpu as pltpu
from jax.sharding import PartitionSpec as P

HEADS = 16
HEAD = 80
EPS = 1e-06
QUERY_BASE = 1.442695041
MASKED = -1000000000.0
MESH = pl.DeviceIdType.MESH
MAJOR = 4
VMEM = pl.BlockSpec(memory_space=pltpu.VMEM)
ANY = pl.BlockSpec(memory_space=pl.ANY)
F32 = jnp.float32
BF16 = jnp.bfloat16
NN = (((1,), (0,)), ((), ()))
NT = (((1,), (1,)), ((), ()))
TN = (((0,), (0,)), ((), ()))


def dot(lhs, rhs, dims=NN):
    return lax.dot_general(lhs, rhs, dims, preferred_element_type=F32)


class Place:
    def __init__(self, shards):
        self.shards = shards
        self.minor = shards // MAJOR
        self.me = lax.axis_index("shard")
        self.rep = lax.axis_index("replica")
        self.a = self.me // self.minor
        self.b = lax.rem(self.me, self.minor)
        self.started = []

    def at(self, da, db):
        a = lax.rem(self.a + da + MAJOR, MAJOR)
        b = lax.rem(self.b + db + self.minor, self.minor)
        return a * self.minor + b

    def peers(self):
        return [(da, db) for da in range(MAJOR) for db in range(self.minor) if da or db]

    def flip(self, mask):
        bit = lax.rem(self.rep // mask, 2)
        return self.rep + mask - 2 * mask * bit

    def greet(self, masks):
        barrier = pltpu.get_barrier_semaphore()
        for da, db in self.peers():
            pl.semaphore_signal(
                barrier, inc=1, device_id=(self.at(da, db), self.rep), device_id_type=MESH
            )
        for mask in masks:
            pl.semaphore_signal(
                barrier, inc=1, device_id=(self.me, self.flip(mask)), device_id_type=MESH
            )
        pl.semaphore_wait(barrier, len(self.peers()) + len(masks))

    def send(self, src, dst, ssem, rsem, shard=None, rep=None, when=None):
        copy = pltpu.make_async_remote_copy(
            src_ref=src,
            dst_ref=dst,
            send_sem=ssem,
            recv_sem=rsem,
            device_id=(self.me if shard is None else shard, self.rep if rep is None else rep),
            device_id_type=MESH,
        )
        if when is None:
            copy.start()
        else:
            @pl.when(when)
            def _():
                copy.start()
        self.started.append((when, copy))

    def arrived(self, dst, rsem):
        pltpu.make_async_remote_copy(
            src_ref=dst,
            dst_ref=dst,
            send_sem=rsem,
            recv_sem=rsem,
            device_id=(self.me, self.rep),
            device_id_type=MESH,
        ).wait_recv()

    def settle(self):
        for when, copy in self.started:
            if when is None:
                copy.wait_send()
            else:
                @pl.when(when)
                def _():
                    copy.wait_send()
        self.started = []


class Line:
    def __init__(self, at, slot, major_send, minor_send, recv):
        self.at, self.slot = at, slot
        self.major_send, self.minor_send, self.recv = major_send, minor_send, recv

    def onward(self, origin, up, down, d):
        at = self.at
        if up is not None:
            at.send(
                self.slot(origin), self.slot(origin), self.major_send.at[0, d], self.recv(origin),
                shard=lax.min(at.a + 1, MAJOR - 1) * at.minor + at.b, when=up,
            )
        if down is not None:
            at.send(
                self.slot(origin), self.slot(origin), self.major_send.at[1, d], self.recv(origin),
                shard=lax.max(at.a - 1, 0) * at.minor + at.b, when=down,
            )

    def across(self, origin, when=None):
        at = self.at
        for db in range(1, at.minor):
            at.send(
                self.slot(origin), self.slot(origin), self.minor_send.at[origin // at.minor, db - 1],
                self.recv(origin), shard=at.at(0, db), when=when,
            )

    def begin(self):
        at = self.at
        self.onward(at.me, at.a + 1 < MAJOR, at.a > 0, 0)
        self.across(at.me)

    def step(self, d, then=None):
        at = self.at
        for side in (-1, 1):
            ok = (at.a - d >= 0) if side < 0 else (at.a + d < MAJOR)
            origin = lax.max(at.a - d, 0) if side < 0 else lax.min(at.a + d, MAJOR - 1)
            origin = origin * at.minor + at.b

            @pl.when(ok)
            def _():
                at.arrived(self.slot(origin), self.recv(origin))

            if d + 1 < MAJOR:
                if side < 0:
                    self.onward(origin, ok & (at.a + 1 < MAJOR), None, d)
                else:
                    self.onward(origin, None, ok & (at.a > 0), d)
            self.across(origin, when=ok)
            if then is not None:
                then(origin, ok)


def parts_of(rows):
    return 4 if rows % 32 == 0 else 2


def part_box(part, parts, rows, cols):
    if parts == 4:
        i, j, rows = lax.rem(part, 2), part // 2, rows // 2
    else:
        i, j = 0, part
    return i * rows, rows, j * (cols // 2), cols // 2


def flipped(part, mask):
    bit = lax.rem(part // mask, 2)
    return part + mask - 2 * mask * bit


def front_kernel(
    shards, wparts, fparts, qblock,
    x_ref, small_ref, w_ref, wout_ref, wup_ref, wdown_ref, cot_ref,
    normed_ref, qkv_ref, query_ref, log_ref, vec_ref, start_ref, wcols_ref,
    out_ref, gmixed_ref, xt_ref, dy_ref, dctx_ref, row_ref,
    xg, packets, pieces, turned, context, att, weights,
    xm_send, xn_send, x_recv, p_send, p_recv, w_send, w_recv, wc_send,
    fm_send, fn_send, f_recv, fy_send, fc_send, local_sem, a_send, a_recv,
):
    at = Place(shards)
    me, minor = at.me, at.minor
    block, width = x_ref.shape
    length = shards * block
    slab = width // shards
    slab3 = 3 * slab
    local = slab // HEAD
    peers = at.peers()
    masks = (2, 1) if fparts == 4 else (1,)
    fpart = lax.rem(at.rep, fparts)
    wpart = lax.rem(at.rep, wparts)

    loads = []
    for m, ref in enumerate((wout_ref, wup_ref, wdown_ref)):
        copy = pltpu.make_async_copy(
            ref, weights.at[m, pl.ds(pl.multiple_of(me * slab, 16), slab), :], local_sem.at[m]
        )
        copy.start()
        loads.append(copy)
    xg[me] = x_ref[...]
    packets[me] = small_ref[:8]
    at.greet(masks)

    def wslot(origin, part):
        row, rows, col, cols = part_box(part, fparts, slab, width)
        return weights.at[
            :,
            pl.ds(pl.multiple_of(origin * slab + row, 16), rows),
            pl.ds(pl.multiple_of(col, 128), cols),
        ]

    rows_line = Line(at, lambda o: xg.at[o], xm_send, xn_send, lambda o: x_recv.at[o])
    ffn_line = Line(
        at, lambda o: wslot(o, fpart), fm_send, fn_send, lambda o: f_recv.at[o, fpart]
    )

    def to_replicas(origin, when=None):
        slot = wslot(origin, fpart)
        for mask in masks:
            sem = fy_send.at[origin] if mask == 2 else fc_send.at[origin, 0]
            at.send(slot, slot, sem, f_recv.at[origin, fpart], rep=at.flip(mask), when=when)

    rows_line.begin()
    for i, (da, db) in enumerate(peers):
        at.send(packets.at[me], packets.at[me], p_send.at[i], p_recv.at[me], shard=at.at(da, db))
    for copy in loads:
        copy.wait()
    ffn_line.begin()

    cut = slab // wparts
    for j in range(shards):
        for t in range(3):
            first = t * width + j * slab
            pieces[j, :, :, t * slab : (t + 1) * slab] = w_ref[:, first : first + slab].reshape(
                wparts, cut, slab
            )
    for i, (da, db) in enumerate(peers):
        dest = at.at(da, db)
        at.send(
            pieces.at[dest, wpart], wcols_ref.at[me, wpart], w_send.at[i], w_recv.at[me, wpart], shard=dest
        )
    wcols_ref[me] = pieces[me]

    rows_line.step(1)
    ffn_line.step(1, to_replicas)

    def ffn_minor(distance):
        for db in range(1, minor):
            sides = ((-1, 1) if distance else (0,))
            for side in sides:
                a = at.a + side * distance
                ok = None
                if distance:
                    ok = (a >= 0) & (a < MAJOR)
                origin = lax.max(lax.min(a, MAJOR - 1), 0) * minor + lax.rem(at.b + db, minor)
                slot = wslot(origin, fpart)
                if ok is None:
                    at.arrived(slot, f_recv.at[origin, fpart])
                else:
                    @pl.when(ok)
                    def _():
                        at.arrived(slot, f_recv.at[origin, fpart])
                to_replicas(origin, ok)

    ffn_minor(0)

    if wparts == 2:
        for i, (da, db) in enumerate(peers):
            origin = at.at(-da, -db)
            slot = wcols_ref.at[origin, wpart]
            at.arrived(slot, w_recv.at[origin, wpart])
            at.send(slot, slot, wc_send.at[i], w_recv.at[origin, wpart], rep=at.flip(1))

    for da, db in peers:
        origin = at.at(-da, -db)
        at.arrived(packets.at[origin], p_recv.at[origin])
    vectors = jnp.zeros((8, width), F32)
    scales = jnp.zeros((1, 128), F32)
    lanes = lax.broadcasted_iota(jnp.int32, (8, width), 1)
    unit = HEAD // shards
    for j in range(shards):
        piece = packets[j]
        wide = jnp.concatenate([piece, jnp.zeros((8, width - piece.shape[1]), F32)], axis=1)
        wide = jnp.where(lanes < slab, wide, 0.0)
        vectors = vectors + (pltpu.roll(wide, j * slab, 1) if j else wide)
        scale = jnp.where(lanes[0:1, :128] < unit, piece[5:6, :128], 0.0)
        scales = scales + (pltpu.roll(scale, j * unit, 1) if j else scale)
        start_ref[:, j * block : (j + 1) * block] = jnp.broadcast_to(piece[6:7, :block], (8, block))
    rows = lax.broadcasted_iota(jnp.int32, (8, width), 0)
    vec_ref[...] = jnp.where(rows < 5, vectors, 0.0)
    vec_ref[5:6, :128] = scales
    gain = vec_ref[0:1, :]
    column = jnp.broadcast_to(scales, (128, 128)).T[:HEAD, 0:1]
    soft = jnp.maximum(column, 0.0) + jnp.log(1.0 + jnp.exp(-jnp.abs(column)))
    factor = jnp.concatenate([QUERY_BASE / math.sqrt(HEAD) * soft] * local, axis=0)
    own = small_ref[8:16, :]
    tall = jnp.concatenate([own, jnp.zeros((120, 256), F32)], axis=0)
    tall = jnp.concatenate([tall[:, :128].T, tall[:, 128:].T], axis=0)
    bias_query = tall[:slab, 0:1]
    bias_value = tall[:slab, 1:2]

    rows_line.step(2)
    ffn_line.step(2, to_replicas)
    ffn_minor(1)
    for da, db in peers:
        origin = at.at(-da, -db)
        last = wparts - 1 - wpart
        at.arrived(wcols_ref.at[origin, last], w_recv.at[origin, last])
    turned[...] = wcols_ref[...].reshape(width, slab3).T

    def project(origin):
        rows_in = xg[origin].astype(F32)
        scale = lax.rsqrt(jnp.mean(rows_in * rows_in, axis=-1, keepdims=True) + EPS)
        normed = (rows_in * scale * gain).astype(BF16)
        tokens = pl.ds(pl.multiple_of(origin * block, block), block)
        normed_ref[tokens, :] = normed
        out = dot(turned[...], normed, NT)
        query = out[:slab] + bias_query
        query_ref[:, tokens] = query
        qkv_ref[:slab, tokens] = (query * factor).astype(BF16)
        qkv_ref[slab : 2 * slab, tokens] = out[slab : 2 * slab].astype(BF16)
        qkv_ref[2 * slab :, tokens] = (out[2 * slab :] + bias_value).astype(BF16)

    rows_line.step(3)
    ffn_line.step(3, to_replicas)

    def project_major(i, carry):
        project(at.at(i, 0))
        return carry

    def project_minor(i, carry):
        origin = at.at(lax.rem(i, MAJOR), 1 + i // MAJOR)
        at.arrived(xg.at[origin], x_recv.at[origin])
        project(origin)
        return carry

    lax.fori_loop(0, MAJOR, project_major, 0)
    ffn_minor(2)
    lax.fori_loop(0, shards - MAJOR, project_minor, 0)
    ffn_minor(3)

    log_ref[...] = jnp.zeros_like(log_ref)
    for i in range(length // qblock):
        reach = (i + 1) * qblock
        span = slice(i * qblock, reach)
        starts = start_ref[0:1, span]
        key_place = lax.broadcasted_iota(jnp.int32, (reach, qblock), 0).astype(F32)
        query_place = (i * qblock + lax.broadcasted_iota(jnp.int32, (1, qblock), 1)).astype(F32)
        allowed = (key_place >= starts) & (key_place <= query_place)
        for h in range(local):
            head = slice(h * HEAD, (h + 1) * HEAD)
            queries = qkv_ref[h * HEAD : (h + 1) * HEAD, span]
            keys = qkv_ref[slab + h * HEAD : slab + (h + 1) * HEAD, :reach]
            values = qkv_ref[2 * slab + h * HEAD : 2 * slab + (h + 1) * HEAD, :reach]
            scores = jnp.where(allowed, dot(keys, queries, TN), MASKED)
            top = jnp.max(scores, axis=0, keepdims=True)
            powers = jnp.exp(scores - top)
            total = jnp.sum(powers, axis=0, keepdims=True)
            probs = (powers * (1.0 / total)).astype(BF16)
            log_ref[h : h + 1, span] = top + jnp.log(total)
            context[head, span] = dot(values, probs).astype(BF16)
        mine = pl.ds(pl.multiple_of(me * slab, 16), slab)
        for j in range(i * qblock // block, reach // block):
            piece = slice(j * block, (j + 1) * block)
            at.send(context.at[:, piece], att.at[mine, :], a_send.at[j], a_recv.at[me], shard=j, when=me != j)

            @pl.when(me == j)
            def _():
                att[mine, :] = context[:, piece]

    order = [(0, db) for db in range(1, minor)]
    order += [(da, db) for da in range(1, MAJOR) for db in range(minor)]
    if fparts == 4:
        for da, db in order:
            origin = at.at(da, db)
            part = flipped(fpart, 2)
            slot = wslot(origin, part)
            at.arrived(slot, f_recv.at[origin, part])
            at.send(slot, slot, fc_send.at[origin, 1], f_recv.at[origin, part], rep=at.flip(1))
    for da, db in peers:
        origin = at.at(-da, -db)
        at.arrived(att.at[pl.ds(pl.multiple_of(origin * slab, 16), slab), :], a_recv.at[origin])
    others = [flipped(fpart, 1)] + ([flipped(flipped(fpart, 1), 2)] if fparts == 4 else [])
    for da, db in order:
        origin = at.at(da, db)
        for part in others:
            at.arrived(wslot(origin, part), f_recv.at[origin, part])

    keep_row = small_ref[10:11, :block]
    b_out, gain_two, b_up, b_down = (vec_ref[i : i + 1, :] for i in range(1, 5))
    att_t = (att[...].astype(F32) * keep_row).astype(BF16)
    halves = xt_ref.shape[2]
    xt_ref[0] = att_t.reshape(shards, halves, slab // halves, block)
    mixed = x_ref[...].astype(F32) + dot(att_t.T, weights[0]) + b_out
    r = lax.rsqrt(jnp.mean(mixed * mixed, axis=-1, keepdims=True) + EPS)
    normed_two = (mixed * r * gain_two).astype(BF16)
    xt_ref[1] = normed_two.T.reshape(shards, halves, slab // halves, block)
    hidden = dot(normed_two, weights[1]) + b_up
    s = 1.0 / (1.0 + jnp.exp(-hidden))
    act = (hidden * s).astype(BF16)
    xt_ref[2] = act.T.reshape(shards, halves, slab // halves, block)
    out_ref[...] = (mixed + dot(act, weights[2]) + b_down).astype(BF16)
    dy_ref[2] = cot_ref[...]
    cot = cot_ref[...].astype(F32)
    g_hidden = dot(cot_ref[...], weights[2], NT) * (s + hidden * s * (1.0 - s))
    low = g_hidden.astype(BF16)
    dy_ref[1] = low
    g_normed = dot(low, weights[1], NT)
    weighted = gain_two * g_normed
    g_mixed = cot + r * weighted - mixed * (r * r * r) * jnp.mean(mixed * weighted, axis=-1, keepdims=True)
    gmixed_ref[...] = g_mixed
    low = g_mixed.astype(BF16)
    dy_ref[0] = low
    dctx_ref[...] = (dot(weights[0], low, NT).astype(BF16).astype(F32) * keep_row).astype(BF16)
    row_ref[...] = jnp.zeros_like(row_ref)
    row_ref[1:2, :] = jnp.sum(g_mixed, axis=0, keepdims=True)
    row_ref[2:3, :] = jnp.sum(g_normed * mixed * r, axis=0, keepdims=True)
    row_ref[3:4, :] = jnp.sum(g_hidden, axis=0, keepdims=True)
    row_ref[4:5, :] = jnp.sum(cot, axis=0, keepdims=True)
    at.settle()


def front(shards, inputs, small, w_qkv, w_out, w_up, w_down, cotangent):
    block, width = inputs.shape
    slab = width // shards
    length = shards * block
    wparts = 2 if slab % 32 == 0 else 1
    fparts = parts_of(slab)
    halves = 2 if fparts == 4 else 1
    minor = shards // MAJOR
    peers = shards - 1
    shape = jax.ShapeDtypeStruct
    shapes = (
        shape((length, width), BF16),
        shape((3 * slab, length), BF16),
        shape((slab, length), F32),
        shape((8, length), F32),
        shape((8, width), F32),
        shape((8, length), F32),
        shape((shards, wparts, slab // wparts, 3 * slab), BF16),
        shape((block, width), BF16),
        shape((block, width), F32),
        shape((3, shards, halves, slab // halves, block), BF16),
        shape((3, block, width), BF16),
        shape((width, block), BF16),
        shape((8, width), F32),
    )
    dma = pltpu.SemaphoreType.DMA
    vm = pltpu.VMEM
    return pl.pallas_call(
        functools.partial(front_kernel, shards, wparts, fparts, 2 * block),
        out_shape=shapes,
        in_specs=[VMEM] * 3 + [ANY] * 3 + [VMEM],
        out_specs=[VMEM] * len(shapes),
        scratch_shapes=[
            vm((shards, block, width), BF16),
            vm((shards, 8, 256), F32),
            vm((shards, wparts, slab // wparts, 3 * slab), BF16),
            vm((3 * slab, width), BF16),
            vm((slab, length), BF16),
            vm((width, block), BF16),
            vm((3, width, width), BF16),
            dma((2, MAJOR)), dma((MAJOR, minor - 1)), dma((shards,)),
            dma((peers,)), dma((shards,)),
            dma((peers,)), dma((shards, wparts)), dma((peers,)),
            dma((2, MAJOR)), dma((MAJOR, minor - 1)), dma((shards, fparts)),
            dma((shards,)), dma((shards, 2)),
            dma((3,)), dma((shards,)), dma((shards,)),
        ],
        compiler_params=pltpu.CompilerParams(
            collective_id=0, has_side_effects=True, vmem_limit_bytes=58 << 20
        ),
        name="front",
    )(inputs, small, w_qkv, w_out, w_up, w_down, cotangent)


def pack(positions, segment_ids, gain_one, b_query, b_value, query_scale, b_out, gain_two, b_up, b_down):
    block = positions.shape[-1]
    me = lax.axis_index("shard")
    starts = (me * block + lax.iota(jnp.int32, block) - positions.reshape(block)).astype(F32)
    keep = (segment_ids.reshape(block) != 0).astype(F32)
    table = {
        0: gain_one, 1: b_out, 2: gain_two, 3: b_up, 4: b_down, 5: query_scale, 6: starts,
        8: b_query, 9: b_value, 10: keep,
    }
    total = jnp.zeros((16, 256), F32)
    for row, vector in table.items():
        total = total + jnp.pad(vector.astype(F32)[None], ((row, 15 - row), (0, 256 - vector.shape[0])))
    return total


def back_kernel(
    shards, replicas, parts, qblock,
    x_ref, gmixed_ref, xt_ref, dy_ref, dctx_ref, qkv_ref, query_ref, log_ref, start_ref, normed_ref, wcols_ref,
    vec_ref, row_ref,
    fin_ref, gw_ref, gin_ref, small_ref,
    dctx, grads, turned, proj,
    left, right, stash, sums, from_x, from_z, extra,
    part_gn, gn_x, gn_z,
    gw, gw_core, gw_y, gw_sum, gw_land, gw_extra,
    windows, small_land, small_got,
    d_send, d_recv, y_send, y_recv, c_send, c_recv, x_send, x_recv, z_send, z_recv,
    r_send, r_recv, e_send, e_recv,
    nx_send, nx_recv, nz_send, nz_recv,
    wc_send, wc_recv, wy_send, wy_recv, wa_send, wa_recv, wr_send, wr_recv, we_send, we_recv,
    v_send, v_recv, b_send, b_recv,
):
    at = Place(shards)
    me, minor = at.me, at.minor
    slab3, length = qkv_ref.shape
    slab = slab3 // 3
    local = slab // HEAD
    block = length // shards
    width = normed_ref.shape[1]
    cols = width // 2
    peers = at.peers()
    core = lax.rem(at.rep, 2)
    mine = lax.rem(at.rep, parts)
    i_part = lax.rem(mine, 2) if parts == 4 else 0
    j_part = mine // 2 if parts == 4 else mine
    every = []
    mask = 1
    while mask < replicas:
        every.append(mask)
        mask *= 2
    extras = [m for m in every if m >= parts]
    at.greet(tuple(every))
    mats = (2, 1, 0)

    def lane(n, size):
        return pl.ds(pl.multiple_of(n * size, 128), size)

    for i, (da, db) in enumerate(peers):
        dest = at.at(da, db)
        at.send(
            dctx_ref.at[pl.ds(pl.multiple_of(dest * slab, 16), slab), :],
            dctx.at[:, lane(me, block)], d_send.at[i], d_recv.at[me], shard=dest,
        )
    def slot(n):
        return slice(n * block, (n + 1) * block)

    for m in mats:
        if parts == 4:
            far = at.flip(2)
            at.send(xt_ref.at[m, :, i_part], left.at[m, :, :, slot(1)], y_send.at[m, 0], y_recv.at[m, 0], rep=far)
            at.send(
                dy_ref.at[m, :, lane(1 - j_part, cols)], right.at[m, slot(1), :],
                y_send.at[m, 1], y_recv.at[m, 1], rep=far,
            )
            at.send(xt_ref.at[m, :, 1 - i_part], stash.at[m], y_send.at[m, 2], y_recv.at[m, 2], rep=far)
            near = 2
            at.send(
                xt_ref.at[m, :, 1 - i_part], left.at[m, :, :, slot(near)], c_send.at[m, 0], c_recv.at[m, 0],
                rep=at.flip(1),
            )
            at.send(
                dy_ref.at[m, :, lane(j_part, cols)], right.at[m, slot(near), :],
                c_send.at[m, 1], c_recv.at[m, 1], rep=at.flip(1),
            )
        else:
            near = 1
            at.send(
                xt_ref.at[m, :, 0], left.at[m, :, :, slot(near)], c_send.at[m, 0], c_recv.at[m, 0], rep=at.flip(1)
            )
            at.send(
                dy_ref.at[m, :, lane(1 - j_part, cols)], right.at[m, slot(near), :],
                c_send.at[m, 1], c_recv.at[m, 1], rep=at.flip(1),
            )
        left[m, :, :, slot(0)] = xt_ref[m, :, i_part]
        right[m, slot(0), :] = dy_ref[m, :, lane(j_part, cols)]
    dctx[:, lane(me, block)] = dctx_ref[pl.ds(pl.multiple_of(me * slab, 16), slab), :]

    def relay(m):
        if parts == 4:
            at.arrived(left.at[m, :, :, slot(1)], y_recv.at[m, 0])
            at.arrived(right.at[m, slot(1), :], y_recv.at[m, 1])
            at.arrived(stash.at[m], y_recv.at[m, 2])
            at.send(stash.at[m], left.at[m, :, :, slot(3)], c_send.at[m, 2], c_recv.at[m, 2], rep=at.flip(1))
            at.send(
                right.at[m, slot(1), :], right.at[m, slot(3), :], c_send.at[m, 3], c_recv.at[m, 3], rep=at.flip(1)
            )

    def weight(m):
        near = 2 if parts == 4 else 1
        at.arrived(left.at[m, :, :, slot(near)], c_recv.at[m, 0])
        at.arrived(right.at[m, slot(near), :], c_recv.at[m, 1])
        if parts == 4:
            at.arrived(left.at[m, :, :, slot(3)], c_recv.at[m, 2])
            at.arrived(right.at[m, slot(3), :], c_recv.at[m, 3])
        rows = left.shape[1] * left.shape[2]
        out = dot(left[m].reshape(rows, parts * block), right[m])
        sums[m] = out.reshape(sums.shape[1:]).astype(BF16)
        for db in range(1, minor):
            at.send(
                sums.at[m, :, lax.rem(at.b + db, minor)], from_x.at[m, db - 1],
                x_send.at[m, db - 1], x_recv.at[m, db - 1], shard=at.at(0, db),
            )

    def after_x(m):
        for db in range(1, minor):
            at.arrived(from_x.at[m, db - 1], x_recv.at[m, db - 1])
        for da in range(1, MAJOR + 1):
            ta = lax.rem(at.a + da, MAJOR)
            total = sums[m, ta, at.b].astype(F32)
            for db in range(1, minor):
                total = total + from_x[m, db - 1, ta].astype(F32)
            sums[m, ta, at.b] = total.astype(BF16)
            if da < MAJOR:
                at.send(
                    sums.at[m, ta, at.b], from_z.at[m, da - 1], z_send.at[m, da - 1], z_recv.at[m, da - 1],
                    shard=at.at(da, 0),
                )

    def fin_slot(part, m=None):
        row, rows, col, wide = part_box(part, parts, slab, width)
        box = (pl.ds(pl.multiple_of(row, 16), rows), pl.ds(pl.multiple_of(col, 128), wide))
        return fin_ref.at[(slice(None) if m is None else m,) + box]

    def after_z(m):
        total = sums[m, at.a, at.b].astype(F32)
        for da in range(1, MAJOR):
            at.arrived(from_z.at[m, da - 1], z_recv.at[m, da - 1])
            total = total + from_z[m, da - 1].astype(F32)
        fin_slot(mine, m)[...] = total.astype(BF16)

    scales = vec_ref[5:6, :128]
    column = jnp.broadcast_to(scales, (128, 128)).T[:HEAD, 0:1]
    base = QUERY_BASE / math.sqrt(HEAD)
    soft = jnp.maximum(column, 0.0) + jnp.log(1.0 + jnp.exp(-jnp.abs(column)))
    factor = base * soft
    grads[...] = jnp.zeros_like(grads)
    for da, db in peers:
        origin = at.at(-da, -db)
        at.arrived(dctx.at[:, lane(origin, block)], d_recv.at[origin])

    def attend(i):
        reach = (i + 1) * qblock
        span = slice(i * qblock, reach)
        starts = start_ref[0:1, span]
        key_place = lax.broadcasted_iota(jnp.int32, (reach, qblock), 0).astype(F32)
        query_place = (i * qblock + lax.broadcasted_iota(jnp.int32, (1, qblock), 1)).astype(F32)
        allowed = (key_place >= starts) & (key_place <= query_place)
        for h in range(local):
            queries = qkv_ref[h * HEAD : (h + 1) * HEAD, span]
            keys = qkv_ref[slab + h * HEAD : slab + (h + 1) * HEAD, :reach]
            values = qkv_ref[2 * slab + h * HEAD : 2 * slab + (h + 1) * HEAD, :reach]
            gctx = dctx[h * HEAD : (h + 1) * HEAD, span]
            scores = dot(keys, queries, TN)
            probs = jnp.where(allowed, jnp.exp(scores - log_ref[h : h + 1, span]), 0.0)
            gprobs = dot(values, gctx, TN)
            delta = jnp.sum(probs * gprobs, axis=0, keepdims=True)
            gscores = (probs * (gprobs - delta)).astype(BF16)
            low = probs.astype(BF16)
            grads[h * HEAD : (h + 1) * HEAD, span] = dot(keys, gscores)
            kv = slice(slab + h * HEAD, slab + (h + 1) * HEAD)
            grads[kv, :reach] += dot(queries, gscores, NT)
            kv = slice(2 * slab + h * HEAD, 2 * slab + (h + 1) * HEAD)
            grads[kv, :reach] += dot(gctx, low, NT)

    steps = length // qblock
    for i in range(steps):
        attend(i)
        if i == steps - 3:
            relay(mats[0])
    relay(mats[1])

    gscale = jnp.zeros((HEAD, 1), F32)
    for h in range(local):
        rows = slice(h * HEAD, (h + 1) * HEAD)
        scaled = grads[rows, :]
        gscale = gscale + jnp.sum(scaled * query_ref[rows, :], axis=1, keepdims=True)
        grads[rows, :] = scaled * factor
    gscale = gscale * (base / (1.0 + jnp.exp(-column)))
    bias_q = jnp.sum(grads[:slab, :], axis=1, keepdims=True)
    bias_v = jnp.sum(grads[2 * slab :, :], axis=1, keepdims=True)
    turned[:slab3, :] = grads[...].astype(BF16)
    proj[...] = turned[...].T[:, :slab3]

    wcols = wcols_ref[...].reshape(width, slab3)

    def partial(origin, acc):
        tokens = lane(origin, block)
        out = dot(proj[tokens, :], wcols, NT)
        part_gn[origin] = out.astype(BF16)
        weighted = out * normed_ref[tokens, :].astype(F32)
        return acc + jnp.sum(weighted.reshape(block // 8, 8, width), axis=0)

    def away_copy(i):
        db = 1 + i // MAJOR
        to = at.at(lax.rem(i + 1, MAJOR), db)
        return to, pltpu.make_async_remote_copy(
            src_ref=part_gn.at[to], dst_ref=gn_x.at[db - 1, to // minor],
            send_sem=nx_send.at[db - 1, to // minor], recv_sem=nx_recv.at[db - 1, to // minor],
            device_id=(at.at(0, db), at.rep), device_id_type=MESH,
        )

    def away(i, acc):
        to, copy = away_copy(i)
        acc = partial(to, acc)
        copy.start()
        return acc

    gain_rows = jnp.zeros((8, width), F32)
    gain_rows = lax.fori_loop(0, shards - MAJOR, away, gain_rows)

    rp = width // (shards * parts)
    halves = parts // 2
    whole = dot(normed_ref[...], proj[...], TN)
    gw[...] = whole.reshape(shards, parts, rp, slab3).astype(BF16)
    for k in range(halves):
        at.send(gw.at[:, (1 - core) + 2 * k], gw_core.at[k], wc_send.at[k], wc_recv.at[k], rep=at.flip(1))
    weight(mats[0])
    gain_rows = lax.fori_loop(0, MAJOR, lambda i, acc: partial(at.at(i, 0), acc), gain_rows)
    for k in range(halves):
        at.arrived(gw_core.at[k], wc_recv.at[k])
        gw_core[k] = gw[:, core + 2 * k] + gw_core[k]
    km = mine // 2 if parts == 4 else 0
    if parts == 4:
        at.send(gw_core.at[1 - km], gw_y, wy_send.at[0], wy_recv.at[0], rep=at.flip(2))
    weight(mats[1])
    relay(mats[2])

    gain_row = jnp.sum(gain_rows, axis=0, keepdims=True) / vec_ref[0:1, :]
    rows = row_ref[...]
    place = lax.broadcasted_iota(jnp.int32, (8, width), 0)
    rows = jnp.where(place == 0, jnp.broadcast_to(gain_row, (8, width)), rows)
    turn_in = jnp.concatenate(
        [jnp.broadcast_to(gscale, (HEAD, 128)), jnp.zeros((128 - HEAD, 128), F32)], axis=0
    )
    scale_row = jnp.broadcast_to(turn_in.T[0:1, :], (8, 128))
    scale_tile = jnp.where(lax.broadcasted_iota(jnp.int32, (8, 128), 0) == 5, scale_row, 0.0)
    for j in range(shards):
        first = j * slab // 128 * 128
        window = rows[:, first : min(first + 384, width)]
        if window.shape[1] < 384:
            window = jnp.concatenate([window, jnp.zeros((8, 384 - window.shape[1]), F32)], axis=1)
        windows[j, :, :384] = window
        windows[j, :, 384:] = scale_tile
    for i, (da, db) in enumerate(peers):
        dest = at.at(da, db)
        at.send(windows.at[dest], small_land.at[me], v_send.at[i], v_recv.at[me], shard=dest)
    small_land[me] = windows[me]

    if parts == 4:
        at.arrived(gw_y, wy_recv.at[0])
        gw_sum[...] = gw_core[km] + gw_y[...]
    else:
        gw_sum[...] = gw_core[0]
    for i, (da, db) in enumerate(peers):
        dest = at.at(da, db)
        at.send(gw_sum.at[dest], gw_land.at[me], wa_send.at[i], wa_recv.at[me], shard=dest)
    gw_land[me] = gw_sum[me]
    weight(mats[2])

    for da in range(1, MAJOR + 1):
        to = at.at(da, 0)
        ta = to // minor
        total = part_gn[to].astype(F32)
        for db in range(1, minor):
            at.arrived(gn_x.at[db - 1, ta], nx_recv.at[db - 1, ta])
            total = total + gn_x[db - 1, ta].astype(F32)
        if da < MAJOR:
            part_gn[to] = total.astype(BF16)
            at.send(part_gn.at[to], gn_z.at[da - 1], nz_send.at[da - 1], nz_recv.at[da - 1], shard=to)
        else:
            gin_ref[...] = total
    after_x(mats[0])
    after_x(mats[1])

    for da, db in peers:
        origin = at.at(-da, -db)
        at.arrived(small_land.at[origin], v_recv.at[origin])
    small = jnp.sum(small_land[...], axis=0)
    lanes = lax.broadcasted_iota(jnp.int32, (slab, 128), 1)
    sides = jnp.concatenate(
        [jnp.where(lanes == 6, bias_q, jnp.where(lanes == 7, bias_v, 0.0)), jnp.zeros((256 - slab, 128), F32)],
        axis=0,
    )
    sides = jnp.concatenate([sides[:128].T[:8], sides[128:].T[:8]], axis=1)
    shift = lax.rem(me * slab, 128)
    window = pltpu.roll(small[:, :384], lax.rem(384 - shift, 384), 1)
    tall = lax.broadcasted_iota(jnp.int32, (8, 256), 0)
    small_got[0, :, :256] = jnp.where(tall < 5, window[:, :256], sides)
    unit = HEAD // shards
    small_got[0, :, 256:] = pltpu.roll(small[:, 384:], lax.rem(128 - me * unit, 128), 1)

    def small_round(n):
        at.send(
            small_got.at[2 * n], small_got.at[2 * n + 1], b_send.at[n], b_recv.at[n], rep=at.flip(every[n])
        )

    def small_add(n):
        at.arrived(small_got.at[2 * n + 1], b_recv.at[n])
        small_got[2 * n + 2] = small_got[2 * n] + small_got[2 * n + 1]

    small_round(0)
    for da, db in peers:
        origin = at.at(-da, -db)
        at.arrived(gw_land.at[origin], wa_recv.at[origin])
    for n, mask in enumerate(extras):
        if n == 0:
            gw_extra[0] = gw_land[...]
        at.send(gw_extra.at[2 * n], gw_extra.at[2 * n + 1], we_send.at[n], we_recv.at[n], rep=at.flip(mask))
        at.arrived(gw_extra.at[2 * n + 1], we_recv.at[n])
        gw_extra[2 * n + 2] = gw_extra[2 * n] + gw_extra[2 * n + 1]
    land = gw_extra.at[2 * len(extras)] if extras else gw_land
    for j in range(shards):
        for t in range(3):
            first = t * width + j * slab
            gw_ref[mine, :, first : first + slab] = land[j, :, t * slab : (t + 1) * slab]

    def hand_round(ref_slot, send_sem, recv_sem):
        have, rounds, k = [mine], [], 0
        for mask in ((2, 1) if parts == 4 else (1,)):
            sends = []
            for part in have:
                sends.append((part, mask, k))
                k += 1
            fresh = [flipped(part, mask) for part in have]
            rounds.append((sends, fresh))
            have = have + fresh

        def go(n):
            for part, mask, k in rounds[n][0]:
                at.send(ref_slot(part), ref_slot(part), send_sem.at[k], recv_sem.at[part], rep=at.flip(mask))

        def take(n):
            for part in rounds[n][1]:
                at.arrived(ref_slot(part), recv_sem.at[part])

        return go, take, len(rounds)

    gw_go, gw_take, count = hand_round(lambda part: gw_ref.at[part], wr_send, wr_recv)
    fin_go, fin_take, _ = hand_round(fin_slot, r_send, r_recv)
    gw_go(0)
    small_add(0)
    small_round(1)
    after_x(mats[2])

    total = gin_ref[...]
    for da in range(1, MAJOR):
        at.arrived(gn_z.at[da - 1], nz_recv.at[da - 1])
        total = total + gn_z[da - 1].astype(F32)
    x = x_ref[...].astype(F32)
    r = lax.rsqrt(jnp.mean(x * x, axis=-1, keepdims=True) + EPS)
    weighted = vec_ref[0:1, :] * total
    gin_ref[...] = gmixed_ref[...] + r * weighted - x * (r * r * r) * jnp.mean(x * weighted, axis=-1, keepdims=True)

    for m in mats:
        after_z(m)
    for n, mask in enumerate(extras):
        if n == 0:
            extra[0] = fin_slot(mine)[...]
        at.send(extra.at[2 * n], extra.at[2 * n + 1], e_send.at[n], e_recv.at[n], rep=at.flip(mask))
        at.arrived(extra.at[2 * n + 1], e_recv.at[n])
        extra[2 * n + 2] = extra[2 * n] + extra[2 * n + 1]
    if extras:
        fin_slot(mine)[...] = extra[2 * len(extras)]
    fin_go(0)
    for n in range(count):
        gw_take(n)
        if n + 1 < count:
            gw_go(n + 1)
        fin_take(n)
        if n + 1 < count:
            fin_go(n + 1)
    for n in range(1, len(every)):
        small_add(n)
        if n + 1 < len(every):
            small_round(n + 1)
    small_ref[...] = small_got[2 * len(every)]

    def away_wait(i, carry):
        away_copy(i)[1].wait_send()
        return carry

    lax.fori_loop(0, shards - MAJOR, away_wait, 0)
    at.settle()


def back(shards, replicas, x, g_mixed, xt, dy, dctx, qkv, query, log, start, normed, wcols, vec, rows):
    slab3, length = qkv.shape
    slab = slab3 // 3
    block, width = x.shape
    parts = parts_of(slab)
    rp = slab // parts
    rows_part = slab // 2 if parts == 4 else slab
    cols = width // 2
    minor = shards // MAJOR
    halves = parts // 2
    peers = shards - 1
    dma = pltpu.SemaphoreType.DMA
    bits = (replicas - 1).bit_length()
    more = bits - (parts - 1).bit_length()
    vm = pltpu.VMEM
    turned_rows = -(-slab3 // 128) * 128
    shape = jax.ShapeDtypeStruct
    return pl.pallas_call(
        functools.partial(back_kernel, shards, replicas, parts, 2 * block),
        out_shape=(
            shape((3, slab, width), BF16),
            shape((parts, rp, 3 * width), BF16),
            shape((block, width), F32),
            shape((8, 384), F32),
        ),
        in_specs=[VMEM] * 13,
        out_specs=[VMEM] * 4,
        scratch_shapes=[
            vm((slab, length), BF16),
            vm((slab3, length), F32),
            vm((turned_rows, length), BF16),
            vm((length, slab3), BF16),
            vm((3, shards, rows_part, parts * block), BF16),
            vm((3, parts * block, cols), BF16),
            vm((3, shards, rows_part, block), BF16),
            vm((3, MAJOR, minor, rows_part, cols), BF16),
            vm((3, minor - 1, MAJOR, rows_part, cols), BF16),
            vm((3, MAJOR - 1, rows_part, cols), BF16),
            vm((2 * more + 1, 3, rows_part, cols), BF16),
            vm((shards, block, width), BF16),
            vm((minor - 1, MAJOR, block, width), BF16),
            vm((MAJOR - 1, block, width), BF16),
            vm((shards, parts, rp, slab3), BF16),
            vm((halves, shards, rp, slab3), BF16),
            vm((shards, rp, slab3), BF16),
            vm((shards, rp, slab3), BF16),
            vm((shards, rp, slab3), BF16),
            vm((2 * more + 1, shards, rp, slab3), BF16),
            vm((shards, 8, 512), F32),
            vm((shards, 8, 512), F32),
            vm((2 * bits + 1, 8, 384), F32),
            dma((peers,)), dma((shards,)),
            dma((3, 3)), dma((3, 3)),
            dma((3, 4)), dma((3, 4)),
            dma((3, minor - 1)), dma((3, minor - 1)),
            dma((3, MAJOR - 1)), dma((3, MAJOR - 1)),
            dma((parts,)), dma((parts,)),
            dma((max(more, 1),)), dma((max(more, 1),)),
            dma((minor - 1, MAJOR)), dma((minor - 1, MAJOR)),
            dma((MAJOR - 1,)), dma((MAJOR - 1,)),
            dma((halves,)), dma((halves,)),
            dma((1,)), dma((1,)),
            dma((peers,)), dma((shards,)),
            dma((parts,)), dma((parts,)),
            dma((max(more, 1),)), dma((max(more, 1),)),
            dma((peers,)), dma((shards,)),
            dma((bits,)), dma((bits,)),
        ],
        compiler_params=pltpu.CompilerParams(
            collective_id=1, has_side_effects=True, vmem_limit_bytes=58 << 20
        ),
        name="back",
    )(x, g_mixed, xt, dy, dctx, qkv, query, log, start, normed, wcols, vec, rows)


def on_device(
    inputs, segment_ids, positions, gain_one, w_qkv, b_query, b_value, query_scale, w_out, b_out,
    gain_two, w_up, b_up, w_down, b_down, cotangent,
):
    shards = lax.axis_size("shard")
    replicas = lax.axis_size("replica")
    block, width = inputs.shape[1:]
    slab = width // shards
    x = inputs.reshape(block, width)
    small = pack(positions, segment_ids, gain_one, b_query, b_value, query_scale, b_out, gain_two, b_up, b_down)
    normed, qkv, query, log, vec, start, wcols, output, g_mixed, xt, dy, dctx, rows = front(
        shards, x, small, w_qkv, w_out, w_up, w_down, cotangent.reshape(block, width)
    )
    fin, gw, input_grad, small = back(
        shards, replicas, x, g_mixed, xt, dy, dctx, qkv, query, log, start, normed, wcols, vec, rows
    )
    gw = gw.reshape(slab, 3 * width).astype(F32)
    fin = fin.astype(F32)
    unit = HEAD // shards
    return (
        output[None], input_grad[None], small[0, :slab], gw, small[6, :slab], small[7, :slab],
        small[5, 256 : 256 + unit], fin[0], small[1, :slab], small[2, :slab], fin[1], small[3, :slab],
        fin[2], small[4, :slab],
    )


def solution(mesh):
    rows = P("replica", "shard", None)
    ids = P("replica", "shard")
    vector = P("shard")
    matrix = P("shard", None)
    in_specs = (
        rows, ids, ids, vector, matrix, vector, vector, vector, matrix, vector, vector, matrix, vector,
        matrix, vector, rows,
    )
    out_specs = (
        rows, rows, vector, matrix, vector, vector, vector, matrix, vector, vector, matrix, vector, matrix,
        vector,
    )
    return jax.shard_map(on_device, mesh=mesh, in_specs=in_specs, out_specs=out_specs, check_vma=False)
```

```python
import functools
import math

import jax
import jax.numpy as jnp
from jax import lax
from jax.experimental import pallas as pl
from jax.experimental.pallas import tpu as pltpu
from jax.sharding import PartitionSpec as P

HEADS = 16
HEAD = 80
EPS = 1e-06
QUERY_BASE = 1.442695041
MASKED = -1000000000.0
MESH = pl.DeviceIdType.MESH
MAJOR = 4
VMEM = pl.BlockSpec(memory_space=pltpu.VMEM)
ANY = pl.BlockSpec(memory_space=pl.ANY)
F32 = jnp.float32
BF16 = jnp.bfloat16
NN = (((1,), (0,)), ((), ()))
NT = (((1,), (1,)), ((), ()))
TN = (((0,), (0,)), ((), ()))


def dot(lhs, rhs, dims=NN):
    return lax.dot_general(lhs, rhs, dims, preferred_element_type=F32)


class Place:
    def __init__(self, shards):
        self.shards = shards
        self.minor = shards // MAJOR
        self.me = lax.axis_index("shard")
        self.rep = lax.axis_index("replica")
        self.a = self.me // self.minor
        self.b = lax.rem(self.me, self.minor)
        self.started = []

    def at(self, da, db):
        a = lax.rem(self.a + da + MAJOR, MAJOR)
        b = lax.rem(self.b + db + self.minor, self.minor)
        return a * self.minor + b

    def peers(self):
        return [(da, db) for da in range(MAJOR) for db in range(self.minor) if da or db]

    def flip(self, mask):
        bit = lax.rem(self.rep // mask, 2)
        return self.rep + mask - 2 * mask * bit

    def greet(self, masks):
        barrier = pltpu.get_barrier_semaphore()
        for da, db in self.peers():
            pl.semaphore_signal(
                barrier, inc=1, device_id=(self.at(da, db), self.rep), device_id_type=MESH
            )
        for mask in masks:
            pl.semaphore_signal(
                barrier, inc=1, device_id=(self.me, self.flip(mask)), device_id_type=MESH
            )
        pl.semaphore_wait(barrier, len(self.peers()) + len(masks))

    def send(self, src, dst, ssem, rsem, shard=None, rep=None, when=None):
        copy = pltpu.make_async_remote_copy(
            src_ref=src,
            dst_ref=dst,
            send_sem=ssem,
            recv_sem=rsem,
            device_id=(self.me if shard is None else shard, self.rep if rep is None else rep),
            device_id_type=MESH,
        )
        if when is None:
            copy.start()
        else:
            @pl.when(when)
            def _():
                copy.start()
        self.started.append((when, copy))

    def arrived(self, dst, rsem):
        pltpu.make_async_remote_copy(
            src_ref=dst,
            dst_ref=dst,
            send_sem=rsem,
            recv_sem=rsem,
            device_id=(self.me, self.rep),
            device_id_type=MESH,
        ).wait_recv()

    def exchange(self, src, dst, ssem, rsem, rep):
        self.send(src, dst, ssem, rsem, rep=rep)
        self.arrived(dst, rsem)
        self.started.pop()[1].wait_send()

    def settle(self):
        for when, copy in self.started:
            if when is None:
                copy.wait_send()
            else:
                @pl.when(when)
                def _():
                    copy.wait_send()
        self.started = []


class Line:
    def __init__(self, at, slot, major_send, minor_send, recv):
        self.at, self.slot = at, slot
        self.major_send, self.minor_send, self.recv = major_send, minor_send, recv

    def onward(self, origin, up, down, d):
        at = self.at
        if up is not None:
            at.send(
                self.slot(origin), self.slot(origin), self.major_send.at[0, d], self.recv(origin),
                shard=lax.min(at.a + 1, MAJOR - 1) * at.minor + at.b, when=up,
            )
        if down is not None:
            at.send(
                self.slot(origin), self.slot(origin), self.major_send.at[1, d], self.recv(origin),
                shard=lax.max(at.a - 1, 0) * at.minor + at.b, when=down,
            )

    def across(self, origin, when=None):
        at = self.at
        for db in range(1, at.minor):
            at.send(
                self.slot(origin), self.slot(origin), self.minor_send.at[origin // at.minor, db - 1],
                self.recv(origin), shard=at.at(0, db), when=when,
            )

    def begin(self):
        at = self.at
        self.onward(at.me, at.a + 1 < MAJOR, at.a > 0, 0)
        self.across(at.me)

    def sides(self, d):
        at = self.at
        for side in (-1, 1):
            ok = (at.a - d >= 0) if side < 0 else (at.a + d < MAJOR)
            origin = lax.max(at.a - d, 0) if side < 0 else lax.min(at.a + d, MAJOR - 1)
            yield side, ok, origin * at.minor + at.b

    def take(self, d, then=None):
        for side, ok, origin in self.sides(d):
            @pl.when(ok)
            def _():
                self.at.arrived(self.slot(origin), self.recv(origin))

            if then is not None:
                then(origin, ok)

    def along(self, d):
        at = self.at
        if d + 1 < MAJOR:
            for side, ok, origin in self.sides(d):
                if side < 0:
                    self.onward(origin, ok & (at.a + 1 < MAJOR), None, d)
                else:
                    self.onward(origin, None, ok & (at.a > 0), d)

    def aside(self, d):
        for side, ok, origin in self.sides(d):
            self.across(origin, when=ok)

    def step(self, d, then=None):
        self.take(d, then)
        self.along(d)
        self.aside(d)


def parts_of(rows):
    return 4 if rows % 32 == 0 else 2


def part_box(part, parts, rows, cols):
    if parts == 4:
        i, j, rows = lax.rem(part, 2), part // 2, rows // 2
    else:
        i, j = 0, part
    return i * rows, rows, j * (cols // 2), cols // 2


def flipped(part, mask):
    bit = lax.rem(part // mask, 2)
    return part + mask - 2 * mask * bit


def layer_kernel(
    shards, replicas, wparts, parts, qblock,
    x_ref, small_ref, w_ref, wout_ref, wup_ref, wdown_ref, cot_ref,
    out_ref, fin_ref, gw_ref, gin_ref, small_out_ref,
    normed_ref, qkv_ref, query_ref, log_ref, vec_ref, start_ref, wcols_ref,
    xt_ref, dy_ref, dctx_ref, row_ref, gmixed_ref,
    xg, packets, pieces, turned, context, att, weights,
    dctx, grads, proj, left, right, stash, sums, from_x, from_z, extra,
    gw, gw_core, gw_y, gw_sum, gw_land, gw_extra,
    windows, small_land, small_got,
    xm_send, xn_send, x_recv, p_send, p_recv, w_send, w_recv, wc_send,
    fm_send, fn_send, f_recv, fy_send, fc_send, local_sem, a_send, a_recv,
    d_send, d_recv, gy_send, gy_recv, gc_send, gc_recv, gx_send, gx_recv, gz_send, gz_recv,
    r_send, r_recv, e_send, e_recv, nx_send, nx_recv, nz_send, nz_recv,
    vc_send, vc_recv, vy_send, vy_recv, va_send, va_recv, vr_send, vr_recv, ve_send, ve_recv,
    s_send, s_recv, b_send, b_recv,
):
    at = Place(shards)
    me, minor = at.me, at.minor
    block, width = x_ref.shape
    length = shards * block
    slab = width // shards
    slab3 = 3 * slab
    local = slab // HEAD
    peers = at.peers()
    masks = (2, 1) if parts == 4 else (1,)
    every = []
    bit = 1
    while bit < replicas:
        every.append(bit)
        bit *= 2
    extras = [m for m in every if m >= parts]
    mine = lax.rem(at.rep, parts)
    wpart = lax.rem(at.rep, wparts)

    loads = []
    for m, ref in enumerate((wout_ref, wup_ref, wdown_ref)):
        copy = pltpu.make_async_copy(
            ref, weights.at[m, pl.ds(pl.multiple_of(me * slab, 16), slab), :], local_sem.at[m]
        )
        copy.start()
        loads.append(copy)
    xg[me] = x_ref[...]
    packets[me] = small_ref[:8]
    at.greet(tuple(every))

    def wslot(origin, part):
        row, rows, col, cols = part_box(part, parts, slab, width)
        return weights.at[
            :,
            pl.ds(pl.multiple_of(origin * slab + row, 16), rows),
            pl.ds(pl.multiple_of(col, 128), cols),
        ]

    rows_line = Line(at, lambda o: xg.at[o], xm_send, xn_send, lambda o: x_recv.at[o])
    ffn_line = Line(
        at, lambda o: wslot(o, mine), fm_send, fn_send, lambda o: f_recv.at[o, mine]
    )

    def to_replicas(origin, when=None):
        slot = wslot(origin, mine)
        for mask in masks:
            sem = fy_send.at[origin] if mask == 2 else fc_send.at[origin, 0]
            at.send(slot, slot, sem, f_recv.at[origin, mine], rep=at.flip(mask), when=when)

    rows_line.begin()
    for i, (da, db) in enumerate(peers):
        at.send(packets.at[me], packets.at[me], p_send.at[i], p_recv.at[me], shard=at.at(da, db))
    for copy in loads:
        copy.wait()
    ffn_line.begin()

    cut = slab // wparts
    for j in range(shards):
        for t in range(3):
            first = t * width + j * slab
            pieces[j, :, :, t * slab : (t + 1) * slab] = w_ref[:, first : first + slab].reshape(
                wparts, cut, slab
            )
    for i, (da, db) in enumerate(peers):
        dest = at.at(da, db)
        at.send(
            pieces.at[dest, wpart], wcols_ref.at[me, wpart], w_send.at[i], w_recv.at[me, wpart], shard=dest
        )
    wcols_ref[me] = pieces[me]

    rows_line.step(1)
    ffn_line.step(1, to_replicas)

    def ffn_minor(distance):
        for db in range(1, minor):
            sides = ((-1, 1) if distance else (0,))
            for side in sides:
                a = at.a + side * distance
                ok = None
                if distance:
                    ok = (a >= 0) & (a < MAJOR)
                origin = lax.max(lax.min(a, MAJOR - 1), 0) * minor + lax.rem(at.b + db, minor)
                slot = wslot(origin, mine)
                if ok is None:
                    at.arrived(slot, f_recv.at[origin, mine])
                else:
                    @pl.when(ok)
                    def _():
                        at.arrived(slot, f_recv.at[origin, mine])
                to_replicas(origin, ok)

    ffn_minor(0)

    if wparts == 2:
        for i, (da, db) in enumerate(peers):
            origin = at.at(-da, -db)
            slot = wcols_ref.at[origin, wpart]
            at.arrived(slot, w_recv.at[origin, wpart])
            at.send(slot, slot, wc_send.at[i], w_recv.at[origin, wpart], rep=at.flip(1))

    for da, db in peers:
        origin = at.at(-da, -db)
        at.arrived(packets.at[origin], p_recv.at[origin])
    vectors = jnp.zeros((8, width), F32)
    scales = jnp.zeros((1, 128), F32)
    lanes = lax.broadcasted_iota(jnp.int32, (8, width), 1)
    unit = HEAD // shards
    for j in range(shards):
        piece = packets[j]
        wide = jnp.concatenate([piece, jnp.zeros((8, width - piece.shape[1]), F32)], axis=1)
        wide = jnp.where(lanes < slab, wide, 0.0)
        vectors = vectors + (pltpu.roll(wide, j * slab, 1) if j else wide)
        scale = jnp.where(lanes[0:1, :128] < unit, piece[5:6, :128], 0.0)
        scales = scales + (pltpu.roll(scale, j * unit, 1) if j else scale)
        start_ref[:, j * block : (j + 1) * block] = jnp.broadcast_to(piece[6:7, :block], (8, block))
    rows = lax.broadcasted_iota(jnp.int32, (8, width), 0)
    vec_ref[...] = jnp.where(rows < 5, vectors, 0.0)
    vec_ref[5:6, :128] = scales
    gain = vec_ref[0:1, :]
    column = jnp.broadcast_to(scales, (128, 128)).T[:HEAD, 0:1]
    soft = jnp.maximum(column, 0.0) + jnp.log(1.0 + jnp.exp(-jnp.abs(column)))
    factor = jnp.concatenate([QUERY_BASE / math.sqrt(HEAD) * soft] * local, axis=0)
    own = small_ref[8:16, :]
    tall = jnp.concatenate([own, jnp.zeros((120, 256), F32)], axis=0)
    tall = jnp.concatenate([tall[:, :128].T, tall[:, 128:].T], axis=0)
    bias_query = tall[:slab, 0:1]
    bias_value = tall[:slab, 1:2]

    rows_line.step(2)
    ffn_line.step(2, to_replicas)
    ffn_minor(1)
    for da, db in peers:
        origin = at.at(-da, -db)
        last = wparts - 1 - wpart
        at.arrived(wcols_ref.at[origin, last], w_recv.at[origin, last])
    turned[...] = wcols_ref[...].reshape(width, slab3).T

    def project(origin):
        rows_in = xg[origin].astype(F32)
        scale = lax.rsqrt(jnp.mean(rows_in * rows_in, axis=-1, keepdims=True) + EPS)
        normed = (rows_in * scale * gain).astype(BF16)
        tokens = pl.ds(pl.multiple_of(origin * block, block), block)
        normed_ref[tokens, :] = normed
        out = dot(turned[...], normed, NT)
        query = out[:slab] + bias_query
        query_ref[:, tokens] = query
        qkv_ref[:slab, tokens] = (query * factor).astype(BF16)
        qkv_ref[slab : 2 * slab, tokens] = out[slab : 2 * slab].astype(BF16)
        qkv_ref[2 * slab :, tokens] = (out[2 * slab :] + bias_value).astype(BF16)

    rows_line.step(3)
    ffn_line.step(3, to_replicas)

    def project_major(i, carry):
        project(at.at(i, 0))
        return carry

    def project_minor(i, carry):
        origin = at.at(lax.rem(i, MAJOR), 1 + i // MAJOR)
        at.arrived(xg.at[origin], x_recv.at[origin])
        project(origin)
        return carry

    lax.fori_loop(0, MAJOR, project_major, 0)
    ffn_minor(2)
    lax.fori_loop(0, shards - MAJOR, project_minor, 0)
    ffn_minor(3)

    log_ref[...] = jnp.zeros_like(log_ref)
    for i in range(length // qblock):
        reach = (i + 1) * qblock
        span = slice(i * qblock, reach)
        starts = start_ref[0:1, span]
        key_place = lax.broadcasted_iota(jnp.int32, (reach, qblock), 0).astype(F32)
        query_place = (i * qblock + lax.broadcasted_iota(jnp.int32, (1, qblock), 1)).astype(F32)
        allowed = (key_place >= starts) & (key_place <= query_place)
        for h in range(local):
            head = slice(h * HEAD, (h + 1) * HEAD)
            queries = qkv_ref[h * HEAD : (h + 1) * HEAD, span]
            keys = qkv_ref[slab + h * HEAD : slab + (h + 1) * HEAD, :reach]
            values = qkv_ref[2 * slab + h * HEAD : 2 * slab + (h + 1) * HEAD, :reach]
            scores = jnp.where(allowed, dot(keys, queries, TN), MASKED)
            top = jnp.max(scores, axis=0, keepdims=True)
            powers = jnp.exp(scores - top)
            total = jnp.sum(powers, axis=0, keepdims=True)
            probs = (powers * (1.0 / total)).astype(BF16)
            log_ref[h : h + 1, span] = top + jnp.log(total)
            context[head, span] = dot(values, probs).astype(BF16)
        heads = pl.ds(pl.multiple_of(me * slab, 16), slab)
        for j in range(i * qblock // block, reach // block):
            piece = slice(j * block, (j + 1) * block)
            at.send(context.at[:, piece], att.at[heads, :], a_send.at[j], a_recv.at[me], shard=j, when=me != j)

            @pl.when(me == j)
            def _():
                att[heads, :] = context[:, piece]

    order = [(0, db) for db in range(1, minor)]
    order += [(da, db) for da in range(1, MAJOR) for db in range(minor)]
    if parts == 4:
        for da, db in order:
            origin = at.at(da, db)
            part = flipped(mine, 2)
            slot = wslot(origin, part)
            at.arrived(slot, f_recv.at[origin, part])
            at.send(slot, slot, fc_send.at[origin, 1], f_recv.at[origin, part], rep=at.flip(1))
    for da, db in peers:
        origin = at.at(-da, -db)
        at.arrived(att.at[pl.ds(pl.multiple_of(origin * slab, 16), slab), :], a_recv.at[origin])
    others = [flipped(mine, 1)] + ([flipped(flipped(mine, 1), 2)] if parts == 4 else [])
    for da, db in order:
        origin = at.at(da, db)
        for part in others:
            at.arrived(wslot(origin, part), f_recv.at[origin, part])

    slab3 = 3 * slab
    cols = width // 2
    core = lax.rem(at.rep, 2)
    i_part = lax.rem(mine, 2) if parts == 4 else 0
    j_part = mine // 2 if parts == 4 else mine
    mats = (2, 1, 0)

    def lane(n, size):
        return pl.ds(pl.multiple_of(n * size, 128), size)

    def slot(n):
        return slice(n * block, (n + 1) * block)

    def meet_near(m):
        near = parts // 2
        at.send(
            xt_ref.at[m, :, 1 - i_part if parts == 4 else 0], left.at[m, :, :, slot(near)],
            gc_send.at[m, 0], gc_recv.at[m, 0], rep=at.flip(1),
        )
        at.send(
            dy_ref.at[m, :, lane(j_part if parts == 4 else 1 - j_part, cols)], right.at[m, slot(near), :],
            gc_send.at[m, 1], gc_recv.at[m, 1], rep=at.flip(1),
        )
        left[m, :, :, slot(0)] = xt_ref[m, :, i_part]
        right[m, slot(0), :] = dy_ref[m, :, lane(j_part, cols)]

    def meet_far(m):
        if parts == 4:
            far = at.flip(2)
            at.send(
                xt_ref.at[m, :, i_part], left.at[m, :, :, slot(1)], gy_send.at[m, 0], gy_recv.at[m, 0], rep=far
            )
            at.send(
                dy_ref.at[m, :, lane(1 - j_part, cols)], right.at[m, slot(1), :],
                gy_send.at[m, 1], gy_recv.at[m, 1], rep=far,
            )
            at.send(xt_ref.at[m, :, 1 - i_part], stash.at[m], gy_send.at[m, 2], gy_recv.at[m, 2], rep=far)

    def relay(m):
        if parts == 4:
            at.arrived(left.at[m, :, :, slot(1)], gy_recv.at[m, 0])
            at.arrived(right.at[m, slot(1), :], gy_recv.at[m, 1])
            at.arrived(stash.at[m], gy_recv.at[m, 2])
            at.send(stash.at[m], left.at[m, :, :, slot(3)], gc_send.at[m, 2], gc_recv.at[m, 2], rep=at.flip(1))
            at.send(
                right.at[m, slot(1), :], right.at[m, slot(3), :], gc_send.at[m, 3], gc_recv.at[m, 3], rep=at.flip(1)
            )

    def weight(m):
        near = 2 if parts == 4 else 1
        at.arrived(left.at[m, :, :, slot(near)], gc_recv.at[m, 0])
        at.arrived(right.at[m, slot(near), :], gc_recv.at[m, 1])
        if parts == 4:
            at.arrived(left.at[m, :, :, slot(3)], gc_recv.at[m, 2])
            at.arrived(right.at[m, slot(3), :], gc_recv.at[m, 3])
        rows = left.shape[1] * left.shape[2]
        out = dot(left[m].reshape(rows, parts * block), right[m])
        sums[m] = out.reshape(sums.shape[1:]).astype(BF16)

    def weight_across(m):
        for db in range(1, minor):
            at.send(
                sums.at[m, :, lax.rem(at.b + db, minor)], from_x.at[m, db - 1],
                gx_send.at[m, db - 1], gx_recv.at[m, db - 1], shard=at.at(0, db),
            )

    ahead = jnp.where(at.a < MAJOR // 2, 1, -1)
    middle = (at.a > 0) & (at.a < MAJOR - 1)

    def turn(n):
        return jnp.where(at.a < MAJOR // 2, MAJOR - 1 - n, n)

    class Chain:
        def __init__(self, own, land, ssem, rsem):
            self.own, self.land, self.ssem, self.rsem = own, land, ssem, rsem

        def go(self, n, when=None):
            t = turn(n)
            way = -ahead if n == 3 else ahead
            to = lax.max(lax.min(at.a + way, MAJOR - 1), 0) * minor + at.b
            dst = jnp.where(middle, MAJOR, t) if n == 1 else t
            at.send(self.own(t), self.land(dst), self.ssem.at[n], self.rsem.at[dst], shard=to, when=when)

        def summed(self, n):
            if n < 3:
                self.go(n, jnp.logical_not(middle))

        def joined(self, n):
            t = turn(n)

            @pl.when(middle)
            def _():
                at.arrived(self.land(t), self.rsem.at[t])
                self.own(t)[...] = self.own(t)[...] + self.land(t)[...]

            self.go(n, middle)

        def result(self):
            at.arrived(self.land(at.a), self.rsem.at[at.a])
            total = self.own(at.a)[...].astype(F32) + self.land(at.a)[...].astype(F32)
            self.own(at.a)[...] = total.astype(BF16)

            @pl.when(middle)
            def _():
                at.arrived(self.land(MAJOR), self.rsem.at[MAJOR])
                self.own(at.a)[...] = (total + self.land(MAJOR)[...].astype(F32)).astype(BF16)

            return self.own(at.a)[...]

    ffn_sums = {
        m: Chain(
            lambda t, m=m: sums.at[m, t, at.b], lambda n, m=m: from_z.at[m, n], gz_send.at[m], gz_recv.at[m]
        )
        for m in mats
    }

    def land_x(db, t):
        return weights.at[db - 1, pl.ds(pl.multiple_of(t * block, block), block), :]

    def land_z(n):
        return weights.at[0, pl.ds(pl.multiple_of((MAJOR + n) * block, block), block), :]

    row_sums = Chain(lambda t: xg.at[t * minor + at.b], land_z, nz_send, nz_recv)

    def rows_across(n):
        t = turn(n)
        for db in range(1, minor):
            to = t * minor + lax.rem(at.b + db, minor)
            at.send(
                xg.at[to], land_x(db, t), nx_send.at[db - 1, n], nx_recv.at[db - 1, t], shard=at.at(0, db)
            )

    def rows_summed(n):
        t = turn(n)
        own = row_sums.own(t)
        total = own[...].astype(F32)
        for db in range(1, minor):
            at.arrived(land_x(db, t), nx_recv.at[db - 1, t])
            total = total + land_x(db, t)[...].astype(F32)
        own[...] = total.astype(BF16)
        row_sums.summed(n)

    def weight_summed(m):
        for db in range(1, minor):
            at.arrived(from_x.at[m, db - 1], gx_recv.at[m, db - 1])
        for n in range(MAJOR):
            t = turn(n)
            total = sums[m, t, at.b].astype(F32)
            for db in range(1, minor):
                total = total + from_x[m, db - 1, t].astype(F32)
            sums[m, t, at.b] = total.astype(BF16)
            ffn_sums[m].summed(n)

    def weight_joined(m, n):
        ffn_sums[m].joined(n)

    def fin_slot(part, m=None):
        row, rows, col, wide = part_box(part, parts, slab, width)
        box = (pl.ds(pl.multiple_of(row, 16), rows), pl.ds(pl.multiple_of(col, 128), wide))
        return fin_ref.at[(slice(None) if m is None else m,) + box]

    def weight_done(m):
        fin_slot(mine, m)[...] = ffn_sums[m].result()

    forward, at.started = at.started, []
    keep_row = small_ref[10:11, :block]
    b_out, gain_two, b_up, b_down = (vec_ref[i : i + 1, :] for i in range(1, 5))
    halves = xt_ref.shape[2]

    def split_rows(value):
        return value.reshape(shards, halves, slab // halves, block)

    att_t = (att[...].astype(F32) * keep_row).astype(BF16)
    dy_ref[2] = cot_ref[...]
    mixed = x_ref[...].astype(F32) + dot(att_t.T, weights[0]) + b_out
    r = lax.rsqrt(jnp.mean(mixed * mixed, axis=-1, keepdims=True) + EPS)
    normed_two = (mixed * r * gain_two).astype(BF16)
    hidden = dot(normed_two, weights[1]) + b_up
    s = 1.0 / (1.0 + jnp.exp(-hidden))
    act = (hidden * s).astype(BF16)
    xt_ref[2] = split_rows(act.T)
    meet_far(2)
    meet_near(2)
    cot = cot_ref[...].astype(F32)
    g_hidden = dot(cot_ref[...], weights[2], NT) * (s + hidden * s * (1.0 - s))
    low = g_hidden.astype(BF16)
    g_normed = dot(low, weights[1], NT)
    weighted = gain_two * g_normed
    g_mixed = cot + r * weighted - mixed * (r * r * r) * jnp.mean(mixed * weighted, axis=-1, keepdims=True)
    g_low = g_mixed.astype(BF16)
    out_ref[...] = (mixed + dot(act, weights[2]) + b_down).astype(BF16)
    dctx_ref[...] = (dot(weights[0], g_low, NT).astype(BF16).astype(F32) * keep_row).astype(BF16)
    backward, at.started = at.started, forward
    at.settle()
    at.started = backward
    for i, (da, db) in enumerate(peers):
        dest = at.at(da, db)
        at.send(
            dctx_ref.at[pl.ds(pl.multiple_of(dest * slab, 16), slab), :],
            dctx.at[:, lane(me, block)], d_send.at[i], d_recv.at[me], shard=dest,
        )
    dctx[:, lane(me, block)] = dctx_ref[pl.ds(pl.multiple_of(me * slab, 16), slab), :]
    dy_ref[1] = low
    xt_ref[1] = split_rows(normed_two.T)
    meet_near(1)
    gmixed_ref[...] = g_mixed
    dy_ref[0] = g_low
    xt_ref[0] = split_rows(att_t)
    meet_near(0)
    row_ref[...] = jnp.zeros_like(row_ref)
    row_ref[1:2, :] = jnp.sum(g_mixed, axis=0, keepdims=True)
    row_ref[2:3, :] = jnp.sum(g_normed * mixed * r, axis=0, keepdims=True)
    row_ref[3:4, :] = jnp.sum(g_hidden, axis=0, keepdims=True)
    row_ref[4:5, :] = jnp.sum(cot, axis=0, keepdims=True)

    base = QUERY_BASE / math.sqrt(HEAD)
    factor = base * soft
    grads[...] = jnp.zeros_like(grads)
    for da, db in peers:
        origin = at.at(-da, -db)
        at.arrived(dctx.at[:, lane(origin, block)], d_recv.at[origin])

    def attend(i):
        reach = (i + 1) * qblock
        span = slice(i * qblock, reach)
        starts = start_ref[0:1, span]
        key_place = lax.broadcasted_iota(jnp.int32, (reach, qblock), 0).astype(F32)
        query_place = (i * qblock + lax.broadcasted_iota(jnp.int32, (1, qblock), 1)).astype(F32)
        allowed = (key_place >= starts) & (key_place <= query_place)
        for h in range(local):
            queries = qkv_ref[h * HEAD : (h + 1) * HEAD, span]
            keys = qkv_ref[slab + h * HEAD : slab + (h + 1) * HEAD, :reach]
            values = qkv_ref[2 * slab + h * HEAD : 2 * slab + (h + 1) * HEAD, :reach]
            gctx = dctx[h * HEAD : (h + 1) * HEAD, span]
            scores = dot(keys, queries, TN)
            probs = jnp.where(allowed, jnp.exp(scores - log_ref[h : h + 1, span]), 0.0)
            gprobs = dot(values, gctx, TN)
            delta = jnp.sum(probs * gprobs, axis=0, keepdims=True)
            gscores = (probs * (gprobs - delta)).astype(BF16)
            low = probs.astype(BF16)
            grads[h * HEAD : (h + 1) * HEAD, span] = dot(keys, gscores)
            kv = slice(slab + h * HEAD, slab + (h + 1) * HEAD)
            grads[kv, :reach] += dot(queries, gscores, NT)
            kv = slice(2 * slab + h * HEAD, 2 * slab + (h + 1) * HEAD)
            grads[kv, :reach] += dot(gctx, low, NT)

    steps = length // qblock
    for i in range(steps):
        attend(i)
        if i == 1:
            relay(2)
            meet_far(1)
        if i == 2:
            weight(2)
            weight_across(2)

    gscale = jnp.zeros((HEAD, 1), F32)
    for h in range(local):
        rows = slice(h * HEAD, (h + 1) * HEAD)
        scaled = grads[rows, :]
        gscale = gscale + jnp.sum(scaled * query_ref[rows, :], axis=1, keepdims=True)
        grads[rows, :] = scaled * factor
    gscale = gscale * (base / (1.0 + jnp.exp(-column)))
    bias_q = jnp.sum(grads[:slab, :], axis=1, keepdims=True)
    bias_v = jnp.sum(grads[2 * slab :, :], axis=1, keepdims=True)
    tall_rows = grads.shape[0]
    low_t = grads[...].astype(BF16)
    if tall_rows % 128:
        low_t = jnp.concatenate([low_t, jnp.zeros((-tall_rows % 128, length), BF16)], axis=0)
    proj[...] = low_t.T[:, :slab3]

    wcols = wcols_ref[...].reshape(width, slab3)

    def partial(origin, acc):
        tokens = lane(origin, block)
        out = dot(proj[tokens, :], wcols, NT)
        xg[origin] = out.astype(BF16)
        weighted = out * normed_ref[tokens, :].astype(F32)
        return acc + jnp.sum(weighted.reshape(block // 8, 8, width), axis=0)

    rp = width // (shards * parts)
    halves = parts // 2
    whole = dot(normed_ref[...], proj[...], TN)
    gw[...] = whole.reshape(shards, parts, rp, slab3).astype(BF16)
    for k in range(halves):
        at.send(gw.at[:, (1 - core) + 2 * k], gw_core.at[k], vc_send.at[k], vc_recv.at[k], rep=at.flip(1))

    def away(i, acc):
        return partial(at.at(lax.rem(i, MAJOR), 1 + i // MAJOR), acc)

    gain_rows = jnp.zeros((8, width), F32)
    gain_rows = lax.fori_loop(0, shards - MAJOR, away, gain_rows)
    rows_across(0)
    rows_across(1)
    relay(1)
    meet_far(0)
    gain_rows = lax.fori_loop(0, MAJOR, lambda i, acc: partial(at.at(i, 0), acc), gain_rows)
    weight(1)
    weight_across(1)
    rows_across(2)
    weight_summed(2)
    for k in range(halves):
        at.arrived(gw_core.at[k], vc_recv.at[k])
        gw_core[k] = gw[:, core + 2 * k] + gw_core[k]
    km = mine // 2 if parts == 4 else 0
    rows_summed(0)
    weight_joined(2, 0)
    weight_joined(2, 1)
    weight_joined(2, 3)
    relay(0)
    if parts == 4:
        at.send(gw_core.at[1 - km], gw_y, vy_send.at[0], vy_recv.at[0], rep=at.flip(2))
    weight(0)
    weight_across(0)
    rows_across(3)

    gain_row = jnp.sum(gain_rows, axis=0, keepdims=True) / vec_ref[0:1, :]
    rows = row_ref[...]
    place = lax.broadcasted_iota(jnp.int32, (8, width), 0)
    rows = jnp.where(place == 0, jnp.broadcast_to(gain_row, (8, width)), rows)
    turn_in = jnp.concatenate(
        [jnp.broadcast_to(gscale, (HEAD, 128)), jnp.zeros((128 - HEAD, 128), F32)], axis=0
    )
    scale_row = jnp.broadcast_to(turn_in.T[0:1, :], (8, 128))
    scale_tile = jnp.where(lax.broadcasted_iota(jnp.int32, (8, 128), 0) == 5, scale_row, 0.0)
    for j in range(shards):
        first = min(j * slab // 128 * 128, width - 256)
        windows[j, :, :256] = rows[:, first : first + 256]
        windows[j, :, 256:] = scale_tile
    for i, (da, db) in enumerate(peers):
        dest = at.at(da, db)
        at.send(windows.at[dest], small_land.at[me], s_send.at[i], s_recv.at[me], shard=dest)
    small_land[me] = windows[me]

    if parts == 4:
        at.arrived(gw_y, vy_recv.at[0])
        gw_sum[...] = gw_core[km] + gw_y[...]
    else:
        gw_sum[...] = gw_core[0]
    for i, (da, db) in enumerate(peers):
        dest = at.at(da, db)
        at.send(gw_sum.at[dest], gw_land.at[me], va_send.at[i], va_recv.at[me], shard=dest)
    gw_land[me] = gw_sum[me]
    rows_summed(1)
    row_sums.joined(0)
    weight_summed(1)
    rows_summed(2)
    row_sums.joined(1)
    weight_joined(1, 0)
    weight_joined(1, 1)
    weight_joined(1, 3)
    weight_summed(0)
    rows_summed(3)
    weight_joined(0, 0)
    weight_joined(0, 1)
    weight_joined(0, 3)
    row_sums.joined(3)

    for da, db in peers:
        origin = at.at(-da, -db)
        at.arrived(small_land.at[origin], s_recv.at[origin])
    small = jnp.sum(small_land[...], axis=0)
    lanes = lax.broadcasted_iota(jnp.int32, (slab, 128), 1)
    sides = jnp.concatenate(
        [jnp.where(lanes == 6, bias_q, jnp.where(lanes == 7, bias_v, 0.0)), jnp.zeros((256 - slab, 128), F32)],
        axis=0,
    )
    sides = jnp.concatenate([sides[:128].T[:8], sides[128:].T[:8]], axis=1)
    shift = me * slab - lax.min(me * slab // 128 * 128, width - 256)
    window = pltpu.roll(small[:, :256], lax.rem(256 - shift, 256), 1)
    tall = lax.broadcasted_iota(jnp.int32, (8, 256), 0)
    small_got[0, :, :256] = jnp.where(tall < 5, window, sides)
    small_got[0, :, 256:] = pltpu.roll(small[:, 256:], lax.rem(128 - me * unit, 128), 1)

    def small_round(n):
        at.send(
            small_got.at[2 * n], small_got.at[2 * n + 1], b_send.at[n], b_recv.at[n], rep=at.flip(every[n])
        )

    def small_add(n):
        at.arrived(small_got.at[2 * n + 1], b_recv.at[n])
        small_got[2 * n + 2] = small_got[2 * n] + small_got[2 * n + 1]

    small_round(0)
    for da, db in peers:
        origin = at.at(-da, -db)
        at.arrived(gw_land.at[origin], va_recv.at[origin])
    for n, mask in enumerate(extras):
        at.exchange(gw_land, gw_extra.at[n], ve_send.at[n], ve_recv.at[n], at.flip(mask))
        gw_land[...] = gw_land[...] + gw_extra[n]
    for j in range(shards):
        for t in range(3):
            first = t * width + j * slab
            gw_ref[mine, :, first : first + slab] = gw_land[j, :, t * slab : (t + 1) * slab]

    def hand_round(ref_slot, send_sem, recv_sem):
        have, rounds, k = [mine], [], 0
        for mask in ((2, 1) if parts == 4 else (1,)):
            sends = []
            for part in have:
                sends.append((part, mask, k))
                k += 1
            fresh = [flipped(part, mask) for part in have]
            rounds.append((sends, fresh))
            have = have + fresh

        def go(n):
            for part, mask, k in rounds[n][0]:
                at.send(ref_slot(part), ref_slot(part), send_sem.at[k], recv_sem.at[part], rep=at.flip(mask))

        def take(n):
            for part in rounds[n][1]:
                at.arrived(ref_slot(part), recv_sem.at[part])

        return go, take, len(rounds)

    gw_go, gw_take, count = hand_round(lambda part: gw_ref.at[part], vr_send, vr_recv)
    fin_go, fin_take, _ = hand_round(fin_slot, r_send, r_recv)
    gw_go(0)
    small_add(0)
    small_round(1)

    for m in mats:
        weight_done(m)
    for n, mask in enumerate(extras):
        at.exchange(fin_slot(mine), extra.at[n], e_send.at[n], e_recv.at[n], at.flip(mask))
        fin_slot(mine)[...] = fin_slot(mine)[...] + extra[n]
    fin_go(0)
    total = row_sums.result().astype(F32)
    x = x_ref[...].astype(F32)
    r = lax.rsqrt(jnp.mean(x * x, axis=-1, keepdims=True) + EPS)
    weighted = vec_ref[0:1, :] * total
    gin_ref[...] = gmixed_ref[...] + r * weighted - x * (r * r * r) * jnp.mean(x * weighted, axis=-1, keepdims=True)

    for n in range(count):
        gw_take(n)
        if n + 1 < count:
            gw_go(n + 1)
        fin_take(n)
        if n + 1 < count:
            fin_go(n + 1)
    for n in range(1, len(every)):
        small_add(n)
        if n + 1 < len(every):
            small_round(n + 1)
    small_out_ref[...] = small_got[2 * len(every)]

    at.settle()


def layer(shards, replicas, inputs, small, w_qkv, w_out, w_up, w_down, cotangent):
    block, width = inputs.shape
    slab = width // shards
    slab3 = 3 * slab
    length = shards * block
    wparts = 2 if slab % 32 == 0 else 1
    parts = parts_of(slab)
    halves = parts // 2
    rp = slab // parts
    rows_part = slab // 2 if parts == 4 else slab
    cols = width // 2
    minor = shards // MAJOR
    peers = shards - 1
    bits = (replicas - 1).bit_length()
    more = bits - (parts - 1).bit_length()
    shape = jax.ShapeDtypeStruct
    dma = pltpu.SemaphoreType.DMA
    vm = pltpu.VMEM
    return pl.pallas_call(
        functools.partial(layer_kernel, shards, replicas, wparts, parts, 2 * block),
        out_shape=(
            shape((block, width), BF16),
            shape((3, slab, width), BF16),
            shape((parts, rp, 3 * width), BF16),
            shape((block, width), F32),
            shape((8, 384), F32),
        ),
        in_specs=[VMEM] * 3 + [ANY] * 3 + [VMEM],
        out_specs=[VMEM] * 5,
        scratch_shapes=[
            vm((length, width), BF16),
            vm((slab3, length), BF16),
            vm((slab, length), F32),
            vm((8, length), F32),
            vm((8, width), F32),
            vm((8, length), F32),
            vm((shards, wparts, slab // wparts, slab3), BF16),
            vm((3, shards, halves, slab // halves, block), BF16),
            vm((3, block, width), BF16),
            vm((width, block), BF16),
            vm((8, width), F32),
            vm((block, width), F32),
            vm((shards, block, width), BF16),
            vm((shards, 8, 256), F32),
            vm((shards, wparts, slab // wparts, slab3), BF16),
            vm((slab3, width), BF16),
            vm((slab, length), BF16),
            vm((width, block), BF16),
            vm((3, width, width), BF16),
            vm((slab, length), BF16),
            vm((slab3, length), F32),
            vm((length, slab3), BF16),
            vm((3, shards, rows_part, parts * block), BF16),
            vm((3, parts * block, cols), BF16),
            vm((3, shards, rows_part, block) if parts == 4 else (1, 1, 16, block), BF16),
            vm((3, MAJOR, minor, rows_part, cols), BF16),
            vm((3, minor - 1, MAJOR, rows_part, cols), BF16),
            vm((3, MAJOR + 1, rows_part, cols), BF16),
            vm((max(more, 1), 3, rows_part, cols), BF16),
            vm((shards, parts, rp, slab3), BF16),
            vm((halves, shards, rp, slab3), BF16),
            vm((shards, rp, slab3) if parts == 4 else (1, 16, 128), BF16),
            vm((shards, rp, slab3), BF16),
            vm((shards, rp, slab3), BF16),
            vm((max(more, 1), shards, rp, slab3), BF16),
            vm((shards, 8, 384), F32),
            vm((shards, 8, 384), F32),
            vm((2 * bits + 1, 8, 384), F32),
            dma((2, MAJOR)), dma((MAJOR, minor - 1)), dma((shards,)),
            dma((peers,)), dma((shards,)),
            dma((peers,)), dma((shards, wparts)), dma((peers,)),
            dma((2, MAJOR)), dma((MAJOR, minor - 1)), dma((shards, parts)),
            dma((shards,)), dma((shards, 2)),
            dma((3,)), dma((shards,)), dma((shards,)),
            dma((peers,)), dma((shards,)),
            dma((3, 3)), dma((3, 3)),
            dma((3, 4)), dma((3, 4)),
            dma((3, minor - 1)), dma((3, minor - 1)),
            dma((3, MAJOR)), dma((3, MAJOR + 1)),
            dma((parts,)), dma((parts,)),
            dma((max(more, 1),)), dma((max(more, 1),)),
            dma((minor - 1, MAJOR)), dma((minor - 1, MAJOR)),
            dma((MAJOR,)), dma((MAJOR + 1,)),
            dma((halves,)), dma((halves,)),
            dma((1,)), dma((1,)),
            dma((peers,)), dma((shards,)),
            dma((parts,)), dma((parts,)),
            dma((max(more, 1),)), dma((max(more, 1),)),
            dma((peers,)), dma((shards,)),
            dma((bits,)), dma((bits,)),
        ],
        compiler_params=pltpu.CompilerParams(
            collective_id=0, has_side_effects=True, vmem_limit_bytes=62 << 20
        ),
        name="layer",
    )(inputs, small, w_qkv, w_out, w_up, w_down, cotangent)


def pack(positions, segment_ids, gain_one, b_query, b_value, query_scale, b_out, gain_two, b_up, b_down):
    block = positions.shape[-1]
    me = lax.axis_index("shard")
    starts = (me * block + lax.iota(jnp.int32, block) - positions.reshape(block)).astype(F32)
    keep = (segment_ids.reshape(block) != 0).astype(F32)
    table = {
        0: gain_one, 1: b_out, 2: gain_two, 3: b_up, 4: b_down, 5: query_scale, 6: starts,
        8: b_query, 9: b_value, 10: keep,
    }
    total = jnp.zeros((16, 256), F32)
    for row, vector in table.items():
        total = total + jnp.pad(vector.astype(F32)[None], ((row, 15 - row), (0, 256 - vector.shape[0])))
    return total


def on_device(
    inputs, segment_ids, positions, gain_one, w_qkv, b_query, b_value, query_scale, w_out, b_out,
    gain_two, w_up, b_up, w_down, b_down, cotangent,
):
    shards = lax.axis_size("shard")
    replicas = lax.axis_size("replica")
    block, width = inputs.shape[1:]
    slab = width // shards
    x = inputs.reshape(block, width)
    small = pack(positions, segment_ids, gain_one, b_query, b_value, query_scale, b_out, gain_two, b_up, b_down)
    output, fin, gw, input_grad, small = layer(
        shards, replicas, x, small, w_qkv, w_out, w_up, w_down, cotangent.reshape(block, width)
    )
    gw = gw.reshape(slab, 3 * width).astype(F32)
    fin = fin.astype(F32)
    unit = HEAD // shards
    return (
        output[None], input_grad[None], small[0, :slab], gw, small[6, :slab], small[7, :slab],
        small[5, 256 : 256 + unit], fin[0], small[1, :slab], small[2, :slab], fin[1], small[3, :slab],
        fin[2], small[4, :slab],
    )


def solution(mesh):
    rows = P("replica", "shard", None)
    ids = P("replica", "shard")
    vector = P("shard")
    matrix = P("shard", None)
    in_specs = (
        rows, ids, ids, vector, matrix, vector, vector, vector, matrix, vector, vector, matrix, vector,
        matrix, vector, rows,
    )
    out_specs = (
        rows, rows, vector, matrix, vector, vector, vector, matrix, vector, vector, matrix, vector, matrix,
        vector,
    )
    return jax.shard_map(on_device, mesh=mesh, in_specs=in_specs, out_specs=out_specs, check_vma=False)
```

```python
import functools
import math

import jax
import jax.numpy as jnp
from jax import lax
from jax.experimental import pallas as pl
from jax.experimental.pallas import tpu as pltpu
from jax.sharding import PartitionSpec as P

HEADS = 16
HEAD = 80
EPS = 1e-06
QUERY_BASE = 1.442695041
MASKED = -1000000000.0
MESH = pl.DeviceIdType.MESH
MAJOR = 4
VMEM = pl.BlockSpec(memory_space=pltpu.VMEM)
ANY = pl.BlockSpec(memory_space=pl.ANY)
F32 = jnp.float32
BF16 = jnp.bfloat16
NN = (((1,), (0,)), ((), ()))
NT = (((1,), (1,)), ((), ()))
TN = (((0,), (0,)), ((), ()))


def dot(lhs, rhs, dims=NN):
    return lax.dot_general(lhs, rhs, dims, preferred_element_type=F32)


class Place:
    def __init__(self, shards):
        self.shards = shards
        self.minor = shards // MAJOR
        self.me = lax.axis_index("shard")
        self.rep = lax.axis_index("replica")
        self.a = self.me // self.minor
        self.b = lax.rem(self.me, self.minor)
        self.started = []

    def at(self, da, db):
        a = lax.rem(self.a + da + MAJOR, MAJOR)
        b = lax.rem(self.b + db + self.minor, self.minor)
        return a * self.minor + b

    def peers(self):
        return [(da, db) for da in range(MAJOR) for db in range(self.minor) if da or db]

    def flip(self, mask):
        bit = lax.rem(self.rep // mask, 2)
        return self.rep + mask - 2 * mask * bit

    def greet(self, masks):
        barrier = pltpu.get_barrier_semaphore()
        for da, db in self.peers():
            pl.semaphore_signal(
                barrier, inc=1, device_id=(self.at(da, db), self.rep), device_id_type=MESH
            )
        for mask in masks:
            pl.semaphore_signal(
                barrier, inc=1, device_id=(self.me, self.flip(mask)), device_id_type=MESH
            )
        pl.semaphore_wait(barrier, len(self.peers()) + len(masks))

    def send(self, src, dst, ssem, rsem, shard=None, rep=None, when=None):
        copy = pltpu.make_async_remote_copy(
            src_ref=src,
            dst_ref=dst,
            send_sem=ssem,
            recv_sem=rsem,
            device_id=(self.me if shard is None else shard, self.rep if rep is None else rep),
            device_id_type=MESH,
        )
        if when is None:
            copy.start()
        else:
            @pl.when(when)
            def _():
                copy.start()
        self.started.append((when, copy))

    def arrived(self, dst, rsem):
        pltpu.make_async_remote_copy(
            src_ref=dst,
            dst_ref=dst,
            send_sem=rsem,
            recv_sem=rsem,
            device_id=(self.me, self.rep),
            device_id_type=MESH,
        ).wait_recv()

    def exchange(self, src, dst, ssem, rsem, rep):
        self.send(src, dst, ssem, rsem, rep=rep)
        self.arrived(dst, rsem)
        self.started.pop()[1].wait_send()

    def settle(self):
        for when, copy in self.started:
            if when is None:
                copy.wait_send()
            else:
                @pl.when(when)
                def _():
                    copy.wait_send()
        self.started = []


class Line:
    def __init__(self, at, slot, major_send, minor_send, recv):
        self.at, self.slot = at, slot
        self.major_send, self.minor_send, self.recv = major_send, minor_send, recv

    def onward(self, origin, up, down, d):
        at = self.at
        if up is not None:
            at.send(
                self.slot(origin), self.slot(origin), self.major_send.at[0, d], self.recv(origin),
                shard=lax.min(at.a + 1, MAJOR - 1) * at.minor + at.b, when=up,
            )
        if down is not None:
            at.send(
                self.slot(origin), self.slot(origin), self.major_send.at[1, d], self.recv(origin),
                shard=lax.max(at.a - 1, 0) * at.minor + at.b, when=down,
            )

    def across(self, origin, when=None):
        at = self.at
        for db in range(1, at.minor):
            at.send(
                self.slot(origin), self.slot(origin), self.minor_send.at[origin // at.minor, db - 1],
                self.recv(origin), shard=at.at(0, db), when=when,
            )

    def along_own(self):
        at = self.at
        self.onward(at.me, at.a + 1 < MAJOR, at.a > 0, 0)

    def sides(self, d):
        at = self.at
        for side in (-1, 1):
            ok = (at.a - d >= 0) if side < 0 else (at.a + d < MAJOR)
            origin = lax.max(at.a - d, 0) if side < 0 else lax.min(at.a + d, MAJOR - 1)
            yield side, ok, origin * at.minor + at.b

    def take(self, d, then=None):
        for side, ok, origin in self.sides(d):
            @pl.when(ok)
            def _():
                self.at.arrived(self.slot(origin), self.recv(origin))

            if then is not None:
                then(origin, ok)

    def along(self, d):
        at = self.at
        if d + 1 < MAJOR:
            for side, ok, origin in self.sides(d):
                if side < 0:
                    self.onward(origin, ok & (at.a + 1 < MAJOR), None, d)
                else:
                    self.onward(origin, None, ok & (at.a > 0), d)

    def aside(self, d):
        for side, ok, origin in self.sides(d):
            self.across(origin, when=ok)

    def step(self, d, then=None):
        self.take(d, then)
        self.along(d)
        self.aside(d)


def parts_of(rows):
    return 4 if rows % 32 == 0 else 2


def part_box(part, parts, rows, cols):
    if parts == 4:
        i, j, rows = lax.rem(part, 2), part // 2, rows // 2
    else:
        i, j = 0, part
    return i * rows, rows, j * (cols // 2), cols // 2


def flipped(part, mask):
    bit = lax.rem(part // mask, 2)
    return part + mask - 2 * mask * bit


def layer_kernel(
    shards, replicas, wparts, parts, qblock,
    x_ref, segment_ref, position_ref, gain_one_ref, b_query_ref, b_value_ref, scale_ref,
    b_out_ref, gain_two_ref, b_up_ref, b_down_ref, w_hbm, wout_ref, wup_ref, wdown_ref, cot_hbm,
    out_hbm, fin_hbm, gw_hbm, gin_hbm, small_out_ref,
    out_ref, fin_ref, gw_ref, gin_ref, w_ref, cot_ref, small_ref,
    normed_ref, qkv_ref, query_ref, log_ref, vec_ref, start_ref, wcols_ref,
    xt_ref, dy_ref, dctx_ref, row_ref, gmixed_ref,
    xg, packets, pieces, turned, context, att, weights,
    dctx, grads, proj, left, right, stash, sums, from_x, from_z, extra,
    gw, gw_core, gw_y, gw_sum, gw_land, gw_extra,
    windows, small_land, small_got,
    xm_send, xn_send, x_recv, p_send, p_recv, w_send, w_recv, wc_send, wy_send,
    fm_send, fn_send, f_recv, fy_send, fc_send, local_sem, a_send, a_recv, done_sem,
    d_send, d_recv, gy_send, gy_recv, gc_send, gc_recv, gx_send, gx_recv, gz_send, gz_recv,
    r_send, r_recv, e_send, e_recv, nx_send, nx_recv, nz_send, nz_recv,
    vc_send, vc_recv, vy_send, vy_recv, va_send, va_recv, vr_send, vr_recv, ve_send, ve_recv,
    s_send, s_recv, b_send, b_recv,
):
    at = Place(shards)
    me, minor = at.me, at.minor
    block, width = x_ref.shape
    length = shards * block
    slab = width // shards
    slab3 = 3 * slab
    local = slab // HEAD
    peers = at.peers()
    masks = (2, 1) if parts == 4 else (1,)
    every = []
    bit = 1
    while bit < replicas:
        every.append(bit)
        bit *= 2
    extras = [m for m in every if m >= parts]
    mine = lax.rem(at.rep, parts)
    wpart = lax.rem(at.rep, wparts)

    loads = []
    for m, ref in enumerate((wout_ref, wup_ref, wdown_ref)):
        copy = pltpu.make_async_copy(
            ref, weights.at[m, pl.ds(pl.multiple_of(me * slab, 16), slab), :], local_sem.at[m]
        )
        copy.start()
        loads.append(copy)
    w_load = pltpu.make_async_copy(w_hbm, w_ref, local_sem.at[3])
    w_load.start()
    cot_load = pltpu.make_async_copy(cot_hbm, cot_ref, local_sem.at[4])
    cot_load.start()
    xg[me] = x_ref[...]
    small_ref[...] = jnp.zeros_like(small_ref)
    table = {
        0: gain_one_ref, 1: b_out_ref, 2: gain_two_ref, 3: b_up_ref, 4: b_down_ref, 5: scale_ref,
        8: b_query_ref, 9: b_value_ref,
    }
    for row, ref in table.items():
        size = ref.shape[0]
        small_ref[row : row + 1, :size] = ref[...].astype(F32).reshape(1, size)
    place = me * block + lax.broadcasted_iota(jnp.int32, (1, block), 1)
    small_ref[6:7, :block] = (place - position_ref[...]).astype(F32)
    small_ref[10:11, :block] = (segment_ref[...] != 0).astype(F32)
    packets[me] = small_ref[:8]
    at.greet(tuple(every))

    def wslot(origin, part):
        row, rows, col, cols = part_box(part, parts, slab, width)
        return weights.at[
            :,
            pl.ds(pl.multiple_of(origin * slab + row, 16), rows),
            pl.ds(pl.multiple_of(col, 128), cols),
        ]

    rows_line = Line(at, lambda o: xg.at[o], xm_send, xn_send, lambda o: x_recv.at[o])
    ffn_line = Line(
        at, lambda o: wslot(o, mine), fm_send, fn_send, lambda o: f_recv.at[o, mine]
    )

    def to_replicas(origin, when=None):
        slot = wslot(origin, mine)
        for mask in masks:
            sem = fy_send.at[origin] if mask == 2 else fc_send.at[origin, 0]
            at.send(slot, slot, sem, f_recv.at[origin, mine], rep=at.flip(mask), when=when)

    for i, (da, db) in enumerate(peers):
        at.send(packets.at[me], packets.at[me], p_send.at[i], p_recv.at[me], shard=at.at(da, db))
    rows_line.along_own()
    for copy in loads:
        copy.wait()
    ffn_line.across(me)
    rows_line.across(me)
    w_load.wait()
    cut = slab // wparts
    for j in range(shards):
        for t in range(3):
            first = t * width + j * slab
            pieces[j, :, :, t * slab : (t + 1) * slab] = w_ref[:, first : first + slab].reshape(
                wparts, cut, slab
            )
    parity = lax.rem(at.a + mine // 2, 2)
    chosen = parity == 0 if parts == 4 else None
    for i, (da, db) in enumerate(peers):
        dest = at.at(da, db)
        at.send(
            pieces.at[dest, wpart], wcols_ref.at[me, wpart], w_send.at[i], w_recv.at[me, wpart], shard=dest,
            when=chosen,
        )
    wcols_ref[me] = pieces[me]
    ffn_line.along_own()

    def ffn_minor(distance):
        for db in range(1, minor):
            sides = ((-1, 1) if distance else (0,))
            for side in sides:
                a = at.a + side * distance
                ok = None
                if distance:
                    ok = (a >= 0) & (a < MAJOR)
                origin = lax.max(lax.min(a, MAJOR - 1), 0) * minor + lax.rem(at.b + db, minor)
                slot = wslot(origin, mine)
                if ok is None:
                    at.arrived(slot, f_recv.at[origin, mine])
                else:
                    @pl.when(ok)
                    def _():
                        at.arrived(slot, f_recv.at[origin, mine])
                to_replicas(origin, ok)

    def columns(phase):
        for q in range(2):
            for db in range(minor):
                da = lax.rem(parity + phase, 2) + 2 * q
                origin = at.at(-da, -db)
                slot = wcols_ref.at[origin, wpart]
                real = origin != me

                @pl.when(real)
                def _():
                    at.arrived(slot, w_recv.at[origin, wpart])

                if parts == 4 and phase == 0:
                    at.send(
                        slot, slot, wy_send.at[origin], w_recv.at[origin, wpart], rep=at.flip(2), when=real
                    )
                if wparts == 2:
                    at.send(
                        slot, slot, wc_send.at[origin], w_recv.at[origin, wpart], rep=at.flip(1), when=real
                    )

    ffn_minor(0)
    rows_line.step(1)
    ffn_line.step(1, to_replicas)
    rows_line.step(2)
    columns(0)

    for da, db in peers:
        origin = at.at(-da, -db)
        at.arrived(packets.at[origin], p_recv.at[origin])
    vectors = jnp.zeros((8, width), F32)
    scales = jnp.zeros((1, 128), F32)
    lanes = lax.broadcasted_iota(jnp.int32, (8, width), 1)
    unit = HEAD // shards
    for j in range(shards):
        piece = packets[j]
        wide = jnp.concatenate([piece, jnp.zeros((8, width - piece.shape[1]), F32)], axis=1)
        wide = jnp.where(lanes < slab, wide, 0.0)
        vectors = vectors + (pltpu.roll(wide, j * slab, 1) if j else wide)
        scale = jnp.where(lanes[0:1, :128] < unit, piece[5:6, :128], 0.0)
        scales = scales + (pltpu.roll(scale, j * unit, 1) if j else scale)
        start_ref[:, j * block : (j + 1) * block] = jnp.broadcast_to(piece[6:7, :block], (8, block))
    rows = lax.broadcasted_iota(jnp.int32, (8, width), 0)
    vec_ref[...] = jnp.where(rows < 5, vectors, 0.0)
    vec_ref[5:6, :128] = scales
    gain = vec_ref[0:1, :]
    column = jnp.broadcast_to(scales, (128, 128)).T[:HEAD, 0:1]
    soft = jnp.maximum(column, 0.0) + jnp.log(1.0 + jnp.exp(-jnp.abs(column)))
    factor = jnp.concatenate([QUERY_BASE / math.sqrt(HEAD) * soft] * local, axis=0)
    own = small_ref[8:16, :]
    tall = jnp.concatenate([own, jnp.zeros((120, 256), F32)], axis=0)
    tall = jnp.concatenate([tall[:, :128].T, tall[:, 128:].T], axis=0)
    bias_query = tall[:slab, 0:1]
    bias_value = tall[:slab, 1:2]

    ffn_line.step(2, to_replicas)
    ffn_minor(1)
    rows_line.step(3)
    columns(1)
    if wparts == 2:
        for da, db in peers:
            origin = at.at(-da, -db)
            last = wparts - 1 - wpart
            at.arrived(wcols_ref.at[origin, last], w_recv.at[origin, last])
    turned[...] = wcols_ref[...].reshape(width, slab3).T

    def project(origin):
        rows_in = xg[origin].astype(F32)
        scale = lax.rsqrt(jnp.mean(rows_in * rows_in, axis=-1, keepdims=True) + EPS)
        normed = (rows_in * scale * gain).astype(BF16)
        tokens = pl.ds(pl.multiple_of(origin * block, block), block)
        normed_ref[tokens, :] = normed
        out = dot(turned[...], normed, NT)
        query = out[:slab] + bias_query
        query_ref[:, tokens] = query
        qkv_ref[:slab, tokens] = (query * factor).astype(BF16)
        qkv_ref[slab : 2 * slab, tokens] = out[slab : 2 * slab].astype(BF16)
        qkv_ref[2 * slab :, tokens] = (out[2 * slab :] + bias_value).astype(BF16)

    ffn_line.step(3, to_replicas)

    def project_major(i, carry):
        project(at.at(i, 0))
        return carry

    def project_minor(i, carry):
        origin = at.at(lax.rem(i, MAJOR), 1 + i // MAJOR)
        at.arrived(xg.at[origin], x_recv.at[origin])
        project(origin)
        return carry

    lax.fori_loop(0, MAJOR, project_major, 0)
    ffn_minor(2)
    lax.fori_loop(0, shards - MAJOR, project_minor, 0)
    ffn_minor(3)

    log_ref[...] = jnp.zeros_like(log_ref)
    for i in range(length // qblock):
        reach = (i + 1) * qblock
        span = slice(i * qblock, reach)
        starts = start_ref[0:1, span]
        key_place = lax.broadcasted_iota(jnp.int32, (reach, qblock), 0).astype(F32)
        query_place = (i * qblock + lax.broadcasted_iota(jnp.int32, (1, qblock), 1)).astype(F32)
        allowed = (key_place >= starts) & (key_place <= query_place)
        for h in range(local):
            head = slice(h * HEAD, (h + 1) * HEAD)
            queries = qkv_ref[h * HEAD : (h + 1) * HEAD, span]
            keys = qkv_ref[slab + h * HEAD : slab + (h + 1) * HEAD, :reach]
            values = qkv_ref[2 * slab + h * HEAD : 2 * slab + (h + 1) * HEAD, :reach]
            scores = jnp.where(allowed, dot(keys, queries, TN), MASKED)
            top = jnp.max(scores, axis=0, keepdims=True)
            powers = jnp.exp(scores - top)
            total = jnp.sum(powers, axis=0, keepdims=True)
            probs = (powers * (1.0 / total)).astype(BF16)
            log_ref[h : h + 1, span] = top + jnp.log(total)
            context[head, span] = dot(values, probs).astype(BF16)
        heads = pl.ds(pl.multiple_of(me * slab, 16), slab)
        for j in range(i * qblock // block, reach // block):
            piece = slice(j * block, (j + 1) * block)
            at.send(context.at[:, piece], att.at[heads, :], a_send.at[j], a_recv.at[me], shard=j, when=me != j)

            @pl.when(me == j)
            def _():
                att[heads, :] = context[:, piece]

    order = [(0, db) for db in range(1, minor)]
    order += [(da, db) for da in range(1, MAJOR) for db in range(minor)]
    if parts == 4:
        for da, db in order:
            origin = at.at(da, db)
            part = flipped(mine, 2)
            slot = wslot(origin, part)
            at.arrived(slot, f_recv.at[origin, part])
            at.send(slot, slot, fc_send.at[origin, 1], f_recv.at[origin, part], rep=at.flip(1))
    for da, db in peers:
        origin = at.at(-da, -db)
        at.arrived(att.at[pl.ds(pl.multiple_of(origin * slab, 16), slab), :], a_recv.at[origin])
    others = [flipped(mine, 1)] + ([flipped(flipped(mine, 1), 2)] if parts == 4 else [])
    for da, db in order:
        origin = at.at(da, db)
        for part in others:
            at.arrived(wslot(origin, part), f_recv.at[origin, part])

    slab3 = 3 * slab
    cols = width // 2
    core = lax.rem(at.rep, 2)
    i_part = lax.rem(mine, 2) if parts == 4 else 0
    j_part = mine // 2 if parts == 4 else mine
    mats = (2, 1, 0)

    def lane(n, size):
        return pl.ds(pl.multiple_of(n * size, 128), size)

    def slot(n):
        return slice(n * block, (n + 1) * block)

    def meet_near(m):
        near = parts // 2
        at.send(
            xt_ref.at[m, :, 1 - i_part if parts == 4 else 0], left.at[m, :, :, slot(near)],
            gc_send.at[m, 0], gc_recv.at[m, 0], rep=at.flip(1),
        )
        at.send(
            dy_ref.at[m, :, lane(j_part if parts == 4 else 1 - j_part, cols)], right.at[m, slot(near), :],
            gc_send.at[m, 1], gc_recv.at[m, 1], rep=at.flip(1),
        )
        left[m, :, :, slot(0)] = xt_ref[m, :, i_part]
        right[m, slot(0), :] = dy_ref[m, :, lane(j_part, cols)]

    def meet_far(m):
        if parts == 4:
            far = at.flip(2)
            at.send(
                xt_ref.at[m, :, i_part], left.at[m, :, :, slot(1)], gy_send.at[m, 0], gy_recv.at[m, 0], rep=far
            )
            at.send(
                dy_ref.at[m, :, lane(1 - j_part, cols)], right.at[m, slot(1), :],
                gy_send.at[m, 1], gy_recv.at[m, 1], rep=far,
            )
            at.send(xt_ref.at[m, :, 1 - i_part], stash.at[m], gy_send.at[m, 2], gy_recv.at[m, 2], rep=far)

    def relay(m):
        if parts == 4:
            at.arrived(left.at[m, :, :, slot(1)], gy_recv.at[m, 0])
            at.arrived(right.at[m, slot(1), :], gy_recv.at[m, 1])
            at.arrived(stash.at[m], gy_recv.at[m, 2])
            at.send(stash.at[m], left.at[m, :, :, slot(3)], gc_send.at[m, 2], gc_recv.at[m, 2], rep=at.flip(1))
            at.send(
                right.at[m, slot(1), :], right.at[m, slot(3), :], gc_send.at[m, 3], gc_recv.at[m, 3], rep=at.flip(1)
            )

    def weight(m):
        near = 2 if parts == 4 else 1
        at.arrived(left.at[m, :, :, slot(near)], gc_recv.at[m, 0])
        at.arrived(right.at[m, slot(near), :], gc_recv.at[m, 1])
        if parts == 4:
            at.arrived(left.at[m, :, :, slot(3)], gc_recv.at[m, 2])
            at.arrived(right.at[m, slot(3), :], gc_recv.at[m, 3])
        rows = left.shape[1] * left.shape[2]
        out = dot(left[m].reshape(rows, parts * block), right[m])
        sums[m] = out.reshape(sums.shape[1:]).astype(BF16)

    def weight_across(m):
        for db in range(1, minor):
            at.send(
                sums.at[m, :, lax.rem(at.b + db, minor)], from_x.at[m, db - 1],
                gx_send.at[m, db - 1], gx_recv.at[m, db - 1], shard=at.at(0, db),
            )

    ahead = jnp.where(at.a < MAJOR // 2, 1, -1)
    middle = (at.a > 0) & (at.a < MAJOR - 1)

    def turn(n):
        return jnp.where(at.a < MAJOR // 2, MAJOR - 1 - n, n)

    class Chain:
        def __init__(self, own, land, ssem, rsem):
            self.own, self.land, self.ssem, self.rsem = own, land, ssem, rsem

        def go(self, n, when=None):
            t = turn(n)
            way = -ahead if n == 3 else ahead
            to = lax.max(lax.min(at.a + way, MAJOR - 1), 0) * minor + at.b
            dst = jnp.where(middle, MAJOR, t) if n == 1 else t
            at.send(self.own(t), self.land(dst), self.ssem.at[n], self.rsem.at[dst], shard=to, when=when)

        def summed(self, n):
            if n < 3:
                self.go(n, jnp.logical_not(middle))

        def joined(self, n):
            t = turn(n)

            @pl.when(middle)
            def _():
                at.arrived(self.land(t), self.rsem.at[t])
                self.own(t)[...] = self.own(t)[...] + self.land(t)[...]

            self.go(n, middle)

        def result(self):
            at.arrived(self.land(at.a), self.rsem.at[at.a])
            total = self.own(at.a)[...].astype(F32) + self.land(at.a)[...].astype(F32)
            self.own(at.a)[...] = total.astype(BF16)

            @pl.when(middle)
            def _():
                at.arrived(self.land(MAJOR), self.rsem.at[MAJOR])
                self.own(at.a)[...] = (total + self.land(MAJOR)[...].astype(F32)).astype(BF16)

            return self.own(at.a)[...]

    ffn_sums = {
        m: Chain(
            lambda t, m=m: sums.at[m, t, at.b], lambda n, m=m: from_z.at[m, n], gz_send.at[m], gz_recv.at[m]
        )
        for m in mats
    }

    def land_x(db, t):
        first = (db - 1) // 2 * MAJOR + t
        return weights.at[(db - 1) % 2, pl.ds(pl.multiple_of(first * block, block), block), :]

    def land_z(n):
        return weights.at[1, pl.ds(pl.multiple_of((MAJOR + n) * block, block), block), :]

    row_sums = Chain(lambda t: xg.at[t * minor + at.b], land_z, nz_send, nz_recv)

    def rows_across(n):
        t = turn(n)
        for db in range(1, minor):
            to = t * minor + lax.rem(at.b + db, minor)
            at.send(
                xg.at[to], land_x(db, t), nx_send.at[db - 1, n], nx_recv.at[db - 1, t], shard=at.at(0, db)
            )

    def rows_summed(n):
        t = turn(n)
        own = row_sums.own(t)
        total = own[...].astype(F32)
        for db in range(1, minor):
            at.arrived(land_x(db, t), nx_recv.at[db - 1, t])
            total = total + land_x(db, t)[...].astype(F32)
        own[...] = total.astype(BF16)
        row_sums.summed(n)

    def weight_summed(m):
        for db in range(1, minor):
            at.arrived(from_x.at[m, db - 1], gx_recv.at[m, db - 1])
        for n in range(MAJOR):
            t = turn(n)
            total = sums[m, t, at.b].astype(F32)
            for db in range(1, minor):
                total = total + from_x[m, db - 1, t].astype(F32)
            sums[m, t, at.b] = total.astype(BF16)
            ffn_sums[m].summed(n)

    def weight_joined(m, n):
        ffn_sums[m].joined(n)

    def fin_slot(part, m=None):
        row, rows, col, wide = part_box(part, parts, slab, width)
        box = (pl.ds(pl.multiple_of(row, 16), rows), pl.ds(pl.multiple_of(col, 128), wide))
        return fin_ref.at[(slice(None) if m is None else m,) + box]

    def weight_done(m):
        fin_slot(mine, m)[...] = ffn_sums[m].result()

    forward, at.started = at.started, []
    keep_row = small_ref[10:11, :block]
    b_out, gain_two, b_up, b_down = (vec_ref[i : i + 1, :] for i in range(1, 5))
    halves = xt_ref.shape[2]

    def split_rows(value):
        return value.reshape(shards, halves, slab // halves, block)

    att_t = (att[...].astype(F32) * keep_row).astype(BF16)
    cot_load.wait()
    dy_ref[2] = cot_ref[...]
    mixed = x_ref[...].astype(F32) + dot(att_t.T, weights[0]) + b_out
    r = lax.rsqrt(jnp.mean(mixed * mixed, axis=-1, keepdims=True) + EPS)
    normed_two = (mixed * r * gain_two).astype(BF16)
    hidden = dot(normed_two, weights[1]) + b_up
    s = 1.0 / (1.0 + jnp.exp(-hidden))
    act = (hidden * s).astype(BF16)
    xt_ref[2] = split_rows(act.T)
    meet_far(2)
    meet_near(2)
    cot = cot_ref[...].astype(F32)
    g_hidden = dot(cot_ref[...], weights[2], NT) * (s + hidden * s * (1.0 - s))
    low = g_hidden.astype(BF16)
    g_normed = dot(low, weights[1], NT)
    weighted = gain_two * g_normed
    g_mixed = cot + r * weighted - mixed * (r * r * r) * jnp.mean(mixed * weighted, axis=-1, keepdims=True)
    g_low = g_mixed.astype(BF16)
    dctx_ref[...] = (dot(weights[0], g_low, NT).astype(BF16).astype(F32) * keep_row).astype(BF16)
    backward, at.started = at.started, forward
    at.settle()
    at.started = backward
    for i, (da, db) in enumerate(peers):
        dest = at.at(da, db)
        at.send(
            dctx_ref.at[pl.ds(pl.multiple_of(dest * slab, 16), slab), :],
            dctx.at[:, lane(me, block)], d_send.at[i], d_recv.at[me], shard=dest,
        )
    dctx[:, lane(me, block)] = dctx_ref[pl.ds(pl.multiple_of(me * slab, 16), slab), :]
    dy_ref[1] = low
    xt_ref[1] = split_rows(normed_two.T)
    meet_far(1)
    meet_near(1)
    gmixed_ref[...] = g_mixed
    dy_ref[0] = g_low
    xt_ref[0] = split_rows(att_t)
    meet_far(0)
    meet_near(0)
    out_ref[...] = (mixed + dot(act, weights[2]) + b_down).astype(BF16)
    written = [pltpu.make_async_copy(out_ref, out_hbm, done_sem.at[0])]
    written[0].start()
    row_ref[...] = jnp.zeros_like(row_ref)
    row_ref[1:2, :] = jnp.sum(g_mixed, axis=0, keepdims=True)
    row_ref[2:3, :] = jnp.sum(g_normed * mixed * r, axis=0, keepdims=True)
    row_ref[3:4, :] = jnp.sum(g_hidden, axis=0, keepdims=True)
    row_ref[4:5, :] = jnp.sum(cot, axis=0, keepdims=True)

    base = QUERY_BASE / math.sqrt(HEAD)
    factor = base * soft
    grads[...] = jnp.zeros_like(grads)
    for da, db in peers:
        origin = at.at(-da, -db)
        at.arrived(dctx.at[:, lane(origin, block)], d_recv.at[origin])

    def attend(i):
        reach = (i + 1) * qblock
        span = slice(i * qblock, reach)
        starts = start_ref[0:1, span]
        key_place = lax.broadcasted_iota(jnp.int32, (reach, qblock), 0).astype(F32)
        query_place = (i * qblock + lax.broadcasted_iota(jnp.int32, (1, qblock), 1)).astype(F32)
        allowed = (key_place >= starts) & (key_place <= query_place)
        for h in range(local):
            queries = qkv_ref[h * HEAD : (h + 1) * HEAD, span]
            keys = qkv_ref[slab + h * HEAD : slab + (h + 1) * HEAD, :reach]
            values = qkv_ref[2 * slab + h * HEAD : 2 * slab + (h + 1) * HEAD, :reach]
            gctx = dctx[h * HEAD : (h + 1) * HEAD, span]
            scores = dot(keys, queries, TN)
            probs = jnp.where(allowed, jnp.exp(scores - log_ref[h : h + 1, span]), 0.0)
            gprobs = dot(values, gctx, TN)
            delta = jnp.sum(probs * gprobs, axis=0, keepdims=True)
            gscores = (probs * (gprobs - delta)).astype(BF16)
            low = probs.astype(BF16)
            grads[h * HEAD : (h + 1) * HEAD, span] = dot(keys, gscores)
            kv = slice(slab + h * HEAD, slab + (h + 1) * HEAD)
            grads[kv, :reach] += dot(queries, gscores, NT)
            kv = slice(2 * slab + h * HEAD, 2 * slab + (h + 1) * HEAD)
            grads[kv, :reach] += dot(gctx, low, NT)

    steps = length // qblock
    for i in range(steps):
        attend(i)
        if i == 1:
            relay(2)
        if i == 2:
            weight(2)
            weight_across(2)

    gscale = jnp.zeros((HEAD, 1), F32)
    for h in range(local):
        rows = slice(h * HEAD, (h + 1) * HEAD)
        scaled = grads[rows, :]
        gscale = gscale + jnp.sum(scaled * query_ref[rows, :], axis=1, keepdims=True)
        grads[rows, :] = scaled * factor
    gscale = gscale * (base / (1.0 + jnp.exp(-column)))
    bias_q = jnp.sum(grads[:slab, :], axis=1, keepdims=True)
    bias_v = jnp.sum(grads[2 * slab :, :], axis=1, keepdims=True)
    tall_rows = grads.shape[0]
    low_t = grads[...].astype(BF16)
    if tall_rows % 128:
        low_t = jnp.concatenate([low_t, jnp.zeros((-tall_rows % 128, length), BF16)], axis=0)
    proj[...] = low_t.T[:, :slab3]

    wcols = wcols_ref[...].reshape(width, slab3)

    def partial(origin, acc):
        tokens = lane(origin, block)
        out = dot(proj[tokens, :], wcols, NT)
        xg[origin] = out.astype(BF16)
        weighted = out * normed_ref[tokens, :].astype(F32)
        return acc + jnp.sum(weighted.reshape(block // 8, 8, width), axis=0)

    def away(i, acc):
        return partial(turn(1 + lax.rem(i, 3)) * minor + lax.rem(at.b + 1 + i // 3, minor), acc)

    gain_rows = jnp.zeros((8, width), F32)
    for db in range(1, minor):
        gain_rows = partial(turn(0) * minor + lax.rem(at.b + db, minor), gain_rows)
    rows_across(0)
    relay(1)
    gain_rows = lax.fori_loop(0, 3 * (minor - 1), away, gain_rows)
    weight(1)
    weight_across(1)

    rp = width // (shards * parts)
    halves = parts // 2
    whole = dot(normed_ref[...], proj[...], TN)
    gw[...] = whole.reshape(shards, parts, rp, slab3).astype(BF16)
    for k in range(halves):
        at.send(gw.at[:, (1 - core) + 2 * k], gw_core.at[k], vc_send.at[k], vc_recv.at[k], rep=at.flip(1))

    gain_rows = lax.fori_loop(0, MAJOR, lambda i, acc: partial(at.at(i, 0), acc), gain_rows)

    gain_row = jnp.sum(gain_rows, axis=0, keepdims=True) / vec_ref[0:1, :]
    rows = row_ref[...]
    place = lax.broadcasted_iota(jnp.int32, (8, width), 0)
    rows = jnp.where(place == 0, jnp.broadcast_to(gain_row, (8, width)), rows)
    turn_in = jnp.concatenate(
        [jnp.broadcast_to(gscale, (HEAD, 128)), jnp.zeros((128 - HEAD, 128), F32)], axis=0
    )
    scale_row = jnp.broadcast_to(turn_in.T[0:1, :], (8, 128))
    scale_tile = jnp.where(lax.broadcasted_iota(jnp.int32, (8, 128), 0) == 5, scale_row, 0.0)
    for j in range(shards):
        first = min(j * slab // 128 * 128, width - 256)
        windows[j, :, :256] = rows[:, first : first + 256]
        windows[j, :, 256:] = scale_tile
    for i, (da, db) in enumerate(peers):
        dest = at.at(da, db)
        at.send(windows.at[dest], small_land.at[me], s_send.at[i], s_recv.at[me], shard=dest)
    small_land[me] = windows[me]

    weight_summed(2)
    relay(0)
    weight(0)
    weight_across(0)
    rows_across(1)
    rows_across(2)
    for k in range(halves):
        at.arrived(gw_core.at[k], vc_recv.at[k])
        gw_core[k] = gw[:, core + 2 * k] + gw_core[k]
    km = mine // 2 if parts == 4 else 0
    if parts == 4:
        at.send(gw_core.at[1 - km], gw_y, vy_send.at[0], vy_recv.at[0], rep=at.flip(2))
    rows_summed(0)
    weight_joined(2, 0)
    weight_joined(2, 1)
    weight_joined(2, 3)
    weight_summed(1)
    row_sums.joined(0)
    if parts == 4:
        at.arrived(gw_y, vy_recv.at[0])
        gw_sum[...] = gw_core[km] + gw_y[...]
    else:
        gw_sum[...] = gw_core[0]
    for i, (da, db) in enumerate(peers):
        dest = at.at(da, db)
        at.send(gw_sum.at[dest], gw_land.at[me], va_send.at[i], va_recv.at[me], shard=dest)
    gw_land[me] = gw_sum[me]
    rows_across(3)
    weight_joined(1, 0)
    weight_joined(1, 1)
    weight_joined(1, 3)
    weight_summed(0)
    weight_joined(0, 0)
    weight_joined(0, 1)
    weight_joined(0, 3)
    rows_summed(1)
    row_sums.joined(1)

    def hand_round(ref_slot, send_sem, recv_sem):
        have, rounds, k = [mine], [], 0
        for mask in ((2, 1) if parts == 4 else (1,)):
            sends = []
            for part in have:
                sends.append((part, mask, k))
                k += 1
            fresh = [flipped(part, mask) for part in have]
            rounds.append((sends, fresh))
            have = have + fresh

        def go(n):
            for part, mask, k in rounds[n][0]:
                at.send(ref_slot(part), ref_slot(part), send_sem.at[k], recv_sem.at[part], rep=at.flip(mask))

        def take(n):
            for part in rounds[n][1]:
                at.arrived(ref_slot(part), recv_sem.at[part])

        return go, take, len(rounds)

    gw_go, gw_take, count = hand_round(lambda part: gw_ref.at[part], vr_send, vr_recv)
    fin_go, fin_take, _ = hand_round(fin_slot, r_send, r_recv)
    for m in mats:
        weight_done(m)
    for n, mask in enumerate(extras):
        at.exchange(fin_slot(mine), extra.at[n], e_send.at[n], e_recv.at[n], at.flip(mask))
        fin_slot(mine)[...] = fin_slot(mine)[...] + extra[n]
    def write(src, dst, n):
        copy = pltpu.make_async_copy(src, dst, done_sem.at[n])
        copy.start()
        written.append(copy)

    fin_go(0)
    for da, db in peers:
        origin = at.at(-da, -db)
        at.arrived(small_land.at[origin], s_recv.at[origin])
    small = jnp.sum(small_land[...], axis=0)
    lanes = lax.broadcasted_iota(jnp.int32, (slab, 128), 1)
    sides = jnp.concatenate(
        [jnp.where(lanes == 6, bias_q, jnp.where(lanes == 7, bias_v, 0.0)), jnp.zeros((256 - slab, 128), F32)],
        axis=0,
    )
    sides = jnp.concatenate([sides[:128].T[:8], sides[128:].T[:8]], axis=1)
    shift = me * slab - lax.min(me * slab // 128 * 128, width - 256)
    window = pltpu.roll(small[:, :256], lax.rem(256 - shift, 256), 1)
    tall = lax.broadcasted_iota(jnp.int32, (8, 256), 0)
    small_got[0, :, :256] = jnp.where(tall < 5, window, sides)
    small_got[0, :, 256:] = pltpu.roll(small[:, 256:], lax.rem(128 - me * unit, 128), 1)

    def small_round(n):
        at.send(
            small_got.at[2 * n], small_got.at[2 * n + 1], b_send.at[n], b_recv.at[n], rep=at.flip(every[n])
        )

    def small_add(n):
        at.arrived(small_got.at[2 * n + 1], b_recv.at[n])
        small_got[2 * n + 2] = small_got[2 * n] + small_got[2 * n + 1]

    small_round(0)
    rows_summed(2)
    for da, db in peers:
        origin = at.at(-da, -db)
        at.arrived(gw_land.at[origin], va_recv.at[origin])
    for n, mask in enumerate(extras):
        at.exchange(gw_land, gw_extra.at[n], ve_send.at[n], ve_recv.at[n], at.flip(mask))
        gw_land[...] = gw_land[...] + gw_extra[n]
    for j in range(shards):
        for t in range(3):
            first = t * width + j * slab
            gw_ref[mine, :, first : first + slab] = gw_land[j, :, t * slab : (t + 1) * slab]

    gw_go(0)
    small_add(0)
    small_round(1)
    rows_summed(3)
    row_sums.joined(3)
    for n in range(count - 1):
        fin_take(n)
        fin_go(n + 1)
        gw_take(n)
        gw_go(n + 1)
    for n in range(1, len(every)):
        small_add(n)
        if n + 1 < len(every):
            small_round(n + 1)
    small_out_ref[...] = small_got[2 * len(every)]

    total = row_sums.result().astype(F32)
    x = x_ref[...].astype(F32)
    r = lax.rsqrt(jnp.mean(x * x, axis=-1, keepdims=True) + EPS)
    weighted = vec_ref[0:1, :] * total
    gin_ref[...] = gmixed_ref[...] + r * weighted - x * (r * r * r) * jnp.mean(x * weighted, axis=-1, keepdims=True)


    write(gin_ref, gin_hbm, 3)
    fin_take(count - 1)
    write(fin_ref, fin_hbm, 1)
    gw_take(count - 1)
    write(gw_ref, gw_hbm, 2)
    at.settle()
    for copy in written:
        copy.wait()


def layer(shards, replicas, inputs, segment_ids, positions, vectors, w_qkv, w_out, w_up, w_down, cotangent):
    block, width = inputs.shape
    slab = width // shards
    slab3 = 3 * slab
    length = shards * block
    wparts = 2 if slab % 32 == 0 else 1
    parts = parts_of(slab)
    halves = parts // 2
    rp = slab // parts
    rows_part = slab // 2 if parts == 4 else slab
    cols = width // 2
    minor = shards // MAJOR
    peers = shards - 1
    bits = (replicas - 1).bit_length()
    more = bits - (parts - 1).bit_length()
    shape = jax.ShapeDtypeStruct
    dma = pltpu.SemaphoreType.DMA
    vm = pltpu.VMEM
    return pl.pallas_call(
        functools.partial(layer_kernel, shards, replicas, wparts, parts, 2 * block),
        out_shape=(
            shape((block, width), BF16),
            shape((3, slab, width), BF16),
            shape((parts, rp, 3 * width), BF16),
            shape((block, width), F32),
            shape((8, 384), F32),
        ),
        in_specs=[VMEM] * 11 + [ANY] * 5,
        out_specs=[ANY] * 4 + [VMEM],
        scratch_shapes=[
            vm((block, width), BF16),
            vm((3, slab, width), BF16),
            vm((parts, rp, 3 * width), BF16),
            vm((block, width), F32),
            vm(w_qkv.shape, BF16),
            vm((block, width), BF16),
            vm((16, 256), F32),
            vm((length, width), BF16),
            vm((slab3, length), BF16),
            vm((slab, length), F32),
            vm((8, length), F32),
            vm((8, width), F32),
            vm((8, length), F32),
            vm((shards, wparts, slab // wparts, slab3), BF16),
            vm((3, shards, halves, slab // halves, block), BF16),
            vm((3, block, width), BF16),
            vm((width, block), BF16),
            vm((8, width), F32),
            vm((block, width), F32),
            vm((shards, block, width), BF16),
            vm((shards, 8, 256), F32),
            vm((shards, wparts, slab // wparts, slab3), BF16),
            vm((slab3, width), BF16),
            vm((slab, length), BF16),
            vm((width, block), BF16),
            vm((3, width, width), BF16),
            vm((slab, length), BF16),
            vm((slab3, length), F32),
            vm((length, slab3), BF16),
            vm((3, shards, rows_part, parts * block), BF16),
            vm((3, parts * block, cols), BF16),
            vm((3, shards, rows_part, block) if parts == 4 else (1, 1, 16, block), BF16),
            vm((3, MAJOR, minor, rows_part, cols), BF16),
            vm((3, minor - 1, MAJOR, rows_part, cols), BF16),
            vm((3, MAJOR + 1, rows_part, cols), BF16),
            vm((max(more, 1), 3, rows_part, cols), BF16),
            vm((shards, parts, rp, slab3), BF16),
            vm((halves, shards, rp, slab3), BF16),
            vm((shards, rp, slab3) if parts == 4 else (1, 16, 128), BF16),
            vm((shards, rp, slab3), BF16),
            vm((shards, rp, slab3), BF16),
            vm((max(more, 1), shards, rp, slab3), BF16),
            vm((shards, 8, 384), F32),
            vm((shards, 8, 384), F32),
            vm((2 * bits + 1, 8, 384), F32),
            dma((2, MAJOR)), dma((MAJOR, minor - 1)), dma((shards,)),
            dma((peers,)), dma((shards,)),
            dma((peers,)), dma((shards, wparts)), dma((shards,)), dma((shards,)),
            dma((2, MAJOR)), dma((MAJOR, minor - 1)), dma((shards, parts)),
            dma((shards,)), dma((shards, 2)),
            dma((5,)), dma((shards,)), dma((shards,)), dma((4,)),
            dma((peers,)), dma((shards,)),
            dma((3, 3)), dma((3, 3)),
            dma((3, 4)), dma((3, 4)),
            dma((3, minor - 1)), dma((3, minor - 1)),
            dma((3, MAJOR)), dma((3, MAJOR + 1)),
            dma((parts,)), dma((parts,)),
            dma((max(more, 1),)), dma((max(more, 1),)),
            dma((minor - 1, MAJOR)), dma((minor - 1, MAJOR)),
            dma((MAJOR,)), dma((MAJOR + 1,)),
            dma((halves,)), dma((halves,)),
            dma((1,)), dma((1,)),
            dma((peers,)), dma((shards,)),
            dma((parts,)), dma((parts,)),
            dma((max(more, 1),)), dma((max(more, 1),)),
            dma((peers,)), dma((shards,)),
            dma((bits,)), dma((bits,)),
        ],
        compiler_params=pltpu.CompilerParams(
            collective_id=0, has_side_effects=True, vmem_limit_bytes=62 << 20
        ),
        name="layer",
    )(inputs, segment_ids, positions, *vectors, w_qkv, w_out, w_up, w_down, cotangent)


def finish_kernel(
    slab, unit, fin_ref, gw_ref, small_ref, gin_ref, out_ref,
    w_out_ref, w_up_ref, w_down_ref, w_qkv_ref, input_ref, output_ref,
    gain_one_ref, b_query_ref, b_value_ref, scale_ref, b_out_ref, gain_two_ref, b_up_ref, b_down_ref,
):
    w_out_ref[...] = fin_ref[0].astype(F32)
    w_up_ref[...] = fin_ref[1].astype(F32)
    w_down_ref[...] = fin_ref[2].astype(F32)
    w_qkv_ref[...] = gw_ref[...].astype(F32)
    input_ref[...] = gin_ref[...]
    output_ref[...] = out_ref[...]

    @pl.when(pl.program_id(0) == 0)
    def _():
        table = {
            0: gain_one_ref, 1: b_out_ref, 2: gain_two_ref, 3: b_up_ref, 4: b_down_ref,
            6: b_query_ref, 7: b_value_ref,
        }
        for row, ref in table.items():
            ref[...] = small_ref[row : row + 1, :slab].reshape(slab)
        scale_ref[...] = small_ref[5:6, 256 : 256 + unit].reshape(unit)


def finish(fin, gw, small, gin, out):
    slab, width = fin.shape[1:]
    block = gin.shape[0]
    steps = 4 if slab % 32 == 0 else 2
    unit = HEAD * slab // width
    part, tokens = slab // steps, block // steps
    shape = jax.ShapeDtypeStruct

    def rows(size, columns):
        return pl.BlockSpec((size, columns), lambda i: (i, 0))

    whole = pl.BlockSpec((8, 384), lambda i: (0, 0))
    vector = pl.BlockSpec((slab,), lambda i: (0,))
    return pl.pallas_call(
        functools.partial(finish_kernel, slab, unit),
        grid=(steps,),
        out_shape=[shape((slab, width), F32)] * 3
        + [shape((slab, 3 * width), F32), shape((block, width), F32), shape((block, width), BF16)]
        + [shape((slab,), F32)] * 3
        + [shape((unit,), F32)]
        + [shape((slab,), F32)] * 4,
        in_specs=[
            pl.BlockSpec((3, part, width), lambda i: (0, i, 0)), rows(part, 3 * width), whole,
            rows(tokens, width), rows(tokens, width),
        ],
        out_specs=[rows(part, width)] * 3
        + [rows(part, 3 * width), rows(tokens, width), rows(tokens, width)]
        + [vector] * 3
        + [pl.BlockSpec((unit,), lambda i: (0,))]
        + [vector] * 4,
        name="finish",
    )(fin, gw, small, gin, out)


def on_device(
    inputs, segment_ids, positions, gain_one, w_qkv, b_query, b_value, query_scale, w_out, b_out,
    gain_two, w_up, b_up, w_down, b_down, cotangent,
):
    shards = lax.axis_size("shard")
    replicas = lax.axis_size("replica")
    block, width = inputs.shape[1:]
    slab = width // shards
    output, fin, gw, input_grad, small = layer(
        shards, replicas, inputs.reshape(block, width), segment_ids, positions,
        (gain_one, b_query, b_value, query_scale, b_out, gain_two, b_up, b_down),
        w_qkv, w_out, w_up, w_down, cotangent.reshape(block, width),
    )
    (
        g_out, g_up, g_down, g_qkv, input_grad, output, g_gain_one, g_b_query, g_b_value, g_scale, g_b_out,
        g_gain_two, g_b_up, g_b_down,
    ) = finish(fin, gw.reshape(slab, 3 * width), small, input_grad, output)
    return (
        output[None], input_grad[None], g_gain_one, g_qkv, g_b_query, g_b_value, g_scale, g_out, g_b_out,
        g_gain_two, g_up, g_b_up, g_down, g_b_down,
    )


def solution(mesh):
    rows = P("replica", "shard", None)
    ids = P("replica", "shard")
    vector = P("shard")
    matrix = P("shard", None)
    in_specs = (
        rows, ids, ids, vector, matrix, vector, vector, vector, matrix, vector, vector, matrix, vector,
        matrix, vector, rows,
    )
    out_specs = (
        rows, rows, vector, matrix, vector, vector, vector, matrix, vector, vector, matrix, vector, matrix,
        vector,
    )
    return jax.shard_map(on_device, mesh=mesh, in_specs=in_specs, out_specs=out_specs, check_vma=False)
```

```python
import functools
import math

import jax
import jax.numpy as jnp
from jax import lax
from jax.experimental import pallas as pl
from jax.experimental.pallas import tpu as pltpu
from jax.sharding import PartitionSpec as P

HEADS = 16
HEAD = 80
EPS = 1e-06
QUERY_BASE = 1.442695041
MASKED = -1000000000.0
MESH = pl.DeviceIdType.MESH
MAJOR = 4
VMEM = pl.BlockSpec(memory_space=pltpu.VMEM)
ANY = pl.BlockSpec(memory_space=pl.ANY)
F32 = jnp.float32
BF16 = jnp.bfloat16
NN = (((1,), (0,)), ((), ()))
NT = (((1,), (1,)), ((), ()))
TN = (((0,), (0,)), ((), ()))


def dot(lhs, rhs, dims=NN):
    return lax.dot_general(lhs, rhs, dims, preferred_element_type=F32)


class Place:
    def __init__(self, shards):
        self.shards = shards
        self.minor = shards // MAJOR
        self.me = lax.axis_index("shard")
        self.rep = lax.axis_index("replica")
        self.a = self.me // self.minor
        self.b = lax.rem(self.me, self.minor)
        self.started = []

    def at(self, da, db):
        a = lax.rem(self.a + da + MAJOR, MAJOR)
        b = lax.rem(self.b + db + self.minor, self.minor)
        return a * self.minor + b

    def peers(self):
        return [(da, db) for da in range(MAJOR) for db in range(self.minor) if da or db]

    def flip(self, mask):
        bit = lax.rem(self.rep // mask, 2)
        return self.rep + mask - 2 * mask * bit

    def greet(self, masks):
        barrier = pltpu.get_barrier_semaphore()
        for da, db in self.peers():
            pl.semaphore_signal(
                barrier, inc=1, device_id=(self.at(da, db), self.rep), device_id_type=MESH
            )
        for mask in masks:
            pl.semaphore_signal(
                barrier, inc=1, device_id=(self.me, self.flip(mask)), device_id_type=MESH
            )
        pl.semaphore_wait(barrier, len(self.peers()) + len(masks))

    def send(self, src, dst, ssem, rsem, shard=None, rep=None, when=None):
        copy = pltpu.make_async_remote_copy(
            src_ref=src,
            dst_ref=dst,
            send_sem=ssem,
            recv_sem=rsem,
            device_id=(self.me if shard is None else shard, self.rep if rep is None else rep),
            device_id_type=MESH,
        )
        if when is None:
            copy.start()
        else:
            @pl.when(when)
            def _():
                copy.start()
        self.started.append((when, copy))

    def arrived(self, dst, rsem):
        pltpu.make_async_remote_copy(
            src_ref=dst,
            dst_ref=dst,
            send_sem=rsem,
            recv_sem=rsem,
            device_id=(self.me, self.rep),
            device_id_type=MESH,
        ).wait_recv()

    def exchange(self, src, dst, ssem, rsem, rep):
        self.send(src, dst, ssem, rsem, rep=rep)
        self.arrived(dst, rsem)
        self.started.pop()[1].wait_send()

    def settle(self):
        for when, copy in self.started:
            if when is None:
                copy.wait_send()
            else:
                @pl.when(when)
                def _():
                    copy.wait_send()
        self.started = []


class Line:
    def __init__(self, at, slot, major_send, minor_send, recv):
        self.at, self.slot = at, slot
        self.major_send, self.minor_send, self.recv = major_send, minor_send, recv

    def onward(self, origin, up, down, d):
        at = self.at
        if up is not None:
            at.send(
                self.slot(origin), self.slot(origin), self.major_send.at[0, d], self.recv(origin),
                shard=lax.min(at.a + 1, MAJOR - 1) * at.minor + at.b, when=up,
            )
        if down is not None:
            at.send(
                self.slot(origin), self.slot(origin), self.major_send.at[1, d], self.recv(origin),
                shard=lax.max(at.a - 1, 0) * at.minor + at.b, when=down,
            )

    def across(self, origin, when=None):
        at = self.at
        for db in range(1, at.minor):
            at.send(
                self.slot(origin), self.slot(origin), self.minor_send.at[origin // at.minor, db - 1],
                self.recv(origin), shard=at.at(0, db), when=when,
            )

    def along_own(self):
        at = self.at
        self.onward(at.me, at.a + 1 < MAJOR, at.a > 0, 0)

    def sides(self, d):
        at = self.at
        for side in (-1, 1):
            ok = (at.a - d >= 0) if side < 0 else (at.a + d < MAJOR)
            origin = lax.max(at.a - d, 0) if side < 0 else lax.min(at.a + d, MAJOR - 1)
            yield side, ok, origin * at.minor + at.b

    def take(self, d, then=None):
        for side, ok, origin in self.sides(d):
            @pl.when(ok)
            def _():
                self.at.arrived(self.slot(origin), self.recv(origin))

            if then is not None:
                then(origin, ok)

    def along(self, d):
        at = self.at
        if d + 1 < MAJOR:
            for side, ok, origin in self.sides(d):
                if side < 0:
                    self.onward(origin, ok & (at.a + 1 < MAJOR), None, d)
                else:
                    self.onward(origin, None, ok & (at.a > 0), d)

    def aside(self, d):
        for side, ok, origin in self.sides(d):
            self.across(origin, when=ok)

    def step(self, d, then=None):
        self.take(d, then)
        self.along(d)
        self.aside(d)


def parts_of(rows):
    return 4 if rows % 32 == 0 else 2


def part_box(part, parts, rows, cols):
    if parts == 4:
        i, j, rows = lax.rem(part, 2), part // 2, rows // 2
    else:
        i, j = 0, part
    return i * rows, rows, j * (cols // 2), cols // 2


def flipped(part, mask):
    bit = lax.rem(part // mask, 2)
    return part + mask - 2 * mask * bit


def layer_kernel(
    shards, replicas, wparts, parts, qblock,
    x_ref, segment_ref, position_ref, gain_one_ref, b_query_ref, b_value_ref, scale_ref,
    b_out_ref, gain_two_ref, b_up_ref, b_down_ref, w_hbm, wout_ref, wup_ref, wdown_ref, cot_hbm,
    out_hbm, fin_hbm, gw_hbm, gin_hbm, small_out_ref,
    out_ref, fin_ref, gw_ref, gin_ref, w_ref, cot_ref, small_ref,
    normed_ref, qkv_ref, query_ref, log_ref, vec_ref, start_ref, wcols_ref,
    xt_ref, dy_ref, dctx_ref, row_ref, gmixed_ref,
    xg, packets, pieces, turned, context, att, weights,
    dctx, grads, proj, left, right, stash, sums, from_x, from_z, extra,
    gw, gw_core, gw_y, gw_sum, gw_land, gw_extra,
    windows, small_land, small_got,
    xm_send, xn_send, x_recv, p_send, p_recv, w_send, w_recv, wc_send, wy_send,
    fm_send, fn_send, f_recv, fy_send, fc_send, local_sem, a_send, a_recv, done_sem,
    d_send, d_recv, gy_send, gy_recv, gc_send, gc_recv, gx_send, gx_recv, gz_send, gz_recv,
    r_send, r_recv, e_send, e_recv, nx_send, nx_recv, nz_send, nz_recv,
    vc_send, vc_recv, vy_send, vy_recv, va_send, va_recv, vr_send, vr_recv, ve_send, ve_recv,
    s_send, s_recv, b_send, b_recv,
):
    at = Place(shards)
    me, minor = at.me, at.minor
    block, width = x_ref.shape
    length = shards * block
    slab = width // shards
    slab3 = 3 * slab
    local = slab // HEAD
    peers = at.peers()
    masks = (2, 1) if parts == 4 else (1,)
    every = []
    bit = 1
    while bit < replicas:
        every.append(bit)
        bit *= 2
    extras = [m for m in every if m >= parts]
    mine = lax.rem(at.rep, parts)
    wpart = lax.rem(at.rep, wparts)

    loads = []
    for m, ref in enumerate((wout_ref, wup_ref, wdown_ref)):
        copy = pltpu.make_async_copy(
            ref, weights.at[m, pl.ds(pl.multiple_of(me * slab, 16), slab), :], local_sem.at[m]
        )
        copy.start()
        loads.append(copy)
    w_load = pltpu.make_async_copy(w_hbm, w_ref, local_sem.at[3])
    w_load.start()
    cot_load = pltpu.make_async_copy(cot_hbm, cot_ref, local_sem.at[4])
    cot_load.start()
    xg[me] = x_ref[...]
    small_ref[...] = jnp.zeros_like(small_ref)
    table = {
        0: gain_one_ref, 1: b_out_ref, 2: gain_two_ref, 3: b_up_ref, 4: b_down_ref, 5: scale_ref,
        8: b_query_ref, 9: b_value_ref,
    }
    for row, ref in table.items():
        size = ref.shape[0]
        small_ref[row : row + 1, :size] = ref[...].astype(F32).reshape(1, size)
    place = me * block + lax.broadcasted_iota(jnp.int32, (1, block), 1)
    small_ref[6:7, :block] = (place - position_ref[...]).astype(F32)
    small_ref[10:11, :block] = (segment_ref[...] != 0).astype(F32)
    packets[me] = small_ref[:8]
    at.greet(tuple(every))

    def wslot(origin, part):
        row, rows, col, cols = part_box(part, parts, slab, width)
        return weights.at[
            :,
            pl.ds(pl.multiple_of(origin * slab + row, 16), rows),
            pl.ds(pl.multiple_of(col, 128), cols),
        ]

    rows_line = Line(at, lambda o: xg.at[o], xm_send, xn_send, lambda o: x_recv.at[o])
    ffn_line = Line(
        at, lambda o: wslot(o, mine), fm_send, fn_send, lambda o: f_recv.at[o, mine]
    )

    def to_replicas(origin, when=None):
        slot = wslot(origin, mine)
        for mask in masks:
            sem = fy_send.at[origin] if mask == 2 else fc_send.at[origin, 0]
            at.send(slot, slot, sem, f_recv.at[origin, mine], rep=at.flip(mask), when=when)

    cols = width // 2
    core = lax.rem(at.rep, 2)
    i_part = lax.rem(mine, 2) if parts == 4 else 0
    j_part = mine // 2 if parts == 4 else mine
    mats = (2, 1, 0)

    def lane(n, size):
        return pl.ds(pl.multiple_of(n * size, 128), size)

    def seat(n):
        return slice(n * block, (n + 1) * block)

    near = parts // 2

    def meet_columns(m):
        if parts == 4:
            at.send(
                dy_ref.at[m, :, lane(1 - j_part, cols)], right.at[m, seat(1), :],
                gy_send.at[m, 1], gy_recv.at[m, 1], rep=at.flip(2),
            )
        at.send(
            dy_ref.at[m, :, lane(j_part if parts == 4 else 1 - j_part, cols)], right.at[m, seat(near), :],
            gc_send.at[m, 1], gc_recv.at[m, 1], rep=at.flip(1),
        )
        right[m, seat(0), :] = dy_ref[m, :, lane(j_part, cols)]

    def meet_rows(m):
        if parts == 4:
            far = at.flip(2)
            at.send(xt_ref.at[m, :, 1 - i_part], stash.at[m], gy_send.at[m, 2], gy_recv.at[m, 2], rep=far)
            at.send(
                xt_ref.at[m, :, i_part], left.at[m, :, :, seat(1)], gy_send.at[m, 0], gy_recv.at[m, 0], rep=far
            )
        at.send(
            xt_ref.at[m, :, 1 - i_part if parts == 4 else 0], left.at[m, :, :, seat(near)],
            gc_send.at[m, 0], gc_recv.at[m, 0], rep=at.flip(1),
        )
        left[m, :, :, seat(0)] = xt_ref[m, :, i_part]

    def relay_columns(m):
        if parts == 4:
            at.arrived(right.at[m, seat(1), :], gy_recv.at[m, 1])
            at.send(
                right.at[m, seat(1), :], right.at[m, seat(3), :], gc_send.at[m, 3], gc_recv.at[m, 3], rep=at.flip(1)
            )

    def relay_rows(m):
        if parts == 4:
            at.arrived(stash.at[m], gy_recv.at[m, 2])
            at.send(stash.at[m], left.at[m, :, :, seat(3)], gc_send.at[m, 2], gc_recv.at[m, 2], rep=at.flip(1))

    for i, (da, db) in enumerate(peers):
        at.send(packets.at[me], packets.at[me], p_send.at[i], p_recv.at[me], shard=at.at(da, db))
    rows_line.along_own()
    for copy in loads:
        copy.wait()
    ffn_line.across(me)
    rows_line.across(me)
    cot_load.wait()
    dy_ref[2] = cot_ref[...]
    meet_columns(2)
    w_load.wait()
    cut = slab // wparts
    for j in range(shards):
        for t in range(3):
            first = t * width + j * slab
            pieces[j, :, :, t * slab : (t + 1) * slab] = w_ref[:, first : first + slab].reshape(
                wparts, cut, slab
            )
    parity = lax.rem(at.a + mine // 2, 2)
    chosen = parity == 0 if parts == 4 else None
    for i, (da, db) in enumerate(peers):
        dest = at.at(da, db)
        at.send(
            pieces.at[dest, wpart], wcols_ref.at[me, wpart], w_send.at[i], w_recv.at[me, wpart], shard=dest,
            when=chosen,
        )
    wcols_ref[me] = pieces[me]
    ffn_line.along_own()

    def ffn_minor(distance):
        for db in range(1, minor):
            sides = ((-1, 1) if distance else (0,))
            for side in sides:
                a = at.a + side * distance
                ok = None
                if distance:
                    ok = (a >= 0) & (a < MAJOR)
                origin = lax.max(lax.min(a, MAJOR - 1), 0) * minor + lax.rem(at.b + db, minor)
                slot = wslot(origin, mine)
                if ok is None:
                    at.arrived(slot, f_recv.at[origin, mine])
                else:
                    @pl.when(ok)
                    def _():
                        at.arrived(slot, f_recv.at[origin, mine])
                to_replicas(origin, ok)

    def columns(phase):
        for q in range(2):
            for db in range(minor):
                da = lax.rem(parity + phase, 2) + 2 * q
                origin = at.at(-da, -db)
                slot = wcols_ref.at[origin, wpart]
                real = origin != me

                @pl.when(real)
                def _():
                    at.arrived(slot, w_recv.at[origin, wpart])

                if parts == 4 and phase == 0:
                    at.send(
                        slot, slot, wy_send.at[origin], w_recv.at[origin, wpart], rep=at.flip(2), when=real
                    )
                if wparts == 2:
                    at.send(
                        slot, slot, wc_send.at[origin], w_recv.at[origin, wpart], rep=at.flip(1), when=real
                    )

    ffn_minor(0)
    rows_line.step(1)
    ffn_line.step(1, to_replicas)
    rows_line.step(2)
    columns(0)

    for da, db in peers:
        origin = at.at(-da, -db)
        at.arrived(packets.at[origin], p_recv.at[origin])
    vectors = jnp.zeros((8, width), F32)
    scales = jnp.zeros((1, 128), F32)
    lanes = lax.broadcasted_iota(jnp.int32, (8, width), 1)
    unit = HEAD // shards
    for j in range(shards):
        piece = packets[j]
        wide = jnp.concatenate([piece, jnp.zeros((8, width - piece.shape[1]), F32)], axis=1)
        wide = jnp.where(lanes < slab, wide, 0.0)
        vectors = vectors + (pltpu.roll(wide, j * slab, 1) if j else wide)
        scale = jnp.where(lanes[0:1, :128] < unit, piece[5:6, :128], 0.0)
        scales = scales + (pltpu.roll(scale, j * unit, 1) if j else scale)
        start_ref[:, j * block : (j + 1) * block] = jnp.broadcast_to(piece[6:7, :block], (8, block))
    rows = lax.broadcasted_iota(jnp.int32, (8, width), 0)
    vec_ref[...] = jnp.where(rows < 5, vectors, 0.0)
    vec_ref[5:6, :128] = scales
    gain = vec_ref[0:1, :]
    column = jnp.broadcast_to(scales, (128, 128)).T[:HEAD, 0:1]
    soft = jnp.maximum(column, 0.0) + jnp.log(1.0 + jnp.exp(-jnp.abs(column)))
    factor = jnp.concatenate([QUERY_BASE / math.sqrt(HEAD) * soft] * local, axis=0)
    own = small_ref[8:16, :]
    tall = jnp.concatenate([own, jnp.zeros((120, 256), F32)], axis=0)
    tall = jnp.concatenate([tall[:, :128].T, tall[:, 128:].T], axis=0)
    bias_query = tall[:slab, 0:1]
    bias_value = tall[:slab, 1:2]

    ffn_line.step(2, to_replicas)
    ffn_minor(1)
    rows_line.step(3)
    columns(1)
    relay_columns(2)
    if wparts == 2:
        for da, db in peers:
            origin = at.at(-da, -db)
            last = wparts - 1 - wpart
            at.arrived(wcols_ref.at[origin, last], w_recv.at[origin, last])
    turned[...] = wcols_ref[...].reshape(width, slab3).T

    def project(origin):
        rows_in = xg[origin].astype(F32)
        scale = lax.rsqrt(jnp.mean(rows_in * rows_in, axis=-1, keepdims=True) + EPS)
        normed = (rows_in * scale * gain).astype(BF16)
        tokens = pl.ds(pl.multiple_of(origin * block, block), block)
        normed_ref[tokens, :] = normed
        out = dot(turned[...], normed, NT)
        query = out[:slab] + bias_query
        query_ref[:, tokens] = query
        qkv_ref[:slab, tokens] = (query * factor).astype(BF16)
        qkv_ref[slab : 2 * slab, tokens] = out[slab : 2 * slab].astype(BF16)
        qkv_ref[2 * slab :, tokens] = (out[2 * slab :] + bias_value).astype(BF16)

    ffn_line.step(3, to_replicas)

    def project_major(i, carry):
        project(at.at(i, 0))
        return carry

    def project_minor(i, carry):
        origin = at.at(lax.rem(i, MAJOR), 1 + i // MAJOR)
        at.arrived(xg.at[origin], x_recv.at[origin])
        project(origin)
        return carry

    lax.fori_loop(0, MAJOR, project_major, 0)
    ffn_minor(2)
    lax.fori_loop(0, shards - MAJOR, project_minor, 0)
    ffn_minor(3)

    log_ref[...] = jnp.zeros_like(log_ref)
    for i in range(length // qblock):
        reach = (i + 1) * qblock
        span = slice(i * qblock, reach)
        starts = start_ref[0:1, span]
        key_place = lax.broadcasted_iota(jnp.int32, (reach, qblock), 0).astype(F32)
        query_place = (i * qblock + lax.broadcasted_iota(jnp.int32, (1, qblock), 1)).astype(F32)
        allowed = (key_place >= starts) & (key_place <= query_place)
        for h in range(local):
            head = slice(h * HEAD, (h + 1) * HEAD)
            queries = qkv_ref[h * HEAD : (h + 1) * HEAD, span]
            keys = qkv_ref[slab + h * HEAD : slab + (h + 1) * HEAD, :reach]
            values = qkv_ref[2 * slab + h * HEAD : 2 * slab + (h + 1) * HEAD, :reach]
            scores = jnp.where(allowed, dot(keys, queries, TN), MASKED)
            top = jnp.max(scores, axis=0, keepdims=True)
            powers = jnp.exp(scores - top)
            total = jnp.sum(powers, axis=0, keepdims=True)
            probs = (powers * (1.0 / total)).astype(BF16)
            log_ref[h : h + 1, span] = top + jnp.log(total)
            context[head, span] = dot(values, probs).astype(BF16)
        heads = pl.ds(pl.multiple_of(me * slab, 16), slab)
        for j in range(i * qblock // block, reach // block):
            piece = slice(j * block, (j + 1) * block)
            at.send(context.at[:, piece], att.at[heads, :], a_send.at[j], a_recv.at[me], shard=j, when=me != j)

            @pl.when(me == j)
            def _():
                att[heads, :] = context[:, piece]

    order = [(0, db) for db in range(1, minor)]
    order += [(da, db) for da in range(1, MAJOR) for db in range(minor)]
    if parts == 4:
        for da, db in order:
            origin = at.at(da, db)
            part = flipped(mine, 2)
            slot = wslot(origin, part)
            at.arrived(slot, f_recv.at[origin, part])
            at.send(slot, slot, fc_send.at[origin, 1], f_recv.at[origin, part], rep=at.flip(1))
    for da, db in peers:
        origin = at.at(-da, -db)
        at.arrived(att.at[pl.ds(pl.multiple_of(origin * slab, 16), slab), :], a_recv.at[origin])
    others = [flipped(mine, 1)] + ([flipped(flipped(mine, 1), 2)] if parts == 4 else [])
    for da, db in order:
        origin = at.at(da, db)
        for part in others:
            at.arrived(wslot(origin, part), f_recv.at[origin, part])

    def weight(m):
        at.arrived(left.at[m, :, :, seat(near)], gc_recv.at[m, 0])
        at.arrived(right.at[m, seat(near), :], gc_recv.at[m, 1])
        if parts == 4:
            at.arrived(left.at[m, :, :, seat(1)], gy_recv.at[m, 0])
            at.arrived(left.at[m, :, :, seat(3)], gc_recv.at[m, 2])
            at.arrived(right.at[m, seat(3), :], gc_recv.at[m, 3])
        rows = left.shape[1] * left.shape[2]
        out = dot(left[m].reshape(rows, parts * block), right[m])
        sums[m] = out.reshape(sums.shape[1:]).astype(BF16)

    def weight_across(m):
        for db in range(1, minor):
            at.send(
                sums.at[m, :, lax.rem(at.b + db, minor)], from_x.at[m, db - 1],
                gx_send.at[m, db - 1], gx_recv.at[m, db - 1], shard=at.at(0, db),
            )

    ahead = jnp.where(at.a < MAJOR // 2, 1, -1)
    middle = (at.a > 0) & (at.a < MAJOR - 1)

    def turn(n):
        return jnp.where(at.a < MAJOR // 2, MAJOR - 1 - n, n)

    class Chain:
        def __init__(self, own, land, ssem, rsem):
            self.own, self.land, self.ssem, self.rsem = own, land, ssem, rsem

        def go(self, n, when=None):
            t = turn(n)
            way = -ahead if n == 3 else ahead
            to = lax.max(lax.min(at.a + way, MAJOR - 1), 0) * minor + at.b
            dst = jnp.where(middle, MAJOR, t) if n == 1 else t
            at.send(self.own(t), self.land(dst), self.ssem.at[n], self.rsem.at[dst], shard=to, when=when)

        def summed(self, n):
            if n < 3:
                self.go(n, jnp.logical_not(middle))

        def joined(self, n):
            t = turn(n)

            @pl.when(middle)
            def _():
                at.arrived(self.land(t), self.rsem.at[t])
                self.own(t)[...] = self.own(t)[...] + self.land(t)[...]

            self.go(n, middle)

        def result(self):
            at.arrived(self.land(at.a), self.rsem.at[at.a])
            total = self.own(at.a)[...].astype(F32) + self.land(at.a)[...].astype(F32)
            self.own(at.a)[...] = total.astype(BF16)

            @pl.when(middle)
            def _():
                at.arrived(self.land(MAJOR), self.rsem.at[MAJOR])
                self.own(at.a)[...] = (total + self.land(MAJOR)[...].astype(F32)).astype(BF16)

            return self.own(at.a)[...]

    ffn_sums = {
        m: Chain(
            lambda t, m=m: sums.at[m, t, at.b], lambda n, m=m: from_z.at[m, n], gz_send.at[m], gz_recv.at[m]
        )
        for m in mats
    }

    def land_x(db, t):
        first = (db - 1) // 2 * MAJOR + t
        return weights.at[(db - 1) % 2, pl.ds(pl.multiple_of(first * block, block), block), :]

    def land_z(n):
        return weights.at[1, pl.ds(pl.multiple_of((MAJOR + n) * block, block), block), :]

    row_sums = Chain(lambda t: xg.at[t * minor + at.b], land_z, nz_send, nz_recv)

    def rows_across(n):
        t = turn(n)
        for db in range(1, minor):
            to = t * minor + lax.rem(at.b + db, minor)
            at.send(
                xg.at[to], land_x(db, t), nx_send.at[db - 1, n], nx_recv.at[db - 1, t], shard=at.at(0, db)
            )

    def rows_summed(n):
        t = turn(n)
        own = row_sums.own(t)
        total = own[...].astype(F32)
        for db in range(1, minor):
            at.arrived(land_x(db, t), nx_recv.at[db - 1, t])
            total = total + land_x(db, t)[...].astype(F32)
        own[...] = total.astype(BF16)
        row_sums.summed(n)

    def weight_summed(m):
        for db in range(1, minor):
            at.arrived(from_x.at[m, db - 1], gx_recv.at[m, db - 1])
        for n in range(MAJOR):
            t = turn(n)
            total = sums[m, t, at.b].astype(F32)
            for db in range(1, minor):
                total = total + from_x[m, db - 1, t].astype(F32)
            sums[m, t, at.b] = total.astype(BF16)
            ffn_sums[m].summed(n)

    def weight_joined(m, n):
        ffn_sums[m].joined(n)

    def rows_last_across():
        t = turn(3)
        for n in range(2):
            half = pl.ds(n * cols, cols)
            for db in range(1, minor):
                to = t * minor + lax.rem(at.b + db, minor)
                at.send(
                    xg.at[to, :, half], land_x(db, t).at[:, half], nx_send.at[db - 1, 3 + n],
                    nx_recv.at[db - 1, MAJOR if n else t], shard=at.at(0, db),
                )

    def rows_last():
        t = turn(3)
        own = row_sums.own(t)
        to = lax.max(lax.min(at.a - ahead, MAJOR - 1), 0) * minor + at.b
        for n in range(2):
            half = pl.ds(n * cols, cols)
            total = own[:, half].astype(F32)
            for db in range(1, minor):
                piece = land_x(db, t).at[:, half]
                at.arrived(piece, nx_recv.at[db - 1, MAJOR if n else t])
                total = total + piece[...].astype(F32)
            own[:, half] = total.astype(BF16)

            @pl.when(middle)
            def _():
                if n == 0:
                    at.arrived(land_z(t), nz_recv.at[t])
                own[:, half] = own[:, half] + land_z(t)[:, half]

            at.send(
                own.at[:, half], land_z(t).at[:, half], nz_send.at[3 + n],
                nz_recv.at[MAJOR + 1 if n else t], shard=to, when=middle,
            )

    def rows_result():
        own = row_sums.own(at.a)
        mine_z = land_z(at.a)

        @pl.when(middle)
        def _():
            at.arrived(mine_z, nz_recv.at[at.a])
            at.arrived(land_z(MAJOR), nz_recv.at[MAJOR])
            first = own[...].astype(F32) + mine_z[...].astype(F32)
            gin_ref[...] = first + land_z(MAJOR)[...].astype(F32)

        @pl.when(jnp.logical_not(middle))
        def _():
            at.arrived(mine_z.at[:, :cols], nz_recv.at[at.a])
            at.arrived(mine_z.at[:, cols:], nz_recv.at[MAJOR + 1])
            gin_ref[...] = own[...].astype(F32) + mine_z[...].astype(F32)

        return gin_ref[...]

    def fin_slot(part, m=None):
        row, rows, col, wide = part_box(part, parts, slab, width)
        box = (pl.ds(pl.multiple_of(row, 16), rows), pl.ds(pl.multiple_of(col, 128), wide))
        return fin_ref.at[(slice(None) if m is None else m,) + box]

    def weight_done(m):
        fin_slot(mine, m)[...] = ffn_sums[m].result()

    forward, at.started = at.started, []
    keep_row = small_ref[10:11, :block]
    b_out, gain_two, b_up, b_down = (vec_ref[i : i + 1, :] for i in range(1, 5))
    halves = xt_ref.shape[2]

    def split_rows(value):
        return value.reshape(shards, halves, slab // halves, block)

    att_t = (att[...].astype(F32) * keep_row).astype(BF16)
    mixed = x_ref[...].astype(F32) + dot(att_t.T, weights[0]) + b_out
    r = lax.rsqrt(jnp.mean(mixed * mixed, axis=-1, keepdims=True) + EPS)
    normed_two = (mixed * r * gain_two).astype(BF16)
    hidden = dot(normed_two, weights[1]) + b_up
    s = 1.0 / (1.0 + jnp.exp(-hidden))
    act = (hidden * s).astype(BF16)
    xt_ref[2] = split_rows(act.T)
    meet_rows(2)
    cot = cot_ref[...].astype(F32)
    g_hidden = dot(cot_ref[...], weights[2], NT) * (s + hidden * s * (1.0 - s))
    low = g_hidden.astype(BF16)
    g_normed = dot(low, weights[1], NT)
    weighted = gain_two * g_normed
    g_mixed = cot + r * weighted - mixed * (r * r * r) * jnp.mean(mixed * weighted, axis=-1, keepdims=True)
    g_low = g_mixed.astype(BF16)
    dctx_ref[...] = (dot(weights[0], g_low, NT).astype(BF16).astype(F32) * keep_row).astype(BF16)
    backward, at.started = at.started, forward
    at.settle()
    at.started = backward
    for i, (da, db) in enumerate(peers):
        dest = at.at(da, db)
        at.send(
            dctx_ref.at[pl.ds(pl.multiple_of(dest * slab, 16), slab), :],
            dctx.at[:, lane(me, block)], d_send.at[i], d_recv.at[me], shard=dest,
        )
    dctx[:, lane(me, block)] = dctx_ref[pl.ds(pl.multiple_of(me * slab, 16), slab), :]
    dy_ref[1] = low
    xt_ref[1] = split_rows(normed_two.T)
    meet_columns(1)
    meet_rows(1)
    gmixed_ref[...] = g_mixed
    dy_ref[0] = g_low
    xt_ref[0] = split_rows(att_t)
    meet_columns(0)
    meet_rows(0)
    out_ref[...] = (mixed + dot(act, weights[2]) + b_down).astype(BF16)
    written = [pltpu.make_async_copy(out_ref, out_hbm, done_sem.at[0])]
    written[0].start()
    row_ref[...] = jnp.zeros_like(row_ref)
    row_ref[1:2, :] = jnp.sum(g_mixed, axis=0, keepdims=True)
    row_ref[2:3, :] = jnp.sum(g_normed * mixed * r, axis=0, keepdims=True)
    row_ref[3:4, :] = jnp.sum(g_hidden, axis=0, keepdims=True)
    row_ref[4:5, :] = jnp.sum(cot, axis=0, keepdims=True)

    def hand_round(ref_slot, send_sem, recv_sem):
        have, rounds, k = [mine], [], 0
        for mask in ((2, 1) if parts == 4 else (1,)):
            sends = []
            for part in have:
                sends.append((part, mask, k))
                k += 1
            fresh = [flipped(part, mask) for part in have]
            rounds.append((sends, fresh))
            have = have + fresh

        def go(n):
            for part, mask, k in rounds[n][0]:
                at.send(ref_slot(part), ref_slot(part), send_sem.at[k], recv_sem.at[part], rep=at.flip(mask))

        def take(n):
            for part in rounds[n][1]:
                at.arrived(ref_slot(part), recv_sem.at[part])

        return go, take, len(rounds)

    gw_go, gw_take, count = hand_round(lambda part: gw_ref.at[part], vr_send, vr_recv)
    fin_hands = [
        hand_round(lambda part, m=m: fin_slot(part, m), r_send.at[m], r_recv.at[m]) for m in range(3)
    ]

    def weight_last(m):
        weight_done(m)
        for n, mask in enumerate(extras):
            here = fin_slot(mine, m)
            at.exchange(here, extra.at[n, m], e_send.at[n, m], e_recv.at[n, m], at.flip(mask))
            here[...] = here[...] + extra[n, m]
        fin_hands[m][0](0)

    base = QUERY_BASE / math.sqrt(HEAD)
    factor = base * soft
    grads[...] = jnp.zeros_like(grads)
    for da, db in peers:
        origin = at.at(-da, -db)
        at.arrived(dctx.at[:, lane(origin, block)], d_recv.at[origin])

    def attend(i):
        reach = (i + 1) * qblock
        span = slice(i * qblock, reach)
        starts = start_ref[0:1, span]
        key_place = lax.broadcasted_iota(jnp.int32, (reach, qblock), 0).astype(F32)
        query_place = (i * qblock + lax.broadcasted_iota(jnp.int32, (1, qblock), 1)).astype(F32)
        allowed = (key_place >= starts) & (key_place <= query_place)
        for h in range(local):
            queries = qkv_ref[h * HEAD : (h + 1) * HEAD, span]
            keys = qkv_ref[slab + h * HEAD : slab + (h + 1) * HEAD, :reach]
            values = qkv_ref[2 * slab + h * HEAD : 2 * slab + (h + 1) * HEAD, :reach]
            gctx = dctx[h * HEAD : (h + 1) * HEAD, span]
            scores = dot(keys, queries, TN)
            probs = jnp.where(allowed, jnp.exp(scores - log_ref[h : h + 1, span]), 0.0)
            gprobs = dot(values, gctx, TN)
            delta = jnp.sum(probs * gprobs, axis=0, keepdims=True)
            gscores = (probs * (gprobs - delta)).astype(BF16)
            low = probs.astype(BF16)
            grads[h * HEAD : (h + 1) * HEAD, span] = dot(keys, gscores)
            kv = slice(slab + h * HEAD, slab + (h + 1) * HEAD)
            grads[kv, :reach] += dot(queries, gscores, NT)
            kv = slice(2 * slab + h * HEAD, 2 * slab + (h + 1) * HEAD)
            grads[kv, :reach] += dot(gctx, low, NT)

    relay_rows(2)
    attend(0)
    weight(2)
    weight_across(2)
    for i in range(1, length // qblock):
        attend(i)

    gscale = jnp.zeros((HEAD, 1), F32)
    for h in range(local):
        rows = slice(h * HEAD, (h + 1) * HEAD)
        scaled = grads[rows, :]
        gscale = gscale + jnp.sum(scaled * query_ref[rows, :], axis=1, keepdims=True)
        grads[rows, :] = scaled * factor
    gscale = gscale * (base / (1.0 + jnp.exp(-column)))
    bias_q = jnp.sum(grads[:slab, :], axis=1, keepdims=True)
    bias_v = jnp.sum(grads[2 * slab :, :], axis=1, keepdims=True)
    tall_rows = grads.shape[0]
    low_t = grads[...].astype(BF16)
    if tall_rows % 128:
        low_t = jnp.concatenate([low_t, jnp.zeros((-tall_rows % 128, length), BF16)], axis=0)
    proj[...] = low_t.T[:, :slab3]

    wcols = wcols_ref[...].reshape(width, slab3)

    def partial(origin, acc):
        tokens = lane(origin, block)
        out = dot(proj[tokens, :], wcols, NT)
        xg[origin] = out.astype(BF16)
        weighted = out * normed_ref[tokens, :].astype(F32)
        return acc + jnp.sum(weighted.reshape(block // 8, 8, width), axis=0)

    def away(i, acc):
        return partial(turn(1 + lax.rem(i, 3)) * minor + lax.rem(at.b + 1 + i // 3, minor), acc)

    gain_rows = jnp.zeros((8, width), F32)
    for db in range(1, minor):
        gain_rows = partial(turn(0) * minor + lax.rem(at.b + db, minor), gain_rows)
    rows_across(0)
    relay_columns(1)
    relay_rows(1)
    gain_rows = lax.fori_loop(0, 3 * (minor - 1), away, gain_rows)
    weight(1)
    weight_across(1)

    rp = width // (shards * parts)
    halves = parts // 2
    whole = dot(normed_ref[...], proj[...], TN)
    gw[...] = whole.reshape(shards, parts, rp, slab3).astype(BF16)
    for k in range(halves):
        at.send(gw.at[:, (1 - core) + 2 * k], gw_core.at[k], vc_send.at[k], vc_recv.at[k], rep=at.flip(1))

    gain_rows = lax.fori_loop(0, MAJOR, lambda i, acc: partial(at.at(i, 0), acc), gain_rows)

    gain_row = jnp.sum(gain_rows, axis=0, keepdims=True) / vec_ref[0:1, :]
    rows = row_ref[...]
    place = lax.broadcasted_iota(jnp.int32, (8, width), 0)
    rows = jnp.where(place == 0, jnp.broadcast_to(gain_row, (8, width)), rows)
    turn_in = jnp.concatenate(
        [jnp.broadcast_to(gscale, (HEAD, 128)), jnp.zeros((128 - HEAD, 128), F32)], axis=0
    )
    scale_row = jnp.broadcast_to(turn_in.T[0:1, :], (8, 128))
    scale_tile = jnp.where(lax.broadcasted_iota(jnp.int32, (8, 128), 0) == 5, scale_row, 0.0)
    for j in range(shards):
        first = min(j * slab // 128 * 128, width - 256)
        windows[j, :, :256] = rows[:, first : first + 256]
        windows[j, :, 256:] = scale_tile
    for i, (da, db) in enumerate(peers):
        dest = at.at(da, db)
        at.send(windows.at[dest], small_land.at[me], s_send.at[i], s_recv.at[me], shard=dest)
    small_land[me] = windows[me]

    weight_summed(2)
    relay_columns(0)
    relay_rows(0)
    weight(0)
    weight_across(0)
    for k in range(halves):
        at.arrived(gw_core.at[k], vc_recv.at[k])
        gw_core[k] = gw[:, core + 2 * k] + gw_core[k]
    km = mine // 2 if parts == 4 else 0
    if parts == 4:
        at.send(gw_core.at[1 - km], gw_y, vy_send.at[0], vy_recv.at[0], rep=at.flip(2))
    rows_summed(0)
    weight_joined(2, 0)
    weight_joined(2, 1)
    weight_joined(2, 3)
    if parts == 4:
        at.arrived(gw_y, vy_recv.at[0])
        gw_sum[...] = gw_core[km] + gw_y[...]
    else:
        gw_sum[...] = gw_core[0]
    for i, (da, db) in enumerate(peers):
        dest = at.at(da, db)
        at.send(gw_sum.at[dest], gw_land.at[me], va_send.at[i], va_recv.at[me], shard=dest)
    gw_land[me] = gw_sum[me]
    rows_across(1)
    rows_across(2)
    rows_last_across()
    weight_summed(1)
    row_sums.joined(0)
    weight_joined(1, 0)
    weight_joined(1, 1)
    weight_joined(1, 3)
    weight_summed(0)
    weight_joined(0, 0)
    weight_joined(0, 1)
    weight_joined(0, 3)
    for da, db in peers:
        origin = at.at(-da, -db)
        at.arrived(gw_land.at[origin], va_recv.at[origin])
    for n, mask in enumerate(extras):
        at.exchange(gw_land, gw_extra.at[n], ve_send.at[n], ve_recv.at[n], at.flip(mask))
        gw_land[...] = gw_land[...] + gw_extra[n]
    for j in range(shards):
        for t in range(3):
            first = t * width + j * slab
            gw_ref[mine, :, first : first + slab] = gw_land[j, :, t * slab : (t + 1) * slab]

    gw_go(0)
    rows_summed(1)
    weight_last(2)
    weight_last(1)
    weight_last(0)
    row_sums.joined(1)
    for n in range(count - 1):
        gw_take(n)
        gw_go(n + 1)


    def write(src, dst, n):
        copy = pltpu.make_async_copy(src, dst, done_sem.at[n])
        copy.start()
        written.append(copy)

    for da, db in peers:
        origin = at.at(-da, -db)
        at.arrived(small_land.at[origin], s_recv.at[origin])
    small = jnp.sum(small_land[...], axis=0)
    lanes = lax.broadcasted_iota(jnp.int32, (slab, 128), 1)
    sides = jnp.concatenate(
        [jnp.where(lanes == 6, bias_q, jnp.where(lanes == 7, bias_v, 0.0)), jnp.zeros((256 - slab, 128), F32)],
        axis=0,
    )
    sides = jnp.concatenate([sides[:128].T[:8], sides[128:].T[:8]], axis=1)
    shift = me * slab - lax.min(me * slab // 128 * 128, width - 256)
    window = pltpu.roll(small[:, :256], lax.rem(256 - shift, 256), 1)
    tall = lax.broadcasted_iota(jnp.int32, (8, 256), 0)
    small_got[0, :, :256] = jnp.where(tall < 5, window, sides)
    small_got[0, :, 256:] = pltpu.roll(small[:, 256:], lax.rem(128 - me * unit, 128), 1)

    def small_round(n):
        at.send(
            small_got.at[2 * n], small_got.at[2 * n + 1], b_send.at[n], b_recv.at[n], rep=at.flip(every[n])
        )

    def small_add(n):
        at.arrived(small_got.at[2 * n + 1], b_recv.at[n])
        small_got[2 * n + 2] = small_got[2 * n] + small_got[2 * n + 1]

    small_round(0)
    rows_summed(2)
    small_add(0)
    small_round(1)
    rows_last()
    gw_take(count - 1)
    write(gw_ref, gw_hbm, 2)
    for n in range(count - 1):
        for m in mats:
            fin_hands[m][1](n)
            fin_hands[m][0](n + 1)
    for n in range(1, len(every)):
        small_add(n)
        if n + 1 < len(every):
            small_round(n + 1)
    small_out_ref[...] = small_got[2 * len(every)]

    total = rows_result()
    x = x_ref[...].astype(F32)
    r = lax.rsqrt(jnp.mean(x * x, axis=-1, keepdims=True) + EPS)
    weighted = vec_ref[0:1, :] * total
    gin_ref[...] = gmixed_ref[...] + r * weighted - x * (r * r * r) * jnp.mean(x * weighted, axis=-1, keepdims=True)


    write(gin_ref, gin_hbm, 3)
    for m in mats:
        fin_hands[m][1](count - 1)
        write(fin_ref.at[m], fin_hbm.at[m], 4 + m)
    at.settle()
    for copy in written:
        copy.wait()


def layer(shards, replicas, inputs, segment_ids, positions, vectors, w_qkv, w_out, w_up, w_down, cotangent):
    block, width = inputs.shape
    slab = width // shards
    slab3 = 3 * slab
    length = shards * block
    wparts = 2 if slab % 32 == 0 else 1
    parts = parts_of(slab)
    halves = parts // 2
    rp = slab // parts
    rows_part = slab // 2 if parts == 4 else slab
    cols = width // 2
    minor = shards // MAJOR
    peers = shards - 1
    bits = (replicas - 1).bit_length()
    more = bits - (parts - 1).bit_length()
    shape = jax.ShapeDtypeStruct
    dma = pltpu.SemaphoreType.DMA
    vm = pltpu.VMEM
    return pl.pallas_call(
        functools.partial(layer_kernel, shards, replicas, wparts, parts, 2 * block),
        out_shape=(
            shape((block, width), BF16),
            shape((3, slab, width), BF16),
            shape((parts, rp, 3 * width), BF16),
            shape((block, width), F32),
            shape((8, 384), F32),
        ),
        in_specs=[VMEM] * 11 + [ANY] * 5,
        out_specs=[ANY] * 4 + [VMEM],
        scratch_shapes=[
            vm((block, width), BF16),
            vm((3, slab, width), BF16),
            vm((parts, rp, 3 * width), BF16),
            vm((block, width), F32),
            vm(w_qkv.shape, BF16),
            vm((block, width), BF16),
            vm((16, 256), F32),
            vm((length, width), BF16),
            vm((slab3, length), BF16),
            vm((slab, length), F32),
            vm((8, length), F32),
            vm((8, width), F32),
            vm((8, length), F32),
            vm((shards, wparts, slab // wparts, slab3), BF16),
            vm((3, shards, halves, slab // halves, block), BF16),
            vm((3, block, width), BF16),
            vm((width, block), BF16),
            vm((8, width), F32),
            vm((block, width), F32),
            vm((shards, block, width), BF16),
            vm((shards, 8, 256), F32),
            vm((shards, wparts, slab // wparts, slab3), BF16),
            vm((slab3, width), BF16),
            vm((slab, length), BF16),
            vm((width, block), BF16),
            vm((3, width, width), BF16),
            vm((slab, length), BF16),
            vm((slab3, length), F32),
            vm((length, slab3), BF16),
            vm((3, shards, rows_part, parts * block), BF16),
            vm((3, parts * block, cols), BF16),
            vm((3, shards, rows_part, block) if parts == 4 else (1, 1, 16, block), BF16),
            vm((3, MAJOR, minor, rows_part, cols), BF16),
            vm((3, minor - 1, MAJOR, rows_part, cols), BF16),
            vm((3, MAJOR + 1, rows_part, cols), BF16),
            vm((max(more, 1), 3, rows_part, cols), BF16),
            vm((shards, parts, rp, slab3), BF16),
            vm((halves, shards, rp, slab3), BF16),
            vm((shards, rp, slab3) if parts == 4 else (1, 16, 128), BF16),
            vm((shards, rp, slab3), BF16),
            vm((shards, rp, slab3), BF16),
            vm((max(more, 1), shards, rp, slab3), BF16),
            vm((shards, 8, 384), F32),
            vm((shards, 8, 384), F32),
            vm((2 * bits + 1, 8, 384), F32),
            dma((2, MAJOR)), dma((MAJOR, minor - 1)), dma((shards,)),
            dma((peers,)), dma((shards,)),
            dma((peers,)), dma((shards, wparts)), dma((shards,)), dma((shards,)),
            dma((2, MAJOR)), dma((MAJOR, minor - 1)), dma((shards, parts)),
            dma((shards,)), dma((shards, 2)),
            dma((5,)), dma((shards,)), dma((shards,)), dma((7,)),
            dma((peers,)), dma((shards,)),
            dma((3, 3)), dma((3, 3)),
            dma((3, 4)), dma((3, 4)),
            dma((3, minor - 1)), dma((3, minor - 1)),
            dma((3, MAJOR)), dma((3, MAJOR + 1)),
            dma((3, parts)), dma((3, parts)),
            dma((max(more, 1), 3)), dma((max(more, 1), 3)),
            dma((minor - 1, MAJOR + 1)), dma((minor - 1, MAJOR + 1)),
            dma((MAJOR + 1,)), dma((MAJOR + 2,)),
            dma((halves,)), dma((halves,)),
            dma((1,)), dma((1,)),
            dma((peers,)), dma((shards,)),
            dma((parts,)), dma((parts,)),
            dma((max(more, 1),)), dma((max(more, 1),)),
            dma((peers,)), dma((shards,)),
            dma((bits,)), dma((bits,)),
        ],
        compiler_params=pltpu.CompilerParams(
            collective_id=0, has_side_effects=True, vmem_limit_bytes=62 << 20
        ),
        name="layer",
    )(inputs, segment_ids, positions, *vectors, w_qkv, w_out, w_up, w_down, cotangent)


def finish_kernel(
    slab, unit, fin_ref, gw_ref, small_ref, gin_ref, out_ref,
    w_out_ref, w_up_ref, w_down_ref, w_qkv_ref, input_ref, output_ref,
    gain_one_ref, b_query_ref, b_value_ref, scale_ref, b_out_ref, gain_two_ref, b_up_ref, b_down_ref,
):
    w_out_ref[...] = fin_ref[0].astype(F32)
    w_up_ref[...] = fin_ref[1].astype(F32)
    w_down_ref[...] = fin_ref[2].astype(F32)
    w_qkv_ref[...] = gw_ref[...].astype(F32)
    input_ref[...] = gin_ref[...]
    output_ref[...] = out_ref[...]

    @pl.when(pl.program_id(0) == 0)
    def _():
        table = {
            0: gain_one_ref, 1: b_out_ref, 2: gain_two_ref, 3: b_up_ref, 4: b_down_ref,
            6: b_query_ref, 7: b_value_ref,
        }
        for row, ref in table.items():
            ref[...] = small_ref[row : row + 1, :slab].reshape(slab)
        scale_ref[...] = small_ref[5:6, 256 : 256 + unit].reshape(unit)


def finish(fin, gw, small, gin, out):
    slab, width = fin.shape[1:]
    block = gin.shape[0]
    steps = 4 if slab % 32 == 0 else 2
    unit = HEAD * slab // width
    part, tokens = slab // steps, block // steps
    shape = jax.ShapeDtypeStruct

    def rows(size, columns):
        return pl.BlockSpec((size, columns), lambda i: (i, 0))

    whole = pl.BlockSpec((8, 384), lambda i: (0, 0))
    vector = pl.BlockSpec((slab,), lambda i: (0,))
    return pl.pallas_call(
        functools.partial(finish_kernel, slab, unit),
        grid=(steps,),
        out_shape=[shape((slab, width), F32)] * 3
        + [shape((slab, 3 * width), F32), shape((block, width), F32), shape((block, width), BF16)]
        + [shape((slab,), F32)] * 3
        + [shape((unit,), F32)]
        + [shape((slab,), F32)] * 4,
        in_specs=[
            pl.BlockSpec((3, part, width), lambda i: (0, i, 0)), rows(part, 3 * width), whole,
            rows(tokens, width), rows(tokens, width),
        ],
        out_specs=[rows(part, width)] * 3
        + [rows(part, 3 * width), rows(tokens, width), rows(tokens, width)]
        + [vector] * 3
        + [pl.BlockSpec((unit,), lambda i: (0,))]
        + [vector] * 4,
        name="finish",
    )(fin, gw, small, gin, out)


def on_device(
    inputs, segment_ids, positions, gain_one, w_qkv, b_query, b_value, query_scale, w_out, b_out,
    gain_two, w_up, b_up, w_down, b_down, cotangent,
):
    shards = lax.axis_size("shard")
    replicas = lax.axis_size("replica")
    block, width = inputs.shape[1:]
    slab = width // shards
    output, fin, gw, input_grad, small = layer(
        shards, replicas, inputs.reshape(block, width), segment_ids, positions,
        (gain_one, b_query, b_value, query_scale, b_out, gain_two, b_up, b_down),
        w_qkv, w_out, w_up, w_down, cotangent.reshape(block, width),
    )
    (
        g_out, g_up, g_down, g_qkv, input_grad, output, g_gain_one, g_b_query, g_b_value, g_scale, g_b_out,
        g_gain_two, g_b_up, g_b_down,
    ) = finish(fin, gw.reshape(slab, 3 * width), small, input_grad, output)
    return (
        output[None], input_grad[None], g_gain_one, g_qkv, g_b_query, g_b_value, g_scale, g_out, g_b_out,
        g_gain_two, g_up, g_b_up, g_down, g_b_down,
    )


def solution(mesh):
    rows = P("replica", "shard", None)
    ids = P("replica", "shard")
    vector = P("shard")
    matrix = P("shard", None)
    in_specs = (
        rows, ids, ids, vector, matrix, vector, vector, vector, matrix, vector, vector, matrix, vector,
        matrix, vector, rows,
    )
    out_specs = (
        rows, rows, vector, matrix, vector, vector, vector, matrix, vector, vector, matrix, vector, matrix,
        vector,
    )
    return jax.shard_map(on_device, mesh=mesh, in_specs=in_specs, out_specs=out_specs, check_vma=False)
```

```python
import functools
import math

import jax
import jax.numpy as jnp
from jax import lax
from jax.experimental import pallas as pl
from jax.experimental.pallas import tpu as pltpu
from jax.sharding import PartitionSpec as P

HEADS = 16
HEAD = 80
EPS = 1e-06
QUERY_BASE = 1.442695041
MASKED = -1000000000.0
MESH = pl.DeviceIdType.MESH
MAJOR = 4
VMEM = pl.BlockSpec(memory_space=pltpu.VMEM)
ANY = pl.BlockSpec(memory_space=pl.ANY)
F32 = jnp.float32
BF16 = jnp.bfloat16
NN = (((1,), (0,)), ((), ()))
NT = (((1,), (1,)), ((), ()))
TN = (((0,), (0,)), ((), ()))


def dot(lhs, rhs, dims=NN):
    return lax.dot_general(lhs, rhs, dims, preferred_element_type=F32)


class Place:
    def __init__(self, shards):
        self.shards = shards
        self.minor = shards // MAJOR
        self.me = lax.axis_index("shard")
        self.rep = lax.axis_index("replica")
        self.a = self.me // self.minor
        self.b = lax.rem(self.me, self.minor)
        self.started = []

    def at(self, da, db):
        a = lax.rem(self.a + da + MAJOR, MAJOR)
        b = lax.rem(self.b + db + self.minor, self.minor)
        return a * self.minor + b

    def peers(self):
        return [(da, db) for da in range(MAJOR) for db in range(self.minor) if da or db]

    def flip(self, mask):
        bit = lax.rem(self.rep // mask, 2)
        return self.rep + mask - 2 * mask * bit

    def greet(self, masks):
        barrier = pltpu.get_barrier_semaphore()
        for da, db in self.peers():
            pl.semaphore_signal(
                barrier, inc=1, device_id=(self.at(da, db), self.rep), device_id_type=MESH
            )
        for mask in masks:
            pl.semaphore_signal(
                barrier, inc=1, device_id=(self.me, self.flip(mask)), device_id_type=MESH
            )
        pl.semaphore_wait(barrier, len(self.peers()) + len(masks))

    def send(self, src, dst, ssem, rsem, shard=None, rep=None, when=None):
        copy = pltpu.make_async_remote_copy(
            src_ref=src,
            dst_ref=dst,
            send_sem=ssem,
            recv_sem=rsem,
            device_id=(self.me if shard is None else shard, self.rep if rep is None else rep),
            device_id_type=MESH,
        )
        if when is None:
            copy.start()
        else:
            @pl.when(when)
            def _():
                copy.start()
        self.started.append((when, copy))

    def arrived(self, dst, rsem):
        pltpu.make_async_remote_copy(
            src_ref=dst,
            dst_ref=dst,
            send_sem=rsem,
            recv_sem=rsem,
            device_id=(self.me, self.rep),
            device_id_type=MESH,
        ).wait_recv()

    def exchange(self, src, dst, ssem, rsem, rep):
        self.send(src, dst, ssem, rsem, rep=rep)
        self.arrived(dst, rsem)
        self.started.pop()[1].wait_send()

    def settle(self):
        for when, copy in self.started:
            if when is None:
                copy.wait_send()
            else:
                @pl.when(when)
                def _():
                    copy.wait_send()
        self.started = []


class Line:
    def __init__(self, at, slot, major_send, minor_send, recv):
        self.at, self.slot = at, slot
        self.major_send, self.minor_send, self.recv = major_send, minor_send, recv

    def onward(self, origin, up, down, d):
        at = self.at
        if up is not None:
            at.send(
                self.slot(origin), self.slot(origin), self.major_send.at[0, d], self.recv(origin),
                shard=lax.min(at.a + 1, MAJOR - 1) * at.minor + at.b, when=up,
            )
        if down is not None:
            at.send(
                self.slot(origin), self.slot(origin), self.major_send.at[1, d], self.recv(origin),
                shard=lax.max(at.a - 1, 0) * at.minor + at.b, when=down,
            )

    def across(self, origin, when=None):
        at = self.at
        for db in range(1, at.minor):
            at.send(
                self.slot(origin), self.slot(origin), self.minor_send.at[origin // at.minor, db - 1],
                self.recv(origin), shard=at.at(0, db), when=when,
            )

    def along_own(self):
        at = self.at
        self.onward(at.me, at.a + 1 < MAJOR, at.a > 0, 0)

    def sides(self, d):
        at = self.at
        for side in (-1, 1):
            ok = (at.a - d >= 0) if side < 0 else (at.a + d < MAJOR)
            origin = lax.max(at.a - d, 0) if side < 0 else lax.min(at.a + d, MAJOR - 1)
            yield side, ok, origin * at.minor + at.b

    def take(self, d, then=None):
        for side, ok, origin in self.sides(d):
            @pl.when(ok)
            def _():
                self.at.arrived(self.slot(origin), self.recv(origin))

            if then is not None:
                then(origin, ok)

    def along(self, d):
        at = self.at
        if d + 1 < MAJOR:
            for side, ok, origin in self.sides(d):
                if side < 0:
                    self.onward(origin, ok & (at.a + 1 < MAJOR), None, d)
                else:
                    self.onward(origin, None, ok & (at.a > 0), d)

    def aside(self, d):
        for side, ok, origin in self.sides(d):
            self.across(origin, when=ok)

    def step(self, d, then=None):
        self.take(d, then)
        self.along(d)
        self.aside(d)


def parts_of(rows):
    return 4 if rows % 32 == 0 else 2


def part_box(part, parts, rows, cols):
    if parts == 4:
        i, j, rows = lax.rem(part, 2), part // 2, rows // 2
    else:
        i, j = 0, part
    return i * rows, rows, j * (cols // 2), cols // 2


def flipped(part, mask):
    bit = lax.rem(part // mask, 2)
    return part + mask - 2 * mask * bit


def layer_kernel(
    shards, replicas, wparts, parts, qblock,
    x_ref, segment_ref, position_ref, gain_one_ref, b_query_ref, b_value_ref, scale_ref,
    b_out_ref, gain_two_ref, b_up_ref, b_down_ref, w_hbm, wout_ref, wup_ref, wdown_ref, cot_hbm,
    out_hbm, fin_hbm, gw_hbm, gin_hbm, small_out_ref,
    out_ref, fin_ref, gw_ref, gin_ref, w_ref, cot_ref, small_ref,
    normed_ref, qkv_ref, query_ref, log_ref, vec_ref, start_ref, wcols_ref,
    xt_ref, dy_ref, dctx_ref, row_ref, gmixed_ref,
    xg, packets, pieces, turned, context, att, weights,
    dctx, grads, proj, left, right, stash, sums, from_x, from_z, extra,
    gw, gw_core, gw_y, gw_sum, gw_land, gw_extra,
    windows, small_land, small_got,
    xm_send, xn_send, x_recv, p_send, p_recv, w_send, w_recv, wc_send, wy_send,
    fm_send, fn_send, f_recv, fy_send, fc_send, local_sem, a_send, a_recv, done_sem,
    d_send, d_recv, gy_send, gy_recv, gc_send, gc_recv, gx_send, gx_recv, gz_send, gz_recv,
    r_send, r_recv, e_send, e_recv, nx_send, nx_recv, nz_send, nz_recv,
    vc_send, vc_recv, vy_send, vy_recv, va_send, va_recv, vr_send, vr_recv, ve_send, ve_recv,
    s_send, s_recv, b_send, b_recv,
):
    at = Place(shards)
    me, minor = at.me, at.minor
    block, width = x_ref.shape
    length = shards * block
    slab = width // shards
    slab3 = 3 * slab
    local = slab // HEAD
    peers = at.peers()
    masks = (2, 1) if parts == 4 else (1,)
    every = []
    bit = 1
    while bit < replicas:
        every.append(bit)
        bit *= 2
    extras = [m for m in every if m >= parts]
    mine = lax.rem(at.rep, parts)
    wpart = lax.rem(at.rep, wparts)

    loads = []
    for m, ref in enumerate((wout_ref, wup_ref, wdown_ref)):
        copy = pltpu.make_async_copy(
            ref, weights.at[m, pl.ds(pl.multiple_of(me * slab, 16), slab), :], local_sem.at[m]
        )
        copy.start()
        loads.append(copy)
    w_load = pltpu.make_async_copy(w_hbm, w_ref, local_sem.at[3])
    w_load.start()
    cot_load = pltpu.make_async_copy(cot_hbm, cot_ref, local_sem.at[4])
    cot_load.start()
    xg[me] = x_ref[...]
    small_ref[...] = jnp.zeros_like(small_ref)
    table = {
        0: gain_one_ref, 1: b_out_ref, 2: gain_two_ref, 3: b_up_ref, 4: b_down_ref, 5: scale_ref,
        8: b_query_ref, 9: b_value_ref,
    }
    for row, ref in table.items():
        size = ref.shape[0]
        small_ref[row : row + 1, :size] = ref[...].astype(F32).reshape(1, size)
    place = me * block + lax.broadcasted_iota(jnp.int32, (1, block), 1)
    small_ref[6:7, :block] = (place - position_ref[...]).astype(F32)
    small_ref[10:11, :block] = (segment_ref[...] != 0).astype(F32)
    packets[me] = small_ref[:8]
    at.greet(tuple(every))

    def wslot(origin, part):
        row, rows, col, cols = part_box(part, parts, slab, width)
        return weights.at[
            :,
            pl.ds(pl.multiple_of(origin * slab + row, 16), rows),
            pl.ds(pl.multiple_of(col, 128), cols),
        ]

    rows_line = Line(at, lambda o: xg.at[o], xm_send, xn_send, lambda o: x_recv.at[o])
    ffn_line = Line(
        at, lambda o: wslot(o, mine), fm_send, fn_send, lambda o: f_recv.at[o, mine]
    )

    def to_replicas(origin, when=None):
        slot = wslot(origin, mine)
        for mask in masks:
            sem = fy_send.at[origin] if mask == 2 else fc_send.at[origin, 0]
            at.send(slot, slot, sem, f_recv.at[origin, mine], rep=at.flip(mask), when=when)

    cols = width // 2
    core = lax.rem(at.rep, 2)
    i_part = lax.rem(mine, 2) if parts == 4 else 0
    j_part = mine // 2 if parts == 4 else mine
    mats = (2, 1, 0)

    def lane(n, size):
        return pl.ds(pl.multiple_of(n * size, 128), size)

    def seat(n):
        return slice(n * block, (n + 1) * block)

    near = parts // 2

    def meet_columns(m):
        if parts == 4:
            at.send(
                dy_ref.at[m, :, lane(1 - j_part, cols)], right.at[m, seat(1), :],
                gy_send.at[m, 1], gy_recv.at[m, 1], rep=at.flip(2),
            )
        at.send(
            dy_ref.at[m, :, lane(j_part if parts == 4 else 1 - j_part, cols)], right.at[m, seat(near), :],
            gc_send.at[m, 1], gc_recv.at[m, 1], rep=at.flip(1),
        )
        right[m, seat(0), :] = dy_ref[m, :, lane(j_part, cols)]

    def meet_rows(m):
        if parts == 4:
            far = at.flip(2)
            at.send(xt_ref.at[m, :, 1 - i_part], stash.at[m], gy_send.at[m, 2], gy_recv.at[m, 2], rep=far)
            at.send(
                xt_ref.at[m, :, i_part], left.at[m, :, :, seat(1)], gy_send.at[m, 0], gy_recv.at[m, 0], rep=far
            )
        at.send(
            xt_ref.at[m, :, 1 - i_part if parts == 4 else 0], left.at[m, :, :, seat(near)],
            gc_send.at[m, 0], gc_recv.at[m, 0], rep=at.flip(1),
        )
        left[m, :, :, seat(0)] = xt_ref[m, :, i_part]

    def relay_columns(m):
        if parts == 4:
            at.arrived(right.at[m, seat(1), :], gy_recv.at[m, 1])
            at.send(
                right.at[m, seat(1), :], right.at[m, seat(3), :], gc_send.at[m, 3], gc_recv.at[m, 3], rep=at.flip(1)
            )

    def relay_rows(m):
        if parts == 4:
            at.arrived(stash.at[m], gy_recv.at[m, 2])
            at.send(stash.at[m], left.at[m, :, :, seat(3)], gc_send.at[m, 2], gc_recv.at[m, 2], rep=at.flip(1))

    for i, (da, db) in enumerate(peers):
        at.send(packets.at[me], packets.at[me], p_send.at[i], p_recv.at[me], shard=at.at(da, db))
    rows_line.along_own()
    for copy in loads:
        copy.wait()
    ffn_line.across(me)
    rows_line.across(me)
    cot_load.wait()
    dy_ref[2] = cot_ref[...]
    meet_columns(2)
    w_load.wait()
    cut = slab // wparts
    for j in range(shards):
        for t in range(3):
            first = t * width + j * slab
            pieces[j, :, :, t * slab : (t + 1) * slab] = w_ref[:, first : first + slab].reshape(
                wparts, cut, slab
            )
    parity = lax.rem(at.a + mine // 2, 2)
    chosen = parity == 0 if parts == 4 else None
    for i, (da, db) in enumerate(peers):
        dest = at.at(da, db)
        at.send(
            pieces.at[dest, wpart], wcols_ref.at[me, wpart], w_send.at[i], w_recv.at[me, wpart], shard=dest,
            when=chosen,
        )
    wcols_ref[me] = pieces[me]
    ffn_line.along_own()

    def ffn_minor(distance):
        for db in range(1, minor):
            sides = ((-1, 1) if distance else (0,))
            for side in sides:
                a = at.a + side * distance
                ok = None
                if distance:
                    ok = (a >= 0) & (a < MAJOR)
                origin = lax.max(lax.min(a, MAJOR - 1), 0) * minor + lax.rem(at.b + db, minor)
                slot = wslot(origin, mine)
                if ok is None:
                    at.arrived(slot, f_recv.at[origin, mine])
                else:
                    @pl.when(ok)
                    def _():
                        at.arrived(slot, f_recv.at[origin, mine])
                to_replicas(origin, ok)

    def columns(phase):
        for q in range(2):
            for db in range(minor):
                da = lax.rem(parity + phase, 2) + 2 * q
                origin = at.at(-da, -db)
                slot = wcols_ref.at[origin, wpart]
                real = origin != me

                @pl.when(real)
                def _():
                    at.arrived(slot, w_recv.at[origin, wpart])

                if parts == 4 and phase == 0:
                    at.send(
                        slot, slot, wy_send.at[origin], w_recv.at[origin, wpart], rep=at.flip(2), when=real
                    )
                if wparts == 2:
                    at.send(
                        slot, slot, wc_send.at[origin], w_recv.at[origin, wpart], rep=at.flip(1), when=real
                    )

    ffn_minor(0)
    rows_line.step(1)
    ffn_line.step(1, to_replicas)
    rows_line.step(2)
    columns(0)

    for da, db in peers:
        origin = at.at(-da, -db)
        at.arrived(packets.at[origin], p_recv.at[origin])
    vectors = jnp.zeros((8, width), F32)
    scales = jnp.zeros((1, 128), F32)
    lanes = lax.broadcasted_iota(jnp.int32, (8, width), 1)
    unit = HEAD // shards
    for j in range(shards):
        piece = packets[j]
        wide = jnp.concatenate([piece, jnp.zeros((8, width - piece.shape[1]), F32)], axis=1)
        wide = jnp.where(lanes < slab, wide, 0.0)
        vectors = vectors + (pltpu.roll(wide, j * slab, 1) if j else wide)
        scale = jnp.where(lanes[0:1, :128] < unit, piece[5:6, :128], 0.0)
        scales = scales + (pltpu.roll(scale, j * unit, 1) if j else scale)
        start_ref[:, j * block : (j + 1) * block] = jnp.broadcast_to(piece[6:7, :block], (8, block))
    rows = lax.broadcasted_iota(jnp.int32, (8, width), 0)
    vec_ref[...] = jnp.where(rows < 5, vectors, 0.0)
    vec_ref[5:6, :128] = scales
    gain = vec_ref[0:1, :]
    column = jnp.broadcast_to(scales, (128, 128)).T[:HEAD, 0:1]
    soft = jnp.maximum(column, 0.0) + jnp.log(1.0 + jnp.exp(-jnp.abs(column)))
    factor = jnp.concatenate([QUERY_BASE / math.sqrt(HEAD) * soft] * local, axis=0)
    own = small_ref[8:16, :]
    tall = jnp.concatenate([own, jnp.zeros((120, 256), F32)], axis=0)
    tall = jnp.concatenate([tall[:, :128].T, tall[:, 128:].T], axis=0)
    bias_query = tall[:slab, 0:1]
    bias_value = tall[:slab, 1:2]

    ffn_line.step(2, to_replicas)
    ffn_minor(1)
    rows_line.step(3)
    columns(1)
    relay_columns(2)
    if wparts == 2:
        for da, db in peers:
            origin = at.at(-da, -db)
            last = wparts - 1 - wpart
            at.arrived(wcols_ref.at[origin, last], w_recv.at[origin, last])
    turned[...] = wcols_ref[...].reshape(width, slab3).T

    def project(origin):
        rows_in = xg[origin].astype(F32)
        scale = lax.rsqrt(jnp.mean(rows_in * rows_in, axis=-1, keepdims=True) + EPS)
        normed = (rows_in * scale * gain).astype(BF16)
        tokens = pl.ds(pl.multiple_of(origin * block, block), block)
        normed_ref[tokens, :] = normed
        out = dot(turned[...], normed, NT)
        query = out[:slab] + bias_query
        query_ref[:, tokens] = query
        qkv_ref[:slab, tokens] = (query * factor).astype(BF16)
        qkv_ref[slab : 2 * slab, tokens] = out[slab : 2 * slab].astype(BF16)
        qkv_ref[2 * slab :, tokens] = (out[2 * slab :] + bias_value).astype(BF16)

    ffn_line.step(3, to_replicas)

    def project_major(i, carry):
        project(at.at(i, 0))
        return carry

    def project_minor(i, carry):
        origin = at.at(lax.rem(i, MAJOR), 1 + i // MAJOR)
        at.arrived(xg.at[origin], x_recv.at[origin])
        project(origin)
        return carry

    lax.fori_loop(0, MAJOR, project_major, 0)
    ffn_minor(2)
    lax.fori_loop(0, shards - MAJOR, project_minor, 0)
    ffn_minor(3)

    log_ref[...] = jnp.zeros_like(log_ref)
    for i in range(length // qblock):
        reach = (i + 1) * qblock
        span = slice(i * qblock, reach)
        starts = start_ref[0:1, span]
        key_place = lax.broadcasted_iota(jnp.int32, (reach, qblock), 0).astype(F32)
        query_place = (i * qblock + lax.broadcasted_iota(jnp.int32, (1, qblock), 1)).astype(F32)
        allowed = (key_place >= starts) & (key_place <= query_place)
        for h in range(local):
            head = slice(h * HEAD, (h + 1) * HEAD)
            queries = qkv_ref[h * HEAD : (h + 1) * HEAD, span]
            keys = qkv_ref[slab + h * HEAD : slab + (h + 1) * HEAD, :reach]
            values = qkv_ref[2 * slab + h * HEAD : 2 * slab + (h + 1) * HEAD, :reach]
            scores = jnp.where(allowed, dot(keys, queries, TN), MASKED)
            top = jnp.max(scores, axis=0, keepdims=True)
            powers = jnp.exp(scores - top)
            total = jnp.sum(powers, axis=0, keepdims=True)
            probs = (powers * (1.0 / total)).astype(BF16)
            log_ref[h : h + 1, span] = top + jnp.log(total)
            context[head, span] = dot(values, probs).astype(BF16)
        heads = pl.ds(pl.multiple_of(me * slab, 16), slab)
        for j in range(i * qblock // block, reach // block):
            piece = slice(j * block, (j + 1) * block)
            at.send(context.at[:, piece], att.at[heads, :], a_send.at[j], a_recv.at[me], shard=j, when=me != j)

            @pl.when(me == j)
            def _():
                att[heads, :] = context[:, piece]

    order = [(0, db) for db in range(1, minor)]
    order += [(da, db) for da in range(1, MAJOR) for db in range(minor)]
    if parts == 4:
        for da, db in order:
            origin = at.at(da, db)
            part = flipped(mine, 2)
            slot = wslot(origin, part)
            at.arrived(slot, f_recv.at[origin, part])
            at.send(slot, slot, fc_send.at[origin, 1], f_recv.at[origin, part], rep=at.flip(1))
    for da, db in peers:
        origin = at.at(-da, -db)
        at.arrived(att.at[pl.ds(pl.multiple_of(origin * slab, 16), slab), :], a_recv.at[origin])
    others = [flipped(mine, 1)] + ([flipped(flipped(mine, 1), 2)] if parts == 4 else [])
    for da, db in order:
        origin = at.at(da, db)
        for part in others:
            at.arrived(wslot(origin, part), f_recv.at[origin, part])

    def weight(m):
        at.arrived(left.at[m, :, :, seat(near)], gc_recv.at[m, 0])
        at.arrived(right.at[m, seat(near), :], gc_recv.at[m, 1])
        if parts == 4:
            at.arrived(left.at[m, :, :, seat(1)], gy_recv.at[m, 0])
            at.arrived(left.at[m, :, :, seat(3)], gc_recv.at[m, 2])
            at.arrived(right.at[m, seat(3), :], gc_recv.at[m, 3])
        rows = left.shape[1] * left.shape[2]
        out = dot(left[m].reshape(rows, parts * block), right[m])
        sums[m] = out.reshape(sums.shape[1:]).astype(BF16)

    def weight_across(m):
        for db in range(1, minor):
            at.send(
                sums.at[m, :, lax.rem(at.b + db, minor)], from_x.at[m, db - 1],
                gx_send.at[m, db - 1], gx_recv.at[m, db - 1], shard=at.at(0, db),
            )

    ahead = jnp.where(at.a < MAJOR // 2, 1, -1)
    middle = (at.a > 0) & (at.a < MAJOR - 1)

    def turn(n):
        return jnp.where(at.a < MAJOR // 2, MAJOR - 1 - n, n)

    class Chain:
        def __init__(self, own, land, ssem, rsem):
            self.own, self.land, self.ssem, self.rsem = own, land, ssem, rsem

        def go(self, n, when=None):
            t = turn(n)
            way = -ahead if n == 3 else ahead
            to = lax.max(lax.min(at.a + way, MAJOR - 1), 0) * minor + at.b
            dst = jnp.where(middle, MAJOR, t) if n == 1 else t
            at.send(self.own(t), self.land(dst), self.ssem.at[n], self.rsem.at[dst], shard=to, when=when)

        def summed(self, n):
            if n < 3:
                self.go(n, jnp.logical_not(middle))

        def joined(self, n):
            t = turn(n)

            @pl.when(middle)
            def _():
                at.arrived(self.land(t), self.rsem.at[t])
                self.own(t)[...] = self.own(t)[...] + self.land(t)[...]

            self.go(n, middle)

        def result(self):
            at.arrived(self.land(at.a), self.rsem.at[at.a])
            total = self.own(at.a)[...].astype(F32) + self.land(at.a)[...].astype(F32)
            self.own(at.a)[...] = total.astype(BF16)

            @pl.when(middle)
            def _():
                at.arrived(self.land(MAJOR), self.rsem.at[MAJOR])
                self.own(at.a)[...] = (total + self.land(MAJOR)[...].astype(F32)).astype(BF16)

            return self.own(at.a)[...]

    ffn_sums = {
        m: Chain(
            lambda t, m=m: sums.at[m, t, at.b], lambda n, m=m: from_z.at[m, n], gz_send.at[m], gz_recv.at[m]
        )
        for m in mats
    }

    def land_x(db, t):
        first = (db - 1) // 2 * MAJOR + t
        return weights.at[(db - 1) % 2, pl.ds(pl.multiple_of(first * block, block), block), :]

    def land_z(n):
        return weights.at[1, pl.ds(pl.multiple_of((MAJOR + n) * block, block), block), :]

    row_sums = Chain(lambda t: xg.at[t * minor + at.b], land_z, nz_send, nz_recv)

    def rows_across(n):
        t = turn(n)
        for db in range(1, minor):
            to = t * minor + lax.rem(at.b + db, minor)
            at.send(
                xg.at[to], land_x(db, t), nx_send.at[db - 1, n], nx_recv.at[db - 1, t], shard=at.at(0, db)
            )

    def rows_summed(n):
        t = turn(n)
        own = row_sums.own(t)
        total = own[...].astype(F32)
        for db in range(1, minor):
            at.arrived(land_x(db, t), nx_recv.at[db - 1, t])
            total = total + land_x(db, t)[...].astype(F32)
        own[...] = total.astype(BF16)
        row_sums.summed(n)

    def weight_summed(m):
        for db in range(1, minor):
            at.arrived(from_x.at[m, db - 1], gx_recv.at[m, db - 1])
        for n in range(MAJOR):
            t = turn(n)
            total = sums[m, t, at.b].astype(F32)
            for db in range(1, minor):
                total = total + from_x[m, db - 1, t].astype(F32)
            sums[m, t, at.b] = total.astype(BF16)
            ffn_sums[m].summed(n)

    def weight_joined(m, n):
        ffn_sums[m].joined(n)

    def rows_last_across():
        t = turn(3)
        for n in range(2):
            half = pl.ds(n * cols, cols)
            for db in range(1, minor):
                to = t * minor + lax.rem(at.b + db, minor)
                at.send(
                    xg.at[to, :, half], land_x(db, t).at[:, half], nx_send.at[db - 1, 3 + n],
                    nx_recv.at[db - 1, MAJOR if n else t], shard=at.at(0, db),
                )

    def rows_last():
        t = turn(3)
        own = row_sums.own(t)
        to = lax.max(lax.min(at.a - ahead, MAJOR - 1), 0) * minor + at.b
        for n in range(2):
            half = pl.ds(n * cols, cols)
            total = own[:, half].astype(F32)
            for db in range(1, minor):
                piece = land_x(db, t).at[:, half]
                at.arrived(piece, nx_recv.at[db - 1, MAJOR if n else t])
                total = total + piece[...].astype(F32)
            own[:, half] = total.astype(BF16)

            @pl.when(middle)
            def _():
                if n == 0:
                    at.arrived(land_z(t), nz_recv.at[t])
                own[:, half] = own[:, half] + land_z(t)[:, half]

            at.send(
                own.at[:, half], land_z(t).at[:, half], nz_send.at[3 + n],
                nz_recv.at[MAJOR + 1 if n else t], shard=to, when=middle,
            )

    def rows_result():
        own = row_sums.own(at.a)
        mine_z = land_z(at.a)

        @pl.when(middle)
        def _():
            at.arrived(mine_z, nz_recv.at[at.a])
            at.arrived(land_z(MAJOR), nz_recv.at[MAJOR])
            first = own[...].astype(F32) + mine_z[...].astype(F32)
            gin_ref[...] = first + land_z(MAJOR)[...].astype(F32)

        @pl.when(jnp.logical_not(middle))
        def _():
            at.arrived(mine_z.at[:, :cols], nz_recv.at[at.a])
            at.arrived(mine_z.at[:, cols:], nz_recv.at[MAJOR + 1])
            gin_ref[...] = own[...].astype(F32) + mine_z[...].astype(F32)

        return gin_ref[...]

    def fin_slot(part, m=None):
        row, rows, col, wide = part_box(part, parts, slab, width)
        box = (pl.ds(pl.multiple_of(row, 16), rows), pl.ds(pl.multiple_of(col, 128), wide))
        return fin_ref.at[(slice(None) if m is None else m,) + box]

    def weight_done(m):
        fin_slot(mine, m)[...] = ffn_sums[m].result()

    forward, at.started = at.started, []
    keep_row = small_ref[10:11, :block]
    b_out, gain_two, b_up, b_down = (vec_ref[i : i + 1, :] for i in range(1, 5))
    halves = xt_ref.shape[2]

    def split_rows(value):
        return value.reshape(shards, halves, slab // halves, block)

    att_t = (att[...].astype(F32) * keep_row).astype(BF16)
    mixed = x_ref[...].astype(F32) + dot(att_t.T, weights[0]) + b_out
    r = lax.rsqrt(jnp.mean(mixed * mixed, axis=-1, keepdims=True) + EPS)
    normed_two = (mixed * r * gain_two).astype(BF16)
    hidden = dot(normed_two, weights[1]) + b_up
    s = 1.0 / (1.0 + jnp.exp(-hidden))
    act = (hidden * s).astype(BF16)
    xt_ref[2] = split_rows(act.T)
    meet_rows(2)
    cot = cot_ref[...].astype(F32)
    g_hidden = dot(cot_ref[...], weights[2], NT) * (s + hidden * s * (1.0 - s))
    low = g_hidden.astype(BF16)
    g_normed = dot(low, weights[1], NT)
    weighted = gain_two * g_normed
    g_mixed = cot + r * weighted - mixed * (r * r * r) * jnp.mean(mixed * weighted, axis=-1, keepdims=True)
    g_low = g_mixed.astype(BF16)
    dctx_ref[...] = (dot(weights[0], g_low, NT).astype(BF16).astype(F32) * keep_row).astype(BF16)
    backward, at.started = at.started, forward
    at.settle()
    at.started = backward
    for i, (da, db) in enumerate(peers):
        dest = at.at(da, db)
        at.send(
            dctx_ref.at[pl.ds(pl.multiple_of(dest * slab, 16), slab), :],
            dctx.at[:, lane(me, block)], d_send.at[i], d_recv.at[me], shard=dest,
        )
    dctx[:, lane(me, block)] = dctx_ref[pl.ds(pl.multiple_of(me * slab, 16), slab), :]
    dy_ref[1] = low
    xt_ref[1] = split_rows(normed_two.T)
    meet_columns(1)
    meet_rows(1)
    gmixed_ref[...] = g_mixed
    dy_ref[0] = g_low
    xt_ref[0] = split_rows(att_t)
    meet_columns(0)
    meet_rows(0)
    out_ref[...] = (mixed + dot(act, weights[2]) + b_down).astype(BF16)
    written = [pltpu.make_async_copy(out_ref, out_hbm, done_sem.at[0])]
    written[0].start()
    row_ref[...] = jnp.zeros_like(row_ref)
    row_ref[1:2, :] = jnp.sum(g_mixed, axis=0, keepdims=True)
    row_ref[2:3, :] = jnp.sum(g_normed * mixed * r, axis=0, keepdims=True)
    row_ref[3:4, :] = jnp.sum(g_hidden, axis=0, keepdims=True)
    row_ref[4:5, :] = jnp.sum(cot, axis=0, keepdims=True)

    def hand_round(ref_slot, send_sem, recv_sem):
        have, rounds, k = [mine], [], 0
        for mask in ((2, 1) if parts == 4 else (1,)):
            sends = []
            for part in have:
                sends.append((part, mask, k))
                k += 1
            fresh = [flipped(part, mask) for part in have]
            rounds.append((sends, fresh))
            have = have + fresh

        def go(n):
            for part, mask, k in rounds[n][0]:
                at.send(ref_slot(part), ref_slot(part), send_sem.at[k], recv_sem.at[part], rep=at.flip(mask))

        def take(n):
            for part in rounds[n][1]:
                at.arrived(ref_slot(part), recv_sem.at[part])

        return go, take, len(rounds)

    gw_go, gw_take, count = hand_round(lambda part: gw_ref.at[part], vr_send, vr_recv)
    fin_hands = [
        hand_round(lambda part, m=m: fin_slot(part, m), r_send.at[m], r_recv.at[m]) for m in range(3)
    ]

    def weight_last(m):
        weight_done(m)
        for n, mask in enumerate(extras):
            here = fin_slot(mine, m)
            at.exchange(here, extra.at[n, m], e_send.at[n, m], e_recv.at[n, m], at.flip(mask))
            here[...] = here[...] + extra[n, m]
        fin_hands[m][0](0)

    base = QUERY_BASE / math.sqrt(HEAD)
    factor = base * soft
    grads[...] = jnp.zeros_like(grads)
    for da, db in peers:
        origin = at.at(-da, -db)
        at.arrived(dctx.at[:, lane(origin, block)], d_recv.at[origin])

    def attend(i):
        reach = (i + 1) * qblock
        span = slice(i * qblock, reach)
        starts = start_ref[0:1, span]
        key_place = lax.broadcasted_iota(jnp.int32, (reach, qblock), 0).astype(F32)
        query_place = (i * qblock + lax.broadcasted_iota(jnp.int32, (1, qblock), 1)).astype(F32)
        allowed = (key_place >= starts) & (key_place <= query_place)
        for h in range(local):
            queries = qkv_ref[h * HEAD : (h + 1) * HEAD, span]
            keys = qkv_ref[slab + h * HEAD : slab + (h + 1) * HEAD, :reach]
            values = qkv_ref[2 * slab + h * HEAD : 2 * slab + (h + 1) * HEAD, :reach]
            gctx = dctx[h * HEAD : (h + 1) * HEAD, span]
            scores = dot(keys, queries, TN)
            probs = jnp.where(allowed, jnp.exp(scores - log_ref[h : h + 1, span]), 0.0)
            gprobs = dot(values, gctx, TN)
            delta = jnp.sum(probs * gprobs, axis=0, keepdims=True)
            gscores = (probs * (gprobs - delta)).astype(BF16)
            low = probs.astype(BF16)
            grads[h * HEAD : (h + 1) * HEAD, span] = dot(keys, gscores)
            kv = slice(slab + h * HEAD, slab + (h + 1) * HEAD)
            grads[kv, :reach] += dot(queries, gscores, NT)
            kv = slice(2 * slab + h * HEAD, 2 * slab + (h + 1) * HEAD)
            grads[kv, :reach] += dot(gctx, low, NT)

    relay_rows(2)
    attend(0)
    weight(2)
    weight_across(2)
    for i in range(1, length // qblock):
        attend(i)

    gscale = jnp.zeros((HEAD, 1), F32)
    for h in range(local):
        rows = slice(h * HEAD, (h + 1) * HEAD)
        scaled = grads[rows, :]
        gscale = gscale + jnp.sum(scaled * query_ref[rows, :], axis=1, keepdims=True)
        grads[rows, :] = scaled * factor
    gscale = gscale * (base / (1.0 + jnp.exp(-column)))
    bias_q = jnp.sum(grads[:slab, :], axis=1, keepdims=True)
    bias_v = jnp.sum(grads[2 * slab :, :], axis=1, keepdims=True)
    tall_rows = grads.shape[0]
    low_t = grads[...].astype(BF16)
    if tall_rows % 128:
        low_t = jnp.concatenate([low_t, jnp.zeros((-tall_rows % 128, length), BF16)], axis=0)
    proj[...] = low_t.T[:, :slab3]

    wcols = wcols_ref[...].reshape(width, slab3)

    def partial(origin, acc):
        tokens = lane(origin, block)
        out = dot(proj[tokens, :], wcols, NT)
        xg[origin] = out.astype(BF16)
        weighted = out * normed_ref[tokens, :].astype(F32)
        return acc + jnp.sum(weighted.reshape(block // 8, 8, width), axis=0)

    def away(i, acc):
        return partial(turn(1 + lax.rem(i, 3)) * minor + lax.rem(at.b + 1 + i // 3, minor), acc)

    gain_rows = jnp.zeros((8, width), F32)
    for db in range(1, minor):
        gain_rows = partial(turn(0) * minor + lax.rem(at.b + db, minor), gain_rows)
    rows_across(0)
    relay_columns(1)
    relay_rows(1)
    gain_rows = lax.fori_loop(0, 3 * (minor - 1), away, gain_rows)
    weight(1)
    weight_across(1)

    rp = width // (shards * parts)
    halves = parts // 2
    whole = dot(normed_ref[...], proj[...], TN)
    gw[...] = whole.reshape(shards, parts, rp, slab3).astype(BF16)
    for k in range(halves):
        at.send(gw.at[:, (1 - core) + 2 * k], gw_core.at[k], vc_send.at[k], vc_recv.at[k], rep=at.flip(1))

    gain_rows = lax.fori_loop(0, MAJOR, lambda i, acc: partial(at.at(i, 0), acc), gain_rows)

    gain_row = jnp.sum(gain_rows, axis=0, keepdims=True) / vec_ref[0:1, :]
    rows = row_ref[...]
    place = lax.broadcasted_iota(jnp.int32, (8, width), 0)
    rows = jnp.where(place == 0, jnp.broadcast_to(gain_row, (8, width)), rows)
    turn_in = jnp.concatenate(
        [jnp.broadcast_to(gscale, (HEAD, 128)), jnp.zeros((128 - HEAD, 128), F32)], axis=0
    )
    scale_row = jnp.broadcast_to(turn_in.T[0:1, :], (8, 128))
    scale_tile = jnp.where(lax.broadcasted_iota(jnp.int32, (8, 128), 0) == 5, scale_row, 0.0)
    for j in range(shards):
        first = min(j * slab // 128 * 128, width - 256)
        windows[j, :, :256] = rows[:, first : first + 256]
        windows[j, :, 256:] = scale_tile
    for i, (da, db) in enumerate(peers):
        dest = at.at(da, db)
        at.send(windows.at[dest], small_land.at[me], s_send.at[i], s_recv.at[me], shard=dest)
    small_land[me] = windows[me]

    weight_summed(2)
    relay_columns(0)
    relay_rows(0)
    weight(0)
    weight_across(0)
    for k in range(halves):
        at.arrived(gw_core.at[k], vc_recv.at[k])
        gw_core[k] = gw[:, core + 2 * k] + gw_core[k]
    km = mine // 2 if parts == 4 else 0
    if parts == 4:
        at.send(gw_core.at[1 - km], gw_y, vy_send.at[0], vy_recv.at[0], rep=at.flip(2))
    rows_summed(0)
    weight_joined(2, 0)
    weight_joined(2, 1)
    weight_joined(2, 3)
    if parts == 4:
        at.arrived(gw_y, vy_recv.at[0])
        gw_sum[...] = gw_core[km] + gw_y[...]
    else:
        gw_sum[...] = gw_core[0]
    for i, (da, db) in enumerate(peers):
        dest = at.at(da, db)
        at.send(gw_sum.at[dest], gw_land.at[me], va_send.at[i], va_recv.at[me], shard=dest)
    gw_land[me] = gw_sum[me]
    rows_across(1)
    rows_across(2)
    rows_last_across()
    weight_summed(1)
    row_sums.joined(0)
    weight_joined(1, 0)
    weight_joined(1, 1)
    weight_joined(1, 3)
    weight_summed(0)
    weight_joined(0, 0)
    weight_joined(0, 1)
    weight_joined(0, 3)
    for da, db in peers:
        origin = at.at(-da, -db)
        at.arrived(gw_land.at[origin], va_recv.at[origin])
    for n, mask in enumerate(extras):
        at.exchange(gw_land, gw_extra.at[n], ve_send.at[n], ve_recv.at[n], at.flip(mask))
        gw_land[...] = gw_land[...] + gw_extra[n]
    for j in range(shards):
        for t in range(3):
            first = t * width + j * slab
            gw_ref[mine, :, first : first + slab] = gw_land[j, :, t * slab : (t + 1) * slab]

    gw_go(0)
    rows_summed(1)
    weight_last(2)
    weight_last(1)
    weight_last(0)
    row_sums.joined(1)
    for n in range(count - 1):
        gw_take(n)
        gw_go(n + 1)


    def write(src, dst, n):
        copy = pltpu.make_async_copy(src, dst, done_sem.at[n])
        copy.start()
        written.append(copy)

    for da, db in peers:
        origin = at.at(-da, -db)
        at.arrived(small_land.at[origin], s_recv.at[origin])
    small = jnp.sum(small_land[...], axis=0)
    lanes = lax.broadcasted_iota(jnp.int32, (slab, 128), 1)
    sides = jnp.concatenate(
        [jnp.where(lanes == 6, bias_q, jnp.where(lanes == 7, bias_v, 0.0)), jnp.zeros((256 - slab, 128), F32)],
        axis=0,
    )
    sides = jnp.concatenate([sides[:128].T[:8], sides[128:].T[:8]], axis=1)
    shift = me * slab - lax.min(me * slab // 128 * 128, width - 256)
    window = pltpu.roll(small[:, :256], lax.rem(256 - shift, 256), 1)
    tall = lax.broadcasted_iota(jnp.int32, (8, 256), 0)
    small_got[0, :, :256] = jnp.where(tall < 5, window, sides)
    small_got[0, :, 256:] = pltpu.roll(small[:, 256:], lax.rem(128 - me * unit, 128), 1)

    def small_round(n):
        at.send(
            small_got.at[2 * n], small_got.at[2 * n + 1], b_send.at[n], b_recv.at[n], rep=at.flip(every[n])
        )

    def small_add(n):
        at.arrived(small_got.at[2 * n + 1], b_recv.at[n])
        small_got[2 * n + 2] = small_got[2 * n] + small_got[2 * n + 1]

    small_round(0)
    rows_summed(2)
    small_add(0)
    small_round(1)
    rows_last()
    gw_take(count - 1)
    write(gw_ref, gw_hbm, 2)
    for n in range(count - 1):
        for m in mats:
            fin_hands[m][1](n)
            fin_hands[m][0](n + 1)
    for n in range(1, len(every)):
        small_add(n)
        if n + 1 < len(every):
            small_round(n + 1)
    small_out_ref[...] = small_got[2 * len(every)]

    total = rows_result()
    x = x_ref[...].astype(F32)
    r = lax.rsqrt(jnp.mean(x * x, axis=-1, keepdims=True) + EPS)
    weighted = vec_ref[0:1, :] * total
    gin_ref[...] = gmixed_ref[...] + r * weighted - x * (r * r * r) * jnp.mean(x * weighted, axis=-1, keepdims=True)


    write(gin_ref, gin_hbm, 3)
    for m in mats:
        fin_hands[m][1](count - 1)
        write(fin_ref.at[m], fin_hbm.at[m], 4 + m)
    at.settle()
    for copy in written:
        copy.wait()


def layer(shards, replicas, inputs, segment_ids, positions, vectors, w_qkv, w_out, w_up, w_down, cotangent):
    block, width = inputs.shape
    slab = width // shards
    slab3 = 3 * slab
    length = shards * block
    wparts = 2 if slab % 32 == 0 else 1
    parts = parts_of(slab)
    halves = parts // 2
    rp = slab // parts
    rows_part = slab // 2 if parts == 4 else slab
    cols = width // 2
    minor = shards // MAJOR
    peers = shards - 1
    bits = (replicas - 1).bit_length()
    more = bits - (parts - 1).bit_length()
    shape = jax.ShapeDtypeStruct
    dma = pltpu.SemaphoreType.DMA
    vm = pltpu.VMEM
    return pl.pallas_call(
        functools.partial(layer_kernel, shards, replicas, wparts, parts, 2 * block),
        out_shape=(
            shape((block, width), BF16),
            shape((3, slab, width), BF16),
            shape((parts, rp, 3 * width), BF16),
            shape((block, width), F32),
            shape((8, 384), F32),
        ),
        in_specs=[VMEM] * 11 + [ANY] * 5,
        out_specs=[ANY] * 4 + [VMEM],
        scratch_shapes=[
            vm((block, width), BF16),
            vm((3, slab, width), BF16),
            vm((parts, rp, 3 * width), BF16),
            vm((block, width), F32),
            vm(w_qkv.shape, BF16),
            vm((block, width), BF16),
            vm((16, 256), F32),
            vm((length, width), BF16),
            vm((slab3, length), BF16),
            vm((slab, length), F32),
            vm((8, length), F32),
            vm((8, width), F32),
            vm((8, length), F32),
            vm((shards, wparts, slab // wparts, slab3), BF16),
            vm((3, shards, halves, slab // halves, block), BF16),
            vm((3, block, width), BF16),
            vm((width, block), BF16),
            vm((8, width), F32),
            vm((block, width), F32),
            vm((shards, block, width), BF16),
            vm((shards, 8, 256), F32),
            vm((shards, wparts, slab // wparts, slab3), BF16),
            vm((slab3, width), BF16),
            vm((slab, length), BF16),
            vm((width, block), BF16),
            vm((3, width, width), BF16),
            vm((slab, length), BF16),
            vm((slab3, length), F32),
            vm((length, slab3), BF16),
            vm((3, shards, rows_part, parts * block), BF16),
            vm((3, parts * block, cols), BF16),
            vm((3, shards, rows_part, block) if parts == 4 else (1, 1, 16, block), BF16),
            vm((3, MAJOR, minor, rows_part, cols), BF16),
            vm((3, minor - 1, MAJOR, rows_part, cols), BF16),
            vm((3, MAJOR + 1, rows_part, cols), BF16),
            vm((max(more, 1), 3, rows_part, cols), BF16),
            vm((shards, parts, rp, slab3), BF16),
            vm((halves, shards, rp, slab3), BF16),
            vm((shards, rp, slab3) if parts == 4 else (1, 16, 128), BF16),
            vm((shards, rp, slab3), BF16),
            vm((shards, rp, slab3), BF16),
            vm((max(more, 1), shards, rp, slab3), BF16),
            vm((shards, 8, 384), F32),
            vm((shards, 8, 384), F32),
            vm((2 * bits + 1, 8, 384), F32),
            dma((2, MAJOR)), dma((MAJOR, minor - 1)), dma((shards,)),
            dma((peers,)), dma((shards,)),
            dma((peers,)), dma((shards, wparts)), dma((shards,)), dma((shards,)),
            dma((2, MAJOR)), dma((MAJOR, minor - 1)), dma((shards, parts)),
            dma((shards,)), dma((shards, 2)),
            dma((5,)), dma((shards,)), dma((shards,)), dma((7,)),
            dma((peers,)), dma((shards,)),
            dma((3, 3)), dma((3, 3)),
            dma((3, 4)), dma((3, 4)),
            dma((3, minor - 1)), dma((3, minor - 1)),
            dma((3, MAJOR)), dma((3, MAJOR + 1)),
            dma((3, parts)), dma((3, parts)),
            dma((max(more, 1), 3)), dma((max(more, 1), 3)),
            dma((minor - 1, MAJOR + 1)), dma((minor - 1, MAJOR + 1)),
            dma((MAJOR + 1,)), dma((MAJOR + 2,)),
            dma((halves,)), dma((halves,)),
            dma((1,)), dma((1,)),
            dma((peers,)), dma((shards,)),
            dma((parts,)), dma((parts,)),
            dma((max(more, 1),)), dma((max(more, 1),)),
            dma((peers,)), dma((shards,)),
            dma((bits,)), dma((bits,)),
        ],
        compiler_params=pltpu.CompilerParams(
            collective_id=0, has_side_effects=True, vmem_limit_bytes=62 << 20
        ),
        name="layer",
    )(inputs, segment_ids, positions, *vectors, w_qkv, w_out, w_up, w_down, cotangent)


def finish_kernel(
    slab, unit, fin_ref, gw_ref, small_ref, gin_ref, out_ref,
    w_out_ref, w_up_ref, w_down_ref, w_qkv_ref, input_ref, output_ref,
    gain_one_ref, b_query_ref, b_value_ref, scale_ref, b_out_ref, gain_two_ref, b_up_ref, b_down_ref,
):
    w_out_ref[...] = fin_ref[0].astype(F32)
    w_up_ref[...] = fin_ref[1].astype(F32)
    w_down_ref[...] = fin_ref[2].astype(F32)
    w_qkv_ref[...] = gw_ref[...].astype(F32)
    input_ref[...] = gin_ref[...]
    output_ref[...] = out_ref[...]

    @pl.when(pl.program_id(0) == 0)
    def _():
        table = {
            0: gain_one_ref, 1: b_out_ref, 2: gain_two_ref, 3: b_up_ref, 4: b_down_ref,
            6: b_query_ref, 7: b_value_ref,
        }
        for row, ref in table.items():
            ref[...] = small_ref[row : row + 1, :slab].reshape(slab)
        scale_ref[...] = small_ref[5:6, 256 : 256 + unit].reshape(unit)


def finish(fin, gw, small, gin, out):
    slab, width = fin.shape[1:]
    block = gin.shape[0]
    steps = 2
    unit = HEAD * slab // width
    part, tokens = slab // steps, block // steps
    shape = jax.ShapeDtypeStruct

    def rows(size, columns):
        return pl.BlockSpec((size, columns), lambda i: (i, 0))

    whole = pl.BlockSpec((8, 384), lambda i: (0, 0))
    vector = pl.BlockSpec((slab,), lambda i: (0,))
    return pl.pallas_call(
        functools.partial(finish_kernel, slab, unit),
        grid=(steps,),
        out_shape=[shape((slab, width), F32)] * 3
        + [shape((slab, 3 * width), F32), shape((block, width), F32), shape((block, width), BF16)]
        + [shape((slab,), F32)] * 3
        + [shape((unit,), F32)]
        + [shape((slab,), F32)] * 4,
        in_specs=[
            pl.BlockSpec((3, part, width), lambda i: (0, i, 0)), rows(part, 3 * width), whole,
            rows(tokens, width), rows(tokens, width),
        ],
        out_specs=[rows(part, width)] * 3
        + [rows(part, 3 * width), rows(tokens, width), rows(tokens, width)]
        + [vector] * 3
        + [pl.BlockSpec((unit,), lambda i: (0,))]
        + [vector] * 4,
        name="finish",
    )(fin, gw, small, gin, out)


def on_device(
    inputs, segment_ids, positions, gain_one, w_qkv, b_query, b_value, query_scale, w_out, b_out,
    gain_two, w_up, b_up, w_down, b_down, cotangent,
):
    shards = lax.axis_size("shard")
    replicas = lax.axis_size("replica")
    block, width = inputs.shape[1:]
    slab = width // shards
    output, fin, gw, input_grad, small = layer(
        shards, replicas, inputs.reshape(block, width), segment_ids, positions,
        (gain_one, b_query, b_value, query_scale, b_out, gain_two, b_up, b_down),
        w_qkv, w_out, w_up, w_down, cotangent.reshape(block, width),
    )
    (
        g_out, g_up, g_down, g_qkv, input_grad, output, g_gain_one, g_b_query, g_b_value, g_scale, g_b_out,
        g_gain_two, g_b_up, g_b_down,
    ) = finish(fin, gw.reshape(slab, 3 * width), small, input_grad, output)
    return (
        output[None], input_grad[None], g_gain_one, g_qkv, g_b_query, g_b_value, g_scale, g_out, g_b_out,
        g_gain_two, g_up, g_b_up, g_down, g_b_down,
    )


def solution(mesh):
    rows = P("replica", "shard", None)
    ids = P("replica", "shard")
    vector = P("shard")
    matrix = P("shard", None)
    in_specs = (
        rows, ids, ids, vector, matrix, vector, vector, vector, matrix, vector, vector, matrix, vector,
        matrix, vector, rows,
    )
    out_specs = (
        rows, rows, vector, matrix, vector, vector, vector, matrix, vector, vector, matrix, vector, matrix,
        vector,
    )
    return jax.shard_map(on_device, mesh=mesh, in_specs=in_specs, out_specs=out_specs, check_vma=False)
```

```python
import functools
import math

import jax
import jax.numpy as jnp
from jax import lax
from jax.experimental import pallas as pl
from jax.experimental.pallas import tpu as pltpu
from jax.sharding import PartitionSpec as P

HEADS = 16
HEAD = 80
EPS = 1e-06
QUERY_BASE = 1.442695041
MASKED = -1000000000.0
MESH = pl.DeviceIdType.MESH
MAJOR = 4
VMEM = pl.BlockSpec(memory_space=pltpu.VMEM)
ANY = pl.BlockSpec(memory_space=pl.ANY)
F32 = jnp.float32
BF16 = jnp.bfloat16
NN = (((1,), (0,)), ((), ()))
NT = (((1,), (1,)), ((), ()))
TN = (((0,), (0,)), ((), ()))


def dot(lhs, rhs, dims=NN):
    return lax.dot_general(lhs, rhs, dims, preferred_element_type=F32)


class Place:
    def __init__(self, shards):
        self.shards = shards
        self.minor = shards // MAJOR
        self.me = lax.axis_index("shard")
        self.rep = lax.axis_index("replica")
        self.a = self.me // self.minor
        self.b = lax.rem(self.me, self.minor)
        self.started = []

    def at(self, da, db):
        a = lax.rem(self.a + da + MAJOR, MAJOR)
        b = lax.rem(self.b + db + self.minor, self.minor)
        return a * self.minor + b

    def peers(self):
        return [(da, db) for da in range(MAJOR) for db in range(self.minor) if da or db]

    def flip(self, mask):
        bit = lax.rem(self.rep // mask, 2)
        return self.rep + mask - 2 * mask * bit

    def greet(self, masks):
        barrier = pltpu.get_barrier_semaphore()
        for da, db in self.peers():
            pl.semaphore_signal(
                barrier, inc=1, device_id=(self.at(da, db), self.rep), device_id_type=MESH
            )
        for mask in masks:
            pl.semaphore_signal(
                barrier, inc=1, device_id=(self.me, self.flip(mask)), device_id_type=MESH
            )
        pl.semaphore_wait(barrier, len(self.peers()) + len(masks))

    def send(self, src, dst, ssem, rsem, shard=None, rep=None, when=None):
        copy = pltpu.make_async_remote_copy(
            src_ref=src,
            dst_ref=dst,
            send_sem=ssem,
            recv_sem=rsem,
            device_id=(self.me if shard is None else shard, self.rep if rep is None else rep),
            device_id_type=MESH,
        )
        if when is None:
            copy.start()
        else:
            @pl.when(when)
            def _():
                copy.start()
        self.started.append((when, copy))

    def arrived(self, dst, rsem):
        pltpu.make_async_remote_copy(
            src_ref=dst,
            dst_ref=dst,
            send_sem=rsem,
            recv_sem=rsem,
            device_id=(self.me, self.rep),
            device_id_type=MESH,
        ).wait_recv()

    def exchange(self, src, dst, ssem, rsem, rep):
        self.send(src, dst, ssem, rsem, rep=rep)
        self.arrived(dst, rsem)
        self.started.pop()[1].wait_send()

    def settle(self):
        for when, copy in self.started:
            if when is None:
                copy.wait_send()
            else:
                @pl.when(when)
                def _():
                    copy.wait_send()
        self.started = []


class Line:
    def __init__(self, at, slot, major_send, minor_send, recv):
        self.at, self.slot = at, slot
        self.major_send, self.minor_send, self.recv = major_send, minor_send, recv

    def onward(self, origin, up, down, d):
        at = self.at
        if up is not None:
            at.send(
                self.slot(origin), self.slot(origin), self.major_send.at[0, d], self.recv(origin),
                shard=lax.min(at.a + 1, MAJOR - 1) * at.minor + at.b, when=up,
            )
        if down is not None:
            at.send(
                self.slot(origin), self.slot(origin), self.major_send.at[1, d], self.recv(origin),
                shard=lax.max(at.a - 1, 0) * at.minor + at.b, when=down,
            )

    def across(self, origin, when=None):
        at = self.at
        for db in range(1, at.minor):
            at.send(
                self.slot(origin), self.slot(origin), self.minor_send.at[origin // at.minor, db - 1],
                self.recv(origin), shard=at.at(0, db), when=when,
            )

    def along_own(self):
        at = self.at
        self.onward(at.me, at.a + 1 < MAJOR, at.a > 0, 0)

    def sides(self, d):
        at = self.at
        for side in (-1, 1):
            ok = (at.a - d >= 0) if side < 0 else (at.a + d < MAJOR)
            origin = lax.max(at.a - d, 0) if side < 0 else lax.min(at.a + d, MAJOR - 1)
            yield side, ok, origin * at.minor + at.b

    def take(self, d, then=None):
        for side, ok, origin in self.sides(d):
            @pl.when(ok)
            def _():
                self.at.arrived(self.slot(origin), self.recv(origin))

            if then is not None:
                then(origin, ok)

    def along(self, d):
        at = self.at
        if d + 1 < MAJOR:
            for side, ok, origin in self.sides(d):
                if side < 0:
                    self.onward(origin, ok & (at.a + 1 < MAJOR), None, d)
                else:
                    self.onward(origin, None, ok & (at.a > 0), d)

    def aside(self, d):
        for side, ok, origin in self.sides(d):
            self.across(origin, when=ok)

    def step(self, d, then=None):
        self.take(d, then)
        self.along(d)
        self.aside(d)


def parts_of(rows):
    return 4 if rows % 32 == 0 else 2


def part_box(part, parts, rows, cols):
    if parts == 4:
        i, j, rows = lax.rem(part, 2), part // 2, rows // 2
    else:
        i, j = 0, part
    return i * rows, rows, j * (cols // 2), cols // 2


def flipped(part, mask):
    bit = lax.rem(part // mask, 2)
    return part + mask - 2 * mask * bit


def layer_kernel(
    shards, replicas, wparts, parts, qblock,
    x_ref, segment_ref, position_ref, gain_one_ref, b_query_ref, b_value_ref, scale_ref,
    b_out_ref, gain_two_ref, b_up_ref, b_down_ref, w_hbm, wout_ref, wup_ref, wdown_ref, cot_hbm,
    out_hbm, fin_hbm, gw_hbm, gin_hbm, small_out_ref,
    out_ref, fin_ref, gw_ref, gin_ref, w_ref, cot_ref, small_ref,
    normed_ref, qkv_ref, query_ref, log_ref, vec_ref, start_ref, wcols_ref,
    xt_ref, dy_ref, dctx_ref, row_ref, gmixed_ref,
    xg, packets, pieces, turned, context, att, weights,
    dctx, grads, proj, left, right, stash, sums, from_x, from_z, extra,
    gw, gw_core, gw_y, gw_sum, gw_land, gw_extra,
    windows, small_land, small_got,
    xm_send, xn_send, x_recv, p_send, p_recv, w_send, w_recv, wc_send, wy_send,
    fm_send, fn_send, f_recv, fy_send, fc_send, local_sem, a_send, a_recv, done_sem,
    d_send, d_recv, gy_send, gy_recv, gc_send, gc_recv, gx_send, gx_recv, gz_send, gz_recv,
    r_send, r_recv, e_send, e_recv, nx_send, nx_recv, nz_send, nz_recv,
    vc_send, vc_recv, vy_send, vy_recv, va_send, va_recv, vr_send, vr_recv, ve_send, ve_recv,
    s_send, s_recv, b_send, b_recv,
):
    at = Place(shards)
    me, minor = at.me, at.minor
    block, width = x_ref.shape
    length = shards * block
    slab = width // shards
    slab3 = 3 * slab
    local = slab // HEAD
    peers = at.peers()
    masks = (2, 1) if parts == 4 else (1,)
    every = []
    bit = 1
    while bit < replicas:
        every.append(bit)
        bit *= 2
    extras = [m for m in every if m >= parts]
    mine = lax.rem(at.rep, parts)
    wpart = lax.rem(at.rep, wparts)

    loads = []
    for m, ref in enumerate((wout_ref, wup_ref, wdown_ref)):
        copy = pltpu.make_async_copy(
            ref, weights.at[m, pl.ds(pl.multiple_of(me * slab, 16), slab), :], local_sem.at[m]
        )
        copy.start()
        loads.append(copy)
    w_load = pltpu.make_async_copy(w_hbm, w_ref, local_sem.at[3])
    w_load.start()
    cot_load = pltpu.make_async_copy(cot_hbm, cot_ref, local_sem.at[4])
    cot_load.start()
    xg[me] = x_ref[...]
    small_ref[...] = jnp.zeros_like(small_ref)
    table = {
        0: gain_one_ref, 1: b_out_ref, 2: gain_two_ref, 3: b_up_ref, 4: b_down_ref, 5: scale_ref,
        8: b_query_ref, 9: b_value_ref,
    }
    for row, ref in table.items():
        size = ref.shape[0]
        small_ref[row : row + 1, :size] = ref[...].astype(F32).reshape(1, size)
    place = me * block + lax.broadcasted_iota(jnp.int32, (1, block), 1)
    small_ref[6:7, :block] = (place - position_ref[...]).astype(F32)
    small_ref[10:11, :block] = (segment_ref[...] != 0).astype(F32)
    packets[me] = small_ref[:8]
    at.greet(tuple(every))

    def wslot(origin, part):
        row, rows, col, cols = part_box(part, parts, slab, width)
        return weights.at[
            :,
            pl.ds(pl.multiple_of(origin * slab + row, 16), rows),
            pl.ds(pl.multiple_of(col, 128), cols),
        ]

    rows_line = Line(at, lambda o: xg.at[o], xm_send, xn_send, lambda o: x_recv.at[o])
    ffn_line = Line(
        at, lambda o: wslot(o, mine), fm_send, fn_send, lambda o: f_recv.at[o, mine]
    )

    def to_replicas(origin, when=None):
        slot = wslot(origin, mine)
        for mask in masks:
            sem = fy_send.at[origin] if mask == 2 else fc_send.at[origin, 0]
            at.send(slot, slot, sem, f_recv.at[origin, mine], rep=at.flip(mask), when=when)

    cols = width // 2
    core = lax.rem(at.rep, 2)
    i_part = lax.rem(mine, 2) if parts == 4 else 0
    j_part = mine // 2 if parts == 4 else mine
    mats = (2, 1, 0)

    def lane(n, size):
        return pl.ds(pl.multiple_of(n * size, 128), size)

    def seat(n):
        return slice(n * block, (n + 1) * block)

    near = parts // 2

    def meet_columns(m):
        if parts == 4:
            at.send(
                dy_ref.at[m, :, lane(1 - j_part, cols)], right.at[m, seat(1), :],
                gy_send.at[m, 1], gy_recv.at[m, 1], rep=at.flip(2),
            )
        at.send(
            dy_ref.at[m, :, lane(j_part if parts == 4 else 1 - j_part, cols)], right.at[m, seat(near), :],
            gc_send.at[m, 1], gc_recv.at[m, 1], rep=at.flip(1),
        )
        right[m, seat(0), :] = dy_ref[m, :, lane(j_part, cols)]

    def meet_rows(m):
        if parts == 4:
            far = at.flip(2)
            at.send(xt_ref.at[m, :, 1 - i_part], stash.at[m], gy_send.at[m, 2], gy_recv.at[m, 2], rep=far)
            at.send(
                xt_ref.at[m, :, i_part], left.at[m, :, :, seat(1)], gy_send.at[m, 0], gy_recv.at[m, 0], rep=far
            )
        at.send(
            xt_ref.at[m, :, 1 - i_part if parts == 4 else 0], left.at[m, :, :, seat(near)],
            gc_send.at[m, 0], gc_recv.at[m, 0], rep=at.flip(1),
        )
        left[m, :, :, seat(0)] = xt_ref[m, :, i_part]

    def relay_columns(m):
        if parts == 4:
            at.arrived(right.at[m, seat(1), :], gy_recv.at[m, 1])
            at.send(
                right.at[m, seat(1), :], right.at[m, seat(3), :], gc_send.at[m, 3], gc_recv.at[m, 3], rep=at.flip(1)
            )

    def relay_rows(m):
        if parts == 4:
            at.arrived(stash.at[m], gy_recv.at[m, 2])
            at.send(stash.at[m], left.at[m, :, :, seat(3)], gc_send.at[m, 2], gc_recv.at[m, 2], rep=at.flip(1))

    for i, (da, db) in enumerate(peers):
        at.send(packets.at[me], packets.at[me], p_send.at[i], p_recv.at[me], shard=at.at(da, db))
    rows_line.along_own()
    for copy in loads:
        copy.wait()
    ffn_line.across(me)
    rows_line.across(me)
    cot_load.wait()
    dy_ref[2] = cot_ref[...]
    meet_columns(2)
    w_load.wait()
    cut = slab // wparts
    for j in range(shards):
        for t in range(3):
            first = t * width + j * slab
            pieces[j, :, :, t * slab : (t + 1) * slab] = w_ref[:, first : first + slab].reshape(
                wparts, cut, slab
            )
    parity = lax.rem(at.a + mine // 2, 2)
    chosen = parity == 0 if parts == 4 else None
    for i, (da, db) in enumerate(peers):
        dest = at.at(da, db)
        at.send(
            pieces.at[dest, wpart], wcols_ref.at[me, wpart], w_send.at[i], w_recv.at[me, wpart], shard=dest,
            when=chosen,
        )
    wcols_ref[me] = pieces[me]
    ffn_line.along_own()

    def ffn_minor(distance):
        for db in range(1, minor):
            sides = ((-1, 1) if distance else (0,))
            for side in sides:
                a = at.a + side * distance
                ok = None
                if distance:
                    ok = (a >= 0) & (a < MAJOR)
                origin = lax.max(lax.min(a, MAJOR - 1), 0) * minor + lax.rem(at.b + db, minor)
                slot = wslot(origin, mine)
                if ok is None:
                    at.arrived(slot, f_recv.at[origin, mine])
                else:
                    @pl.when(ok)
                    def _():
                        at.arrived(slot, f_recv.at[origin, mine])
                to_replicas(origin, ok)

    def columns(phase):
        for q in range(2):
            for db in range(minor):
                da = lax.rem(parity + phase, 2) + 2 * q
                origin = at.at(-da, -db)
                slot = wcols_ref.at[origin, wpart]
                real = origin != me

                @pl.when(real)
                def _():
                    at.arrived(slot, w_recv.at[origin, wpart])

                if parts == 4 and phase == 0:
                    at.send(
                        slot, slot, wy_send.at[origin], w_recv.at[origin, wpart], rep=at.flip(2), when=real
                    )
                if wparts == 2:
                    at.send(
                        slot, slot, wc_send.at[origin], w_recv.at[origin, wpart], rep=at.flip(1), when=real
                    )

    ffn_minor(0)
    rows_line.step(1)
    ffn_line.step(1, to_replicas)
    rows_line.step(2)
    columns(0)

    for da, db in peers:
        origin = at.at(-da, -db)
        at.arrived(packets.at[origin], p_recv.at[origin])
    vectors = jnp.zeros((8, width), F32)
    scales = jnp.zeros((1, 128), F32)
    lanes = lax.broadcasted_iota(jnp.int32, (8, width), 1)
    unit = HEAD // shards
    for j in range(shards):
        piece = packets[j]
        wide = jnp.concatenate([piece, jnp.zeros((8, width - piece.shape[1]), F32)], axis=1)
        wide = jnp.where(lanes < slab, wide, 0.0)
        vectors = vectors + (pltpu.roll(wide, j * slab, 1) if j else wide)
        scale = jnp.where(lanes[0:1, :128] < unit, piece[5:6, :128], 0.0)
        scales = scales + (pltpu.roll(scale, j * unit, 1) if j else scale)
        start_ref[:, j * block : (j + 1) * block] = jnp.broadcast_to(piece[6:7, :block], (8, block))
    rows = lax.broadcasted_iota(jnp.int32, (8, width), 0)
    vec_ref[...] = jnp.where(rows < 5, vectors, 0.0)
    vec_ref[5:6, :128] = scales
    gain = vec_ref[0:1, :]
    column = jnp.broadcast_to(scales, (128, 128)).T[:HEAD, 0:1]
    soft = jnp.maximum(column, 0.0) + jnp.log(1.0 + jnp.exp(-jnp.abs(column)))
    factor = jnp.concatenate([QUERY_BASE / math.sqrt(HEAD) * soft] * local, axis=0)
    own = small_ref[8:16, :]
    tall = jnp.concatenate([own, jnp.zeros((120, 256), F32)], axis=0)
    tall = jnp.concatenate([tall[:, :128].T, tall[:, 128:].T], axis=0)
    bias_query = tall[:slab, 0:1]
    bias_value = tall[:slab, 1:2]

    ffn_line.step(2, to_replicas)
    ffn_minor(1)
    rows_line.step(3)
    columns(1)
    relay_columns(2)
    if wparts == 2:
        for da, db in peers:
            origin = at.at(-da, -db)
            last = wparts - 1 - wpart
            at.arrived(wcols_ref.at[origin, last], w_recv.at[origin, last])
    turned[...] = wcols_ref[...].reshape(width, slab3).T

    def project(origin):
        rows_in = xg[origin].astype(F32)
        scale = lax.rsqrt(jnp.mean(rows_in * rows_in, axis=-1, keepdims=True) + EPS)
        normed = (rows_in * scale * gain).astype(BF16)
        tokens = pl.ds(pl.multiple_of(origin * block, block), block)
        normed_ref[tokens, :] = normed
        out = dot(turned[...], normed, NT)
        query = out[:slab] + bias_query
        query_ref[:, tokens] = query
        qkv_ref[:slab, tokens] = (query * factor).astype(BF16)
        qkv_ref[slab : 2 * slab, tokens] = out[slab : 2 * slab].astype(BF16)
        qkv_ref[2 * slab :, tokens] = (out[2 * slab :] + bias_value).astype(BF16)

    ffn_line.step(3, to_replicas)

    def project_major(i, carry):
        project(at.at(i, 0))
        return carry

    def project_minor(i, carry):
        origin = at.at(lax.rem(i, MAJOR), 1 + i // MAJOR)
        at.arrived(xg.at[origin], x_recv.at[origin])
        project(origin)
        return carry

    lax.fori_loop(0, MAJOR, project_major, 0)
    ffn_minor(2)
    lax.fori_loop(0, shards - MAJOR, project_minor, 0)
    ffn_minor(3)

    log_ref[...] = jnp.zeros_like(log_ref)
    for i in range(length // qblock):
        reach = (i + 1) * qblock
        span = slice(i * qblock, reach)
        starts = start_ref[0:1, span]
        key_place = lax.broadcasted_iota(jnp.int32, (reach, qblock), 0).astype(F32)
        query_place = (i * qblock + lax.broadcasted_iota(jnp.int32, (1, qblock), 1)).astype(F32)
        allowed = (key_place >= starts) & (key_place <= query_place)
        for h in range(local):
            head = slice(h * HEAD, (h + 1) * HEAD)
            queries = qkv_ref[h * HEAD : (h + 1) * HEAD, span]
            keys = qkv_ref[slab + h * HEAD : slab + (h + 1) * HEAD, :reach]
            values = qkv_ref[2 * slab + h * HEAD : 2 * slab + (h + 1) * HEAD, :reach]
            scores = jnp.where(allowed, dot(keys, queries, TN), MASKED)
            top = jnp.max(scores, axis=0, keepdims=True)
            powers = jnp.exp(scores - top)
            total = jnp.sum(powers, axis=0, keepdims=True)
            probs = (powers * (1.0 / total)).astype(BF16)
            log_ref[h : h + 1, span] = top + jnp.log(total)
            context[head, span] = dot(values, probs).astype(BF16)
        heads = pl.ds(pl.multiple_of(me * slab, 16), slab)
        for j in range(i * qblock // block, reach // block):
            piece = slice(j * block, (j + 1) * block)
            at.send(context.at[:, piece], att.at[heads, :], a_send.at[j], a_recv.at[me], shard=j, when=me != j)

            @pl.when(me == j)
            def _():
                att[heads, :] = context[:, piece]

    order = [(0, db) for db in range(1, minor)]
    order += [(da, db) for da in range(1, MAJOR) for db in range(minor)]
    if parts == 4:
        for da, db in order:
            origin = at.at(da, db)
            part = flipped(mine, 2)
            slot = wslot(origin, part)
            at.arrived(slot, f_recv.at[origin, part])
            at.send(slot, slot, fc_send.at[origin, 1], f_recv.at[origin, part], rep=at.flip(1))
    for da, db in peers:
        origin = at.at(-da, -db)
        at.arrived(att.at[pl.ds(pl.multiple_of(origin * slab, 16), slab), :], a_recv.at[origin])
    others = [flipped(mine, 1)] + ([flipped(flipped(mine, 1), 2)] if parts == 4 else [])
    for da, db in order:
        origin = at.at(da, db)
        for part in others:
            at.arrived(wslot(origin, part), f_recv.at[origin, part])

    def weight(m):
        at.arrived(left.at[m, :, :, seat(near)], gc_recv.at[m, 0])
        at.arrived(right.at[m, seat(near), :], gc_recv.at[m, 1])
        if parts == 4:
            at.arrived(left.at[m, :, :, seat(1)], gy_recv.at[m, 0])
            at.arrived(left.at[m, :, :, seat(3)], gc_recv.at[m, 2])
            at.arrived(right.at[m, seat(3), :], gc_recv.at[m, 3])
        rows = left.shape[1] * left.shape[2]
        out = dot(left[m].reshape(rows, parts * block), right[m])
        sums[m] = out.reshape(sums.shape[1:]).astype(BF16)

    def weight_across(m):
        for db in range(1, minor):
            at.send(
                sums.at[m, :, lax.rem(at.b + db, minor)], from_x.at[m, db - 1],
                gx_send.at[m, db - 1], gx_recv.at[m, db - 1], shard=at.at(0, db),
            )

    ahead = jnp.where(at.a < MAJOR // 2, 1, -1)
    middle = (at.a > 0) & (at.a < MAJOR - 1)

    def turn(n):
        return jnp.where(at.a < MAJOR // 2, MAJOR - 1 - n, n)

    class Chain:
        def __init__(self, own, land, ssem, rsem):
            self.own, self.land, self.ssem, self.rsem = own, land, ssem, rsem

        def go(self, n, when=None):
            t = turn(n)
            way = -ahead if n == 3 else ahead
            to = lax.max(lax.min(at.a + way, MAJOR - 1), 0) * minor + at.b
            dst = jnp.where(middle, MAJOR, t) if n == 1 else t
            at.send(self.own(t), self.land(dst), self.ssem.at[n], self.rsem.at[dst], shard=to, when=when)

        def summed(self, n):
            if n < 3:
                self.go(n, jnp.logical_not(middle))

        def joined(self, n):
            t = turn(n)

            @pl.when(middle)
            def _():
                at.arrived(self.land(t), self.rsem.at[t])
                self.own(t)[...] = self.own(t)[...] + self.land(t)[...]

            self.go(n, middle)

        def result(self):
            at.arrived(self.land(at.a), self.rsem.at[at.a])
            total = self.own(at.a)[...].astype(F32) + self.land(at.a)[...].astype(F32)
            self.own(at.a)[...] = total.astype(BF16)

            @pl.when(middle)
            def _():
                at.arrived(self.land(MAJOR), self.rsem.at[MAJOR])
                self.own(at.a)[...] = (total + self.land(MAJOR)[...].astype(F32)).astype(BF16)

            return self.own(at.a)[...]

    ffn_sums = {
        m: Chain(
            lambda t, m=m: sums.at[m, t, at.b], lambda n, m=m: from_z.at[m, n], gz_send.at[m], gz_recv.at[m]
        )
        for m in mats
    }

    def land_x(db, t):
        first = (db - 1) // 2 * MAJOR + t
        return weights.at[(db - 1) % 2, pl.ds(pl.multiple_of(first * block, block), block), :]

    def land_z(n):
        return weights.at[1, pl.ds(pl.multiple_of((MAJOR + n) * block, block), block), :]

    row_sums = Chain(lambda t: xg.at[t * minor + at.b], land_z, nz_send, nz_recv)

    def rows_across(n):
        t = turn(n)
        for db in range(1, minor):
            to = t * minor + lax.rem(at.b + db, minor)
            at.send(
                xg.at[to], land_x(db, t), nx_send.at[db - 1, n], nx_recv.at[db - 1, t], shard=at.at(0, db)
            )

    def rows_summed(n):
        t = turn(n)
        own = row_sums.own(t)
        total = own[...].astype(F32)
        for db in range(1, minor):
            at.arrived(land_x(db, t), nx_recv.at[db - 1, t])
            total = total + land_x(db, t)[...].astype(F32)
        own[...] = total.astype(BF16)
        row_sums.summed(n)

    def weight_summed(m):
        for db in range(1, minor):
            at.arrived(from_x.at[m, db - 1], gx_recv.at[m, db - 1])
        for n in range(MAJOR):
            t = turn(n)
            total = sums[m, t, at.b].astype(F32)
            for db in range(1, minor):
                total = total + from_x[m, db - 1, t].astype(F32)
            sums[m, t, at.b] = total.astype(BF16)
            ffn_sums[m].summed(n)

    def weight_joined(m, n):
        ffn_sums[m].joined(n)

    def rows_last_across():
        t = turn(3)
        for n in range(2):
            half = pl.ds(n * cols, cols)
            for db in range(1, minor):
                to = t * minor + lax.rem(at.b + db, minor)
                at.send(
                    xg.at[to, :, half], land_x(db, t).at[:, half], nx_send.at[db - 1, 3 + n],
                    nx_recv.at[db - 1, MAJOR if n else t], shard=at.at(0, db),
                )

    def rows_last():
        t = turn(3)
        own = row_sums.own(t)
        to = lax.max(lax.min(at.a - ahead, MAJOR - 1), 0) * minor + at.b
        for n in range(2):
            half = pl.ds(n * cols, cols)
            total = own[:, half].astype(F32)
            for db in range(1, minor):
                piece = land_x(db, t).at[:, half]
                at.arrived(piece, nx_recv.at[db - 1, MAJOR if n else t])
                total = total + piece[...].astype(F32)
            own[:, half] = total.astype(BF16)

            @pl.when(middle)
            def _():
                if n == 0:
                    at.arrived(land_z(t), nz_recv.at[t])
                own[:, half] = own[:, half] + land_z(t)[:, half]

            at.send(
                own.at[:, half], land_z(t).at[:, half], nz_send.at[3 + n],
                nz_recv.at[MAJOR + 1 if n else t], shard=to, when=middle,
            )

    def rows_result():
        own = row_sums.own(at.a)
        mine_z = land_z(at.a)

        @pl.when(middle)
        def _():
            at.arrived(mine_z, nz_recv.at[at.a])
            at.arrived(land_z(MAJOR), nz_recv.at[MAJOR])
            first = own[...].astype(F32) + mine_z[...].astype(F32)
            gin_ref[...] = first + land_z(MAJOR)[...].astype(F32)

        @pl.when(jnp.logical_not(middle))
        def _():
            at.arrived(mine_z.at[:, :cols], nz_recv.at[at.a])
            at.arrived(mine_z.at[:, cols:], nz_recv.at[MAJOR + 1])
            gin_ref[...] = own[...].astype(F32) + mine_z[...].astype(F32)

        return gin_ref[...]

    def fin_slot(part, m=None):
        row, rows, col, wide = part_box(part, parts, slab, width)
        box = (pl.ds(pl.multiple_of(row, 16), rows), pl.ds(pl.multiple_of(col, 128), wide))
        return fin_ref.at[(slice(None) if m is None else m,) + box]

    def weight_done(m):
        fin_slot(mine, m)[...] = ffn_sums[m].result()

    forward, at.started = at.started, []
    keep_row = small_ref[10:11, :block]
    b_out, gain_two, b_up, b_down = (vec_ref[i : i + 1, :] for i in range(1, 5))
    halves = xt_ref.shape[2]

    def split_rows(value):
        return value.reshape(shards, halves, slab // halves, block)

    att_t = (att[...].astype(F32) * keep_row).astype(BF16)
    mixed = x_ref[...].astype(F32) + dot(att_t.T, weights[0]) + b_out
    r = lax.rsqrt(jnp.mean(mixed * mixed, axis=-1, keepdims=True) + EPS)
    normed_two = (mixed * r * gain_two).astype(BF16)
    hidden = dot(normed_two, weights[1]) + b_up
    s = 1.0 / (1.0 + jnp.exp(-hidden))
    act = (hidden * s).astype(BF16)
    xt_ref[2] = split_rows(act.T)
    meet_rows(2)
    cot = cot_ref[...].astype(F32)
    g_hidden = dot(cot_ref[...], weights[2], NT) * (s + hidden * s * (1.0 - s))
    low = g_hidden.astype(BF16)
    g_normed = dot(low, weights[1], NT)
    weighted = gain_two * g_normed
    g_mixed = cot + r * weighted - mixed * (r * r * r) * jnp.mean(mixed * weighted, axis=-1, keepdims=True)
    g_low = g_mixed.astype(BF16)
    dctx_ref[...] = (dot(weights[0], g_low, NT).astype(BF16).astype(F32) * keep_row).astype(BF16)
    backward, at.started = at.started, forward
    at.settle()
    at.started = backward
    for i, (da, db) in enumerate(peers):
        dest = at.at(da, db)
        at.send(
            dctx_ref.at[pl.ds(pl.multiple_of(dest * slab, 16), slab), :],
            dctx.at[:, lane(me, block)], d_send.at[i], d_recv.at[me], shard=dest,
        )
    dctx[:, lane(me, block)] = dctx_ref[pl.ds(pl.multiple_of(me * slab, 16), slab), :]
    dy_ref[1] = low
    xt_ref[1] = split_rows(normed_two.T)
    meet_columns(1)
    meet_rows(1)
    gmixed_ref[...] = g_mixed
    dy_ref[0] = g_low
    xt_ref[0] = split_rows(att_t)
    meet_columns(0)
    meet_rows(0)
    out_ref[...] = (mixed + dot(act, weights[2]) + b_down).astype(BF16)
    written = [pltpu.make_async_copy(out_ref, out_hbm, done_sem.at[0])]
    written[0].start()
    row_ref[...] = jnp.zeros_like(row_ref)
    row_ref[1:2, :] = jnp.sum(g_mixed, axis=0, keepdims=True)
    row_ref[2:3, :] = jnp.sum(g_normed * mixed * r, axis=0, keepdims=True)
    row_ref[3:4, :] = jnp.sum(g_hidden, axis=0, keepdims=True)
    row_ref[4:5, :] = jnp.sum(cot, axis=0, keepdims=True)

    def hand_round(ref_slot, send_sem, recv_sem):
        have, rounds, k = [mine], [], 0
        for mask in ((2, 1) if parts == 4 else (1,)):
            sends = []
            for part in have:
                sends.append((part, mask, k))
                k += 1
            fresh = [flipped(part, mask) for part in have]
            rounds.append((sends, fresh))
            have = have + fresh

        def go(n):
            for part, mask, k in rounds[n][0]:
                at.send(ref_slot(part), ref_slot(part), send_sem.at[k], recv_sem.at[part], rep=at.flip(mask))

        def take(n):
            for part in rounds[n][1]:
                at.arrived(ref_slot(part), recv_sem.at[part])

        return go, take, len(rounds)

    gw_go, gw_take, count = hand_round(lambda part: gw_ref.at[part], vr_send, vr_recv)
    fin_hands = [
        hand_round(lambda part, m=m: fin_slot(part, m), r_send.at[m], r_recv.at[m]) for m in range(3)
    ]

    def weight_last(m):
        weight_done(m)
        for n, mask in enumerate(extras):
            here = fin_slot(mine, m)
            at.exchange(here, extra.at[n, m], e_send.at[n, m], e_recv.at[n, m], at.flip(mask))
            here[...] = here[...] + extra[n, m]
        fin_hands[m][0](0)

    base = QUERY_BASE / math.sqrt(HEAD)
    factor = base * soft
    grads[...] = jnp.zeros_like(grads)
    relay_rows(2)
    for da, db in peers:
        origin = at.at(-da, -db)
        at.arrived(dctx.at[:, lane(origin, block)], d_recv.at[origin])

    def attend(i):
        reach = (i + 1) * qblock
        span = slice(i * qblock, reach)
        starts = start_ref[0:1, span]
        key_place = lax.broadcasted_iota(jnp.int32, (reach, qblock), 0).astype(F32)
        query_place = (i * qblock + lax.broadcasted_iota(jnp.int32, (1, qblock), 1)).astype(F32)
        allowed = (key_place >= starts) & (key_place <= query_place)
        for h in range(local):
            queries = qkv_ref[h * HEAD : (h + 1) * HEAD, span]
            keys = qkv_ref[slab + h * HEAD : slab + (h + 1) * HEAD, :reach]
            values = qkv_ref[2 * slab + h * HEAD : 2 * slab + (h + 1) * HEAD, :reach]
            gctx = dctx[h * HEAD : (h + 1) * HEAD, span]
            scores = dot(keys, queries, TN)
            probs = jnp.where(allowed, jnp.exp(scores - log_ref[h : h + 1, span]), 0.0)
            gprobs = dot(values, gctx, TN)
            delta = jnp.sum(probs * gprobs, axis=0, keepdims=True)
            gscores = (probs * (gprobs - delta)).astype(BF16)
            low = probs.astype(BF16)
            grads[h * HEAD : (h + 1) * HEAD, span] = dot(keys, gscores)
            kv = slice(slab + h * HEAD, slab + (h + 1) * HEAD)
            grads[kv, :reach] += dot(queries, gscores, NT)
            kv = slice(2 * slab + h * HEAD, 2 * slab + (h + 1) * HEAD)
            grads[kv, :reach] += dot(gctx, low, NT)

    weight(2)
    weight_across(2)
    attend(0)
    for i in range(1, length // qblock):
        attend(i)

    gscale = jnp.zeros((HEAD, 1), F32)
    for h in range(local):
        rows = slice(h * HEAD, (h + 1) * HEAD)
        scaled = grads[rows, :]
        gscale = gscale + jnp.sum(scaled * query_ref[rows, :], axis=1, keepdims=True)
        grads[rows, :] = scaled * factor
    gscale = gscale * (base / (1.0 + jnp.exp(-column)))
    bias_q = jnp.sum(grads[:slab, :], axis=1, keepdims=True)
    bias_v = jnp.sum(grads[2 * slab :, :], axis=1, keepdims=True)
    tall_rows = grads.shape[0]
    low_t = grads[...].astype(BF16)
    if tall_rows % 128:
        low_t = jnp.concatenate([low_t, jnp.zeros((-tall_rows % 128, length), BF16)], axis=0)
    proj[...] = low_t.T[:, :slab3]

    wcols = wcols_ref[...].reshape(width, slab3)

    def partial(origin, acc):
        tokens = lane(origin, block)
        out = dot(proj[tokens, :], wcols, NT)
        xg[origin] = out.astype(BF16)
        weighted = out * normed_ref[tokens, :].astype(F32)
        return acc + jnp.sum(weighted.reshape(block // 8, 8, width), axis=0)

    def away(i, acc):
        return partial(turn(1 + lax.rem(i, 3)) * minor + lax.rem(at.b + 1 + i // 3, minor), acc)

    gain_rows = jnp.zeros((8, width), F32)
    for db in range(1, minor):
        gain_rows = partial(turn(0) * minor + lax.rem(at.b + db, minor), gain_rows)
    rows_across(0)
    relay_columns(1)
    relay_rows(1)
    gain_rows = lax.fori_loop(0, 3 * (minor - 1), away, gain_rows)
    weight(1)
    weight_across(1)

    rp = width // (shards * parts)
    halves = parts // 2
    whole = dot(normed_ref[...], proj[...], TN)
    gw[...] = whole.reshape(shards, parts, rp, slab3).astype(BF16)
    for k in range(halves):
        at.send(gw.at[:, (1 - core) + 2 * k], gw_core.at[k], vc_send.at[k], vc_recv.at[k], rep=at.flip(1))

    gain_rows = lax.fori_loop(0, MAJOR, lambda i, acc: partial(at.at(i, 0), acc), gain_rows)

    gain_row = jnp.sum(gain_rows, axis=0, keepdims=True) / vec_ref[0:1, :]
    rows = row_ref[...]
    place = lax.broadcasted_iota(jnp.int32, (8, width), 0)
    rows = jnp.where(place == 0, jnp.broadcast_to(gain_row, (8, width)), rows)
    turn_in = jnp.concatenate(
        [jnp.broadcast_to(gscale, (HEAD, 128)), jnp.zeros((128 - HEAD, 128), F32)], axis=0
    )
    scale_row = jnp.broadcast_to(turn_in.T[0:1, :], (8, 128))
    scale_tile = jnp.where(lax.broadcasted_iota(jnp.int32, (8, 128), 0) == 5, scale_row, 0.0)
    for j in range(shards):
        first = min(j * slab // 128 * 128, width - 256)
        windows[j, :, :256] = rows[:, first : first + 256]
        windows[j, :, 256:] = scale_tile
    for i, (da, db) in enumerate(peers):
        dest = at.at(da, db)
        at.send(windows.at[dest], small_land.at[me], s_send.at[i], s_recv.at[me], shard=dest)
    small_land[me] = windows[me]

    weight_summed(2)
    relay_columns(0)
    relay_rows(0)
    weight(0)
    weight_across(0)
    for k in range(halves):
        at.arrived(gw_core.at[k], vc_recv.at[k])
        gw_core[k] = gw[:, core + 2 * k] + gw_core[k]
    km = mine // 2 if parts == 4 else 0
    if parts == 4:
        at.send(gw_core.at[1 - km], gw_y, vy_send.at[0], vy_recv.at[0], rep=at.flip(2))
    rows_summed(0)
    weight_joined(2, 0)
    weight_joined(2, 1)
    weight_joined(2, 3)
    if parts == 4:
        at.arrived(gw_y, vy_recv.at[0])
        gw_sum[...] = gw_core[km] + gw_y[...]
    else:
        gw_sum[...] = gw_core[0]
    for i, (da, db) in enumerate(peers):
        dest = at.at(da, db)
        at.send(gw_sum.at[dest], gw_land.at[me], va_send.at[i], va_recv.at[me], shard=dest)
    gw_land[me] = gw_sum[me]
    rows_across(1)
    rows_across(2)
    rows_last_across()
    weight_summed(1)
    row_sums.joined(0)
    weight_joined(1, 0)
    weight_joined(1, 1)
    weight_joined(1, 3)
    weight_summed(0)
    weight_joined(0, 0)
    weight_joined(0, 1)
    weight_joined(0, 3)
    for da, db in peers:
        origin = at.at(-da, -db)
        at.arrived(gw_land.at[origin], va_recv.at[origin])
    for n, mask in enumerate(extras):
        at.exchange(gw_land, gw_extra.at[n], ve_send.at[n], ve_recv.at[n], at.flip(mask))
        gw_land[...] = gw_land[...] + gw_extra[n]
    for j in range(shards):
        for t in range(3):
            first = t * width + j * slab
            gw_ref[mine, :, first : first + slab] = gw_land[j, :, t * slab : (t + 1) * slab]

    gw_go(0)
    rows_summed(1)
    weight_last(2)
    weight_last(1)
    weight_last(0)
    row_sums.joined(1)
    for n in range(count - 1):
        gw_take(n)
        gw_go(n + 1)


    def write(src, dst, n):
        copy = pltpu.make_async_copy(src, dst, done_sem.at[n])
        copy.start()
        written.append(copy)

    for da, db in peers:
        origin = at.at(-da, -db)
        at.arrived(small_land.at[origin], s_recv.at[origin])
    small = jnp.sum(small_land[...], axis=0)
    lanes = lax.broadcasted_iota(jnp.int32, (slab, 128), 1)
    sides = jnp.concatenate(
        [jnp.where(lanes == 6, bias_q, jnp.where(lanes == 7, bias_v, 0.0)), jnp.zeros((256 - slab, 128), F32)],
        axis=0,
    )
    sides = jnp.concatenate([sides[:128].T[:8], sides[128:].T[:8]], axis=1)
    shift = me * slab - lax.min(me * slab // 128 * 128, width - 256)
    window = pltpu.roll(small[:, :256], lax.rem(256 - shift, 256), 1)
    tall = lax.broadcasted_iota(jnp.int32, (8, 256), 0)
    small_got[0, :, :256] = jnp.where(tall < 5, window, sides)
    small_got[0, :, 256:] = pltpu.roll(small[:, 256:], lax.rem(128 - me * unit, 128), 1)

    def small_round(n):
        at.send(
            small_got.at[2 * n], small_got.at[2 * n + 1], b_send.at[n], b_recv.at[n], rep=at.flip(every[n])
        )

    def small_add(n):
        at.arrived(small_got.at[2 * n + 1], b_recv.at[n])
        small_got[2 * n + 2] = small_got[2 * n] + small_got[2 * n + 1]

    small_round(0)
    rows_summed(2)
    small_add(0)
    small_round(1)
    rows_last()
    gw_take(count - 1)
    write(gw_ref, gw_hbm, 2)
    for n in range(count - 1):
        for m in mats:
            fin_hands[m][1](n)
            fin_hands[m][0](n + 1)
    for n in range(1, len(every)):
        small_add(n)
        if n + 1 < len(every):
            small_round(n + 1)
    small_out_ref[...] = small_got[2 * len(every)]

    total = rows_result()
    x = x_ref[...].astype(F32)
    r = lax.rsqrt(jnp.mean(x * x, axis=-1, keepdims=True) + EPS)
    weighted = vec_ref[0:1, :] * total
    gin_ref[...] = gmixed_ref[...] + r * weighted - x * (r * r * r) * jnp.mean(x * weighted, axis=-1, keepdims=True)


    write(gin_ref, gin_hbm, 3)
    for m in mats:
        fin_hands[m][1](count - 1)
        write(fin_ref.at[m], fin_hbm.at[m], 4 + m)
    at.settle()
    for copy in written:
        copy.wait()


def layer(shards, replicas, inputs, segment_ids, positions, vectors, w_qkv, w_out, w_up, w_down, cotangent):
    block, width = inputs.shape
    slab = width // shards
    slab3 = 3 * slab
    length = shards * block
    wparts = 2 if slab % 32 == 0 else 1
    parts = parts_of(slab)
    halves = parts // 2
    rp = slab // parts
    rows_part = slab // 2 if parts == 4 else slab
    cols = width // 2
    minor = shards // MAJOR
    peers = shards - 1
    bits = (replicas - 1).bit_length()
    more = bits - (parts - 1).bit_length()
    shape = jax.ShapeDtypeStruct
    dma = pltpu.SemaphoreType.DMA
    vm = pltpu.VMEM
    return pl.pallas_call(
        functools.partial(layer_kernel, shards, replicas, wparts, parts, 2 * block),
        out_shape=(
            shape((block, width), BF16),
            shape((3, slab, width), BF16),
            shape((parts, rp, 3 * width), BF16),
            shape((block, width), F32),
            shape((8, 384), F32),
        ),
        in_specs=[VMEM] * 11 + [ANY] * 5,
        out_specs=[ANY] * 4 + [VMEM],
        scratch_shapes=[
            vm((block, width), BF16),
            vm((3, slab, width), BF16),
            vm((parts, rp, 3 * width), BF16),
            vm((block, width), F32),
            vm(w_qkv.shape, BF16),
            vm((block, width), BF16),
            vm((16, 256), F32),
            vm((length, width), BF16),
            vm((slab3, length), BF16),
            vm((slab, length), F32),
            vm((8, length), F32),
            vm((8, width), F32),
            vm((8, length), F32),
            vm((shards, wparts, slab // wparts, slab3), BF16),
            vm((3, shards, halves, slab // halves, block), BF16),
            vm((3, block, width), BF16),
            vm((width, block), BF16),
            vm((8, width), F32),
            vm((block, width), F32),
            vm((shards, block, width), BF16),
            vm((shards, 8, 256), F32),
            vm((shards, wparts, slab // wparts, slab3), BF16),
            vm((slab3, width), BF16),
            vm((slab, length), BF16),
            vm((width, block), BF16),
            vm((3, width, width), BF16),
            vm((slab, length), BF16),
            vm((slab3, length), F32),
            vm((length, slab3), BF16),
            vm((3, shards, rows_part, parts * block), BF16),
            vm((3, parts * block, cols), BF16),
            vm((3, shards, rows_part, block) if parts == 4 else (1, 1, 16, block), BF16),
            vm((3, MAJOR, minor, rows_part, cols), BF16),
            vm((3, minor - 1, MAJOR, rows_part, cols), BF16),
            vm((3, MAJOR + 1, rows_part, cols), BF16),
            vm((max(more, 1), 3, rows_part, cols), BF16),
            vm((shards, parts, rp, slab3), BF16),
            vm((halves, shards, rp, slab3), BF16),
            vm((shards, rp, slab3) if parts == 4 else (1, 16, 128), BF16),
            vm((shards, rp, slab3), BF16),
            vm((shards, rp, slab3), BF16),
            vm((max(more, 1), shards, rp, slab3), BF16),
            vm((shards, 8, 384), F32),
            vm((shards, 8, 384), F32),
            vm((2 * bits + 1, 8, 384), F32),
            dma((2, MAJOR)), dma((MAJOR, minor - 1)), dma((shards,)),
            dma((peers,)), dma((shards,)),
            dma((peers,)), dma((shards, wparts)), dma((shards,)), dma((shards,)),
            dma((2, MAJOR)), dma((MAJOR, minor - 1)), dma((shards, parts)),
            dma((shards,)), dma((shards, 2)),
            dma((5,)), dma((shards,)), dma((shards,)), dma((7,)),
            dma((peers,)), dma((shards,)),
            dma((3, 3)), dma((3, 3)),
            dma((3, 4)), dma((3, 4)),
            dma((3, minor - 1)), dma((3, minor - 1)),
            dma((3, MAJOR)), dma((3, MAJOR + 1)),
            dma((3, parts)), dma((3, parts)),
            dma((max(more, 1), 3)), dma((max(more, 1), 3)),
            dma((minor - 1, MAJOR + 1)), dma((minor - 1, MAJOR + 1)),
            dma((MAJOR + 1,)), dma((MAJOR + 2,)),
            dma((halves,)), dma((halves,)),
            dma((1,)), dma((1,)),
            dma((peers,)), dma((shards,)),
            dma((parts,)), dma((parts,)),
            dma((max(more, 1),)), dma((max(more, 1),)),
            dma((peers,)), dma((shards,)),
            dma((bits,)), dma((bits,)),
        ],
        compiler_params=pltpu.CompilerParams(
            collective_id=0, has_side_effects=True, vmem_limit_bytes=62 << 20
        ),
        name="layer",
    )(inputs, segment_ids, positions, *vectors, w_qkv, w_out, w_up, w_down, cotangent)


def finish_kernel(
    slab, unit, fin_ref, gw_ref, small_ref, gin_ref, out_ref,
    w_out_ref, w_up_ref, w_down_ref, w_qkv_ref, input_ref, output_ref,
    gain_one_ref, b_query_ref, b_value_ref, scale_ref, b_out_ref, gain_two_ref, b_up_ref, b_down_ref,
):
    w_out_ref[...] = fin_ref[0].astype(F32)
    w_up_ref[...] = fin_ref[1].astype(F32)
    w_down_ref[...] = fin_ref[2].astype(F32)
    w_qkv_ref[...] = gw_ref[...].astype(F32)
    input_ref[...] = gin_ref[...]
    output_ref[...] = out_ref[...]

    @pl.when(pl.program_id(0) == 0)
    def _():
        table = {
            0: gain_one_ref, 1: b_out_ref, 2: gain_two_ref, 3: b_up_ref, 4: b_down_ref,
            6: b_query_ref, 7: b_value_ref,
        }
        for row, ref in table.items():
            ref[...] = small_ref[row : row + 1, :slab].reshape(slab)
        scale_ref[...] = small_ref[5:6, 256 : 256 + unit].reshape(unit)


def finish(fin, gw, small, gin, out):
    slab, width = fin.shape[1:]
    block = gin.shape[0]
    steps = 2
    unit = HEAD * slab // width
    part, tokens = slab // steps, block // steps
    shape = jax.ShapeDtypeStruct

    def rows(size, columns):
        return pl.BlockSpec((size, columns), lambda i: (i, 0))

    whole = pl.BlockSpec((8, 384), lambda i: (0, 0))
    vector = pl.BlockSpec((slab,), lambda i: (0,))
    return pl.pallas_call(
        functools.partial(finish_kernel, slab, unit),
        grid=(steps,),
        out_shape=[shape((slab, width), F32)] * 3
        + [shape((slab, 3 * width), F32), shape((block, width), F32), shape((block, width), BF16)]
        + [shape((slab,), F32)] * 3
        + [shape((unit,), F32)]
        + [shape((slab,), F32)] * 4,
        in_specs=[
            pl.BlockSpec((3, part, width), lambda i: (0, i, 0)), rows(part, 3 * width), whole,
            rows(tokens, width), rows(tokens, width),
        ],
        out_specs=[rows(part, width)] * 3
        + [rows(part, 3 * width), rows(tokens, width), rows(tokens, width)]
        + [vector] * 3
        + [pl.BlockSpec((unit,), lambda i: (0,))]
        + [vector] * 4,
        name="finish",
    )(fin, gw, small, gin, out)


def on_device(
    inputs, segment_ids, positions, gain_one, w_qkv, b_query, b_value, query_scale, w_out, b_out,
    gain_two, w_up, b_up, w_down, b_down, cotangent,
):
    shards = lax.axis_size("shard")
    replicas = lax.axis_size("replica")
    block, width = inputs.shape[1:]
    slab = width // shards
    output, fin, gw, input_grad, small = layer(
        shards, replicas, inputs.reshape(block, width), segment_ids, positions,
        (gain_one, b_query, b_value, query_scale, b_out, gain_two, b_up, b_down),
        w_qkv, w_out, w_up, w_down, cotangent.reshape(block, width),
    )
    (
        g_out, g_up, g_down, g_qkv, input_grad, output, g_gain_one, g_b_query, g_b_value, g_scale, g_b_out,
        g_gain_two, g_b_up, g_b_down,
    ) = finish(fin, gw.reshape(slab, 3 * width), small, input_grad, output)
    return (
        output[None], input_grad[None], g_gain_one, g_qkv, g_b_query, g_b_value, g_scale, g_out, g_b_out,
        g_gain_two, g_up, g_b_up, g_down, g_b_down,
    )


def solution(mesh):
    rows = P("replica", "shard", None)
    ids = P("replica", "shard")
    vector = P("shard")
    matrix = P("shard", None)
    in_specs = (
        rows, ids, ids, vector, matrix, vector, vector, vector, matrix, vector, vector, matrix, vector,
        matrix, vector, rows,
    )
    out_specs = (
        rows, rows, vector, matrix, vector, vector, vector, matrix, vector, vector, matrix, vector, matrix,
        vector,
    )
    return jax.shard_map(on_device, mesh=mesh, in_specs=in_specs, out_specs=out_specs, check_vma=False)
```
